32 devices in a mesh: dev: 32 (over z, y, x, core).
Axes of the slice: x: 2, y: 2, z: 4, core: 2. Of those that a mesh axis runs over, the one named last changes fastest.
Arguments:
- tokens: bfloat16 [12288, 576], P('dev'), may hold values from -8 to 8
- positions: int32 [12288], P('dev'), may hold values from 0 to 383, as said below
- gain_attn: float32 [576], replicated, may hold values from 0.1 to 1.9
- w_query: bfloat16 [331776], P('dev'), may hold values from -2 to 2
- w_kv: bfloat16 [221184], P('dev'), may hold values from -2 to 2
- w_out: bfloat16 [331776], P('dev'), may hold values from -1.5 to 1.5
- gain_ffn: float32 [576], replicated, may hold values from 0.1 to 1.9
- w_gate_up: bfloat16 [1769472], P('dev'), may hold values from -0.25 to 0.25
- w_down: bfloat16 [884736], P('dev'), may hold values from -0.15625 to 0.15625
- cotangent: bfloat16 [12288, 576], P('dev'), may hold values from -16 to 16
Outputs:
- mixed: bfloat16 [12288, 576], P('dev')
- d_tokens: float32 [12288, 576], P('dev')
- d_gain_attn: float32 [576], replicated
- d_query: float32 [331776], P('dev')
- d_kv: float32 [221184], P('dev')
- d_out: float32 [331776], P('dev')
- d_gain_ffn: float32 [576], replicated
- d_gate_up: float32 [1769472], P('dev')
- d_down: float32 [884736], P('dev')
The draws below stay inside these ranges and needn't reach their ends.
Inputs may be any that keep to these rules, and one draw needn't show every extreme that they name: positions count 0 at a document's first token and rise by one along it; documents lie end to end, so token t's document begins at token t - positions[t]; token 0 has position 0; some document has exactly 384 tokens.
All inputs are finite; a program needn't handle non-finite values.
Results may differ from the reference program's by a relative error of at most 0.012.
Values may be sent and summed in bfloat16 or wider, within the bound.
No kernel may reach another device: no remote copies, remote signals or barrier semaphores. Data moves between devices by JAX's collectives and lax.ppermute only.
A program may use at most 128 MiB of HBM per device.

```python
import math
import jax
import jax.numpy as jnp
from jax import lax

D = 576
H = 9
KVH = 3
HD = 64
FF = 1536
TOK_DEV = 384
SEG_MAX = 384
TOKENS = 12288
N_DEV = 32


def draw_positions(key, part):
    offset_key, frame_key, cut_key = jax.random.split(key, 3)
    token_index = jnp.arange(TOKENS, dtype=jnp.int32)
    offset = jax.random.randint(offset_key, (), 1, SEG_MAX, dtype=jnp.int32)
    shifted = token_index + offset
    frame_index = shifted // SEG_MAX
    whole_frame = jax.random.randint(frame_key, (), 1, TOKENS // SEG_MAX, dtype=jnp.int32)
    cut_marks = (jax.random.randint(cut_key, (TOKENS,), 0, SEG_MAX, dtype=jnp.int32) < 2) & (frame_index != whole_frame)
    starts = (shifted % SEG_MAX == 0) | cut_marks | (token_index == 0)
    doc_start = lax.cummax(jnp.where(starts, token_index, 0), axis=0)
    return token_index - doc_start


def scaled_columns(key, columns):
    base_key = jax.random.fold_in(key, 0)
    values = jnp.clip(jax.random.normal(base_key, (D, columns), jnp.float32), -6.0, 6.0) / math.sqrt(D)
    values = jnp.clip(values, -2.0, 2.0)
    return values.reshape(D * columns).astype(jnp.bfloat16)


def draw_w_query(key, part):
    return scaled_columns(jax.random.fold_in(key, 11), H * HD)


def draw_w_kv(key, part):
    return scaled_columns(jax.random.fold_in(key, 12), 2 * KVH * HD)


def draw_cotangent(key, part):
    base_key = jax.random.fold_in(jax.random.fold_in(key, 13), 0)
    along = jnp.arange(TOKENS, dtype=jnp.float32) / TOKENS
    rising = jnp.exp(math.log(3.0) * along)[:, None]
    values = jax.random.normal(base_key, (TOKENS, D), jnp.float32) * rising
    return jnp.clip(values, -16.0, 16.0).astype(jnp.bfloat16)


def steps_of(stream_key, shape, cuts, smallest, high):
    loudness = 1.0
    for dim, blocks in cuts:
        steps = jax.random.uniform(jax.random.fold_in(jax.random.fold_in(stream_key, 6), dim), (blocks,), jnp.float32, smallest / len(cuts), high / len(cuts))
        loudness = loudness * jnp.repeat(jnp.exp(steps), shape[dim] // blocks).reshape((-1,) + (1,) * (len(shape) - 1 - dim))
    return loudness


def normal_values(own_key, dims, spread, limit, cuts=(), kind=jnp.bfloat16):
    entries = spread * jax.random.normal(own_key, dims, jnp.float32)
    if cuts:
        entries = entries * steps_of(own_key, dims, cuts, -0.22, 0.18)
    return jnp.clip(entries, -limit, limit).astype(kind)


def setup_inputs(seed: int = 0) -> dict:
    arg_keys = jax.random.split(jax.random.key(seed), 11)
    return {
        "tokens": normal_values(arg_keys[0], (TOKENS, D), 1.0, 8.0, ((0, 32),)),
        "positions": draw_positions(jax.random.fold_in(arg_keys[10], 71), 0),
        "gain_attn": jnp.clip(1.0 + 0.18 * jax.random.normal(arg_keys[2], (D,), jnp.float32), 0.1, 1.9),
        "w_query": draw_w_query(jax.random.fold_in(arg_keys[10], 71), 0),
        "w_kv": draw_w_kv(jax.random.fold_in(arg_keys[10], 71), 0),
        "w_out": normal_values(arg_keys[5], (H * HD * D,), (D // 32) ** -0.5, 1.5, ((0, 32),)),
        "gain_ffn": jnp.clip(1.0 + 0.18 * jax.random.normal(arg_keys[6], (D,), jnp.float32), 0.1, 1.9),
        "w_gate_up": normal_values(arg_keys[7], (2 * D * FF,), D ** -0.5, 0.25, ((0, 32),)),
        "w_down": normal_values(arg_keys[8], (FF * D,), FF ** -0.5, 0.15625, ((0, 32),)),
        "cotangent": draw_cotangent(jax.random.fold_in(arg_keys[10], 71), 0),
    }


norm_epsilon = 1e-05
theta_base = 100000.0

def norm_forward(values, scale_gain):
    inverse = lax.rsqrt(lax.optimization_barrier(jnp.mean(values * values, axis=-1, keepdims=True)) + norm_epsilon)
    return (values * inverse * scale_gain, inverse)

def norm_backward(grad_output, values, inverse, scale_gain):
    unit_rows = values * inverse
    scaled = grad_output * scale_gain
    grad_gain = lax.optimization_barrier(jnp.sum(grad_output * unit_rows, axis=0))
    grad_input = inverse * (scaled - unit_rows * lax.optimization_barrier(jnp.mean(scaled * unit_rows, axis=-1, keepdims=True)))
    return (grad_input, grad_gain)

def rope_angles(position_block):
    half_dim = HD // 2
    frequency = jnp.exp(jnp.arange(half_dim, dtype=jnp.float32) * (-2.0 * math.log(theta_base) / HD))
    angles = position_block.astype(jnp.float32)[:, None] * frequency[None, :]
    return (jnp.cos(angles)[:, None, :], jnp.sin(angles)[:, None, :])

def rotate(values, cos_table, sin_table):
    half_dim = values.shape[-1] // 2
    first_half = values[..., :half_dim]
    second_half = values[..., half_dim:]
    return jnp.concatenate([first_half * cos_table - second_half * sin_table, second_half * cos_table + first_half * sin_table], axis=-1)

def project_heads(normed, query_mat, keyval_mat, cos_table, sin_table):
    row_count = normed.shape[0]
    queries = jnp.dot(normed, query_mat, preferred_element_type=jnp.float32).reshape(row_count, H, HD)
    keyvals = jnp.dot(normed, keyval_mat, preferred_element_type=jnp.float32)
    keys_rot = rotate(keyvals[:, :KVH * HD].reshape(row_count, KVH, HD), cos_table, sin_table).reshape(row_count, KVH * HD)
    query_rot = rotate(queries, cos_table, sin_table).reshape(row_count, H * HD).astype(jnp.bfloat16)
    keyval_rot = jnp.concatenate([keys_rot, keyvals[:, KVH * HD:]], axis=1).astype(jnp.bfloat16)
    return (query_rot, keyval_rot)

def window_mask(position_block, row_count, reach_rows):
    query_at = jnp.arange(row_count, dtype=jnp.int32)[:, None] + (row_count + reach_rows)
    key_at = jnp.arange(2 * row_count + reach_rows, dtype=jnp.int32)[None, :]
    return (key_at <= query_at) & (key_at >= query_at - position_block[:, None])

def masked_scores(query_group, key_group, allowed):
    scale_factor = 1.0 / math.sqrt(HD)
    scores = jnp.einsum('tqd,wd->qtw', query_group.astype(jnp.float32), key_group.astype(jnp.float32)) * scale_factor
    return jnp.where(allowed[None], scores, -1e+30)

def attend_forward(query_rot, window, allowed):
    row_count = query_rot.shape[0]
    grouped = H // KVH
    queries = query_rot.reshape(row_count, H, HD)
    outputs = []
    totals = []
    for group_index in range(KVH):
        query_group = queries[:, group_index * grouped:(group_index + 1) * grouped]
        key_group = window[:, group_index * HD:(group_index + 1) * HD]
        value_group = window[:, (KVH + group_index) * HD:(KVH + group_index + 1) * HD]
        scores = masked_scores(query_group, key_group, allowed)
        highest = lax.optimization_barrier(jnp.max(scores, axis=-1, keepdims=True))
        log_total = highest + jnp.log(lax.optimization_barrier(jnp.sum(jnp.exp(scores - highest), axis=-1, keepdims=True)))
        probability = jnp.exp(scores - log_total).astype(jnp.bfloat16)
        head_out = jnp.einsum('qtw,wd->tqd', probability.astype(jnp.float32), value_group.astype(jnp.float32))
        outputs.append(head_out.astype(jnp.bfloat16))
        totals.append(log_total)
    return (jnp.concatenate(outputs, axis=1).reshape(row_count, H * HD), totals)

def attend_backward(query_rot, window, allowed, attended, grad_attended, totals):
    row_count = query_rot.shape[0]
    grouped = H // KVH
    scale_factor = 1.0 / math.sqrt(HD)
    queries = query_rot.reshape(row_count, H, HD)
    attended_heads = attended.reshape(row_count, H, HD)
    grad_heads = grad_attended.reshape(row_count, H, HD)
    query_grads = []
    key_grads = []
    value_grads = []
    for group_index in range(KVH):
        head_slice = slice(group_index * grouped, (group_index + 1) * grouped)
        query_group = queries[:, head_slice].astype(jnp.float32)
        key_group = window[:, group_index * HD:(group_index + 1) * HD]
        value_group = window[:, (KVH + group_index) * HD:(KVH + group_index + 1) * HD].astype(jnp.float32)
        scores = masked_scores(queries[:, head_slice], key_group, allowed)
        probability = jnp.exp(scores - totals[group_index])
        grad_group = grad_heads[:, head_slice].astype(jnp.float32)
        row_delta = lax.optimization_barrier(jnp.sum(grad_group * attended_heads[:, head_slice].astype(jnp.float32), axis=-1))
        grad_prob = jnp.einsum('tqd,wd->qtw', grad_group, value_group)
        grad_scores = (probability * (grad_prob - row_delta.T[:, :, None]) * scale_factor).astype(jnp.bfloat16).astype(jnp.float32)
        query_grads.append(jnp.einsum('qtw,wd->tqd', grad_scores, key_group.astype(jnp.float32)))
        key_grads.append(jnp.einsum('qtw,tqd->wd', grad_scores, query_group))
        value_grads.append(jnp.einsum('qtw,tqd->wd', probability.astype(jnp.bfloat16).astype(jnp.float32), grad_group))
    return (jnp.concatenate(query_grads, axis=1), jnp.concatenate(key_grads + value_grads, axis=1))

def reference(tokens, positions, gain_attn, w_query, w_kv, w_out, gain_ffn, w_gate_up, w_down, cotangent):
    row_count = TOK_DEV
    reach_rows = SEG_MAX - TOK_DEV
    span_rows = 2 * row_count + reach_rows
    width_kv = 2 * KVH * HD
    query_mat = w_query.reshape(D, H * HD)
    keyval_mat = w_kv.reshape(D, width_kv)
    out_mat = w_out.reshape(H * HD, D)
    gate_up_mat = w_gate_up.reshape(D, 2 * FF)
    down_mat = w_down.reshape(FF, D)
    token_blocks = tokens.reshape(N_DEV, row_count, D)
    position_blocks = positions.reshape(N_DEV, row_count)
    cotangent_blocks = cotangent.reshape(N_DEV, row_count, D)

    def first_pass(block):
        token_block, position_block = block
        normed, inverse = norm_forward(token_block.astype(jnp.float32), gain_attn)
        cos_table, sin_table = rope_angles(position_block)
        return project_heads(normed.astype(jnp.bfloat16), query_mat, keyval_mat, cos_table, sin_table)
    query_blocks, keyval_blocks = lax.map(first_pass, (token_blocks, position_blocks))
    padded = jnp.concatenate([jnp.zeros((row_count + reach_rows, width_kv), jnp.bfloat16), keyval_blocks.reshape(TOKENS, width_kv)], axis=0)

    def second_pass(carry, block):
        grad_window_all, grad_out, grad_gate_up, grad_down, grad_gain_ffn = carry
        block_index, token_block, position_block, cotangent_block, query_rot = block
        start_row = block_index * row_count
        window = lax.dynamic_slice_in_dim(padded, start_row, span_rows, 0)
        allowed = window_mask(position_block, row_count, reach_rows)
        attended, totals = attend_forward(query_rot, window, allowed)
        inputs = token_block.astype(jnp.float32)
        residual = inputs + jnp.dot(attended, out_mat, preferred_element_type=jnp.float32)
        normed_ffn, inverse_ffn = norm_forward(residual, gain_ffn)
        normed_ffn = normed_ffn.astype(jnp.bfloat16)
        gate_up = jnp.dot(normed_ffn, gate_up_mat, preferred_element_type=jnp.float32)
        gate_part = gate_up[:, :FF]
        up_part = gate_up[:, FF:]
        activated = (jax.nn.silu(gate_part) * up_part).astype(jnp.bfloat16)
        mixed = (residual + jnp.dot(activated, down_mat, preferred_element_type=jnp.float32)).astype(jnp.bfloat16)
        grad_act = jnp.dot(cotangent_block, down_mat.T, preferred_element_type=jnp.float32)
        sigmoid_gate = jax.nn.sigmoid(gate_part)
        grad_gate_up_act = jnp.concatenate([grad_act * up_part * sigmoid_gate * (1.0 + gate_part * (1.0 - sigmoid_gate)), grad_act * jax.nn.silu(gate_part)], axis=1).astype(jnp.bfloat16)
        grad_down = grad_down + jnp.dot(activated.T, cotangent_block, preferred_element_type=jnp.float32)
        grad_gate_up = grad_gate_up + jnp.dot(normed_ffn.T, grad_gate_up_act, preferred_element_type=jnp.float32)
        grad_normed_ffn = jnp.dot(grad_gate_up_act, gate_up_mat.T, preferred_element_type=jnp.float32)
        grad_norm_ffn, gain_term = norm_backward(grad_normed_ffn, residual, inverse_ffn, gain_ffn)
        grad_residual = cotangent_block.astype(jnp.float32) + grad_norm_ffn
        grad_residual_b = grad_residual.astype(jnp.bfloat16)
        grad_out = grad_out + jnp.dot(attended.T, grad_residual_b, preferred_element_type=jnp.float32)
        grad_attended = jnp.dot(grad_residual_b, out_mat.T, preferred_element_type=jnp.float32).astype(jnp.bfloat16)
        grad_query_rot, grad_window = attend_backward(query_rot, window, allowed, attended, grad_attended, totals)
        cos_table, sin_table = rope_angles(position_block)
        grad_query_act = rotate(grad_query_rot, cos_table, -sin_table).reshape(row_count, H * HD).astype(jnp.bfloat16)
        old_rows = lax.dynamic_slice_in_dim(grad_window_all, start_row, span_rows, 0)
        grad_window_all = lax.dynamic_update_slice_in_dim(grad_window_all, old_rows + grad_window, start_row, 0)
        return ((grad_window_all, grad_out, grad_gate_up, grad_down, grad_gain_ffn + gain_term), (mixed, grad_residual, grad_query_act))
    start_carry = (jnp.zeros((TOKENS + row_count + reach_rows, width_kv), jnp.float32), jnp.zeros((H * HD, D), jnp.float32), jnp.zeros((D, 2 * FF), jnp.float32), jnp.zeros((FF, D), jnp.float32), jnp.zeros((D,), jnp.float32))
    block_numbers = jnp.arange(N_DEV, dtype=jnp.int32)
    second_carry, second_out = lax.scan(second_pass, start_carry, (block_numbers, token_blocks, position_blocks, cotangent_blocks, query_blocks))
    grad_window_all, grad_out, grad_gate_up, grad_down, grad_gain_ffn = second_carry
    mixed_blocks, residual_grads, query_act_grads = second_out
    keyval_grads = grad_window_all[row_count + reach_rows:].reshape(N_DEV, row_count, width_kv)

    def third_pass(carry, block):
        grad_query, grad_keyval, grad_gain_attn = carry
        token_block, position_block, grad_residual, grad_query_act, grad_keyval_rot = block
        inputs = token_block.astype(jnp.float32)
        normed, inverse = norm_forward(inputs, gain_attn)
        normed = normed.astype(jnp.bfloat16)
        cos_table, sin_table = rope_angles(position_block)
        key_part = rotate(grad_keyval_rot[:, :KVH * HD].reshape(row_count, KVH, HD), cos_table, -sin_table).reshape(row_count, KVH * HD)
        grad_keyval_act = jnp.concatenate([key_part, grad_keyval_rot[:, KVH * HD:]], axis=1).astype(jnp.bfloat16)
        grad_query = grad_query + jnp.dot(normed.T, grad_query_act, preferred_element_type=jnp.float32)
        grad_keyval = grad_keyval + jnp.dot(normed.T, grad_keyval_act, preferred_element_type=jnp.float32)
        grad_normed = jnp.dot(grad_query_act, query_mat.T, preferred_element_type=jnp.float32) + jnp.dot(grad_keyval_act, keyval_mat.T, preferred_element_type=jnp.float32)
        grad_input, gain_term = norm_backward(grad_normed, inputs, inverse, gain_attn)
        return ((grad_query, grad_keyval, grad_gain_attn + gain_term), grad_residual + grad_input)
    third_start = (jnp.zeros((D, H * HD), jnp.float32), jnp.zeros((D, width_kv), jnp.float32), jnp.zeros((D,), jnp.float32))
    third_carry, token_grads = lax.scan(third_pass, third_start, (token_blocks, position_blocks, residual_grads, query_act_grads, keyval_grads))
    grad_query, grad_keyval, grad_gain_attn = third_carry
    return (mixed_blocks.reshape(TOKENS, D), token_grads.reshape(TOKENS, D), grad_gain_attn, grad_query.reshape(-1), grad_keyval.reshape(-1), grad_out.reshape(-1), grad_gain_ffn, grad_gate_up.reshape(-1), grad_down.reshape(-1))
```

```python
import math

import jax
import jax.numpy as jnp
from jax import lax
from jax.sharding import PartitionSpec as P

D = 576
H = 9
KVH = 3
HD = 64
FF = 1536


norm_epsilon = 1e-05
theta_base = 100000.0


def passed_along(value, axis, steps):
    count = lax.axis_size(axis)
    first, last = (max(0, -steps), min(count, count - steps))
    return lax.ppermute(value, axis, [(source, source + steps) for source in range(first, last)])


def link_masks(count):
    bits = [1 << b for b in range(count.bit_length() - 1)]
    if count == 32:
        bits = [1, 2, 4, 8, 24]
    return bits[0], bits[1:]


def swapped(value, mask):
    count = lax.axis_size("dev")
    return lax.ppermute(value, "dev", [(i, i ^ mask) for i in range(count)])


def color_orders(count, colors):
    first, rest = link_masks(count)
    if colors == 1:
        return [rest + [first]]
    step = len(rest) // colors
    return [rest[c * step :] + rest[: c * step] + [first] for c in range(colors)]


def slot_masks(order):
    slots = [0]
    for mask in order:
        slots = slots + [s ^ mask for s in slots]
    return slots


def cut_rows(rows, colors):
    edges = [rows * c // colors for c in range(colors + 1)]
    return list(zip(edges[:-1], edges[1:]))


def gather_all(block, colors):
    count = lax.axis_size("dev")
    me = lax.axis_index("dev")
    orders = color_orders(count, colors)
    held = [block[a:b][None] for a, b in cut_rows(block.shape[0], colors)]
    for t in range(len(orders[0])):
        got = [swapped(h, order[t]) for h, order in zip(held, orders)]
        held = [jnp.concatenate([h, g], axis=0) for h, g in zip(held, got)]
    whole = []
    for h, order in zip(held, orders):
        slots = slot_masks(order)
        where = [0] * count
        for place, mask in enumerate(slots):
            where[mask] = place
        index = jnp.asarray(where, jnp.int32)[me ^ jnp.arange(count, dtype=jnp.int32)]
        whole.append(jnp.take(h, index, axis=0, mode="clip"))
    return jnp.concatenate(whole, axis=1)


def scatter_sum(parts, colors):
    count = lax.axis_size("dev")
    me = lax.axis_index("dev")
    orders = color_orders(count, colors)
    held = []
    for (a, b), order in zip(cut_rows(parts.shape[1], colors), orders):
        slots = jnp.asarray(slot_masks(order), jnp.int32)
        held.append(jnp.take(parts[:, a:b], me ^ slots, axis=0, mode="clip"))
    for t in range(len(orders[0])):
        half = held[0].shape[0] // 2
        masks = [order[-1 - t] for order in orders]
        got = [swapped(h[half:].astype(jnp.bfloat16), m) for h, m in zip(held, masks)]
        held = [h[:half].astype(jnp.float32) + g.astype(jnp.float32) for h, g in zip(held, got)]
    return jnp.concatenate([h[0] for h in held], axis=0)


def sum_all(value):
    first, rest = link_masks(lax.axis_size("dev"))
    for mask in [first] + rest:
        value = value + swapped(value, mask)
    return value


def norm_forward(values, scale_gain):
    inverse = lax.rsqrt(jnp.mean(values * values, axis=-1, keepdims=True) + norm_epsilon)
    return (values * inverse * scale_gain, inverse)


def norm_backward(grad_output, values, inverse, scale_gain):
    unit_rows = values * inverse
    scaled = grad_output * scale_gain
    grad_gain = jnp.sum(grad_output * unit_rows, axis=0)
    grad_input = inverse * (
        scaled - unit_rows * jnp.mean(scaled * unit_rows, axis=-1, keepdims=True)
    )
    return (grad_input, grad_gain)


def rope_angles(position_block):
    half_dim = HD // 2
    frequency = jnp.exp(
        jnp.arange(half_dim, dtype=jnp.float32) * (-2.0 * math.log(theta_base) / HD)
    )
    angles = position_block.astype(jnp.float32)[:, None] * frequency[None, :]
    return (jnp.cos(angles)[:, None, :], jnp.sin(angles)[:, None, :])


def rotate(values, cos_table, sin_table):
    half_dim = values.shape[-1] // 2
    first_half = values[..., :half_dim]
    second_half = values[..., half_dim:]
    return jnp.concatenate(
        [
            first_half * cos_table - second_half * sin_table,
            second_half * cos_table + first_half * sin_table,
        ],
        axis=-1,
    )


def project_heads(normed, query_mat, keyval_mat, cos_table, sin_table):
    row_count = normed.shape[0]
    queries = jnp.dot(normed, query_mat, preferred_element_type=jnp.float32).reshape(
        row_count, H, HD
    )
    keyvals = jnp.dot(normed, keyval_mat, preferred_element_type=jnp.float32)
    keys_rot = rotate(
        keyvals[:, : KVH * HD].reshape(row_count, KVH, HD), cos_table, sin_table
    ).reshape(row_count, KVH * HD)
    query_rot = (
        rotate(queries, cos_table, sin_table).reshape(row_count, H * HD).astype(jnp.bfloat16)
    )
    keyval_rot = jnp.concatenate([keys_rot, keyvals[:, KVH * HD :]], axis=1).astype(jnp.bfloat16)
    return (query_rot, keyval_rot)


def window_mask(position_block, row_count):
    query_at = jnp.arange(row_count, dtype=jnp.int32)[:, None] + row_count
    key_at = jnp.arange(2 * row_count, dtype=jnp.int32)[None, :]
    return (key_at <= query_at) & (key_at >= query_at - position_block[:, None])


def masked_scores(query_group, key_group, allowed):
    scale_factor = 1.0 / math.sqrt(HD)
    scores = (
        jnp.einsum("tqd,wd->qtw", query_group, key_group, preferred_element_type=jnp.float32)
        * scale_factor
    )
    return jnp.where(allowed[None], scores, -1e30)


def attend_forward(query_rot, window, allowed):
    row_count = query_rot.shape[0]
    grouped = H // KVH
    queries = query_rot.reshape(row_count, H, HD)
    outputs = []
    totals = []
    for group_index in range(KVH):
        query_group = queries[:, group_index * grouped : (group_index + 1) * grouped]
        key_group = window[:, group_index * HD : (group_index + 1) * HD]
        value_group = window[:, (KVH + group_index) * HD : (KVH + group_index + 1) * HD]
        scores = masked_scores(query_group, key_group, allowed)
        highest = jnp.max(scores, axis=-1, keepdims=True)
        log_total = highest + jnp.log(jnp.sum(jnp.exp(scores - highest), axis=-1, keepdims=True))
        probability = jnp.exp(scores - log_total).astype(jnp.bfloat16)
        head_out = jnp.einsum(
            "qtw,wd->tqd", probability, value_group, preferred_element_type=jnp.float32
        )
        outputs.append(head_out.astype(jnp.bfloat16))
        totals.append(log_total)
    return (jnp.concatenate(outputs, axis=1).reshape(row_count, H * HD), totals)


def attend_backward(query_rot, window, allowed, attended, grad_attended, totals):
    row_count = query_rot.shape[0]
    grouped = H // KVH
    scale_factor = 1.0 / math.sqrt(HD)
    queries = query_rot.reshape(row_count, H, HD)
    attended_heads = attended.reshape(row_count, H, HD)
    grad_heads = grad_attended.reshape(row_count, H, HD)
    query_grads = []
    key_grads = []
    value_grads = []
    for group_index in range(KVH):
        head_slice = slice(group_index * grouped, (group_index + 1) * grouped)
        query_group = queries[:, head_slice]
        key_group = window[:, group_index * HD : (group_index + 1) * HD]
        value_group = window[:, (KVH + group_index) * HD : (KVH + group_index + 1) * HD]
        scores = masked_scores(query_group, key_group, allowed)
        probability = jnp.exp(scores - totals[group_index])
        grad_group = grad_heads[:, head_slice]
        row_delta = jnp.sum(
            grad_group.astype(jnp.float32) * attended_heads[:, head_slice].astype(jnp.float32),
            axis=-1,
        )
        grad_prob = jnp.einsum(
            "tqd,wd->qtw", grad_group, value_group, preferred_element_type=jnp.float32
        )
        grad_scores = (probability * (grad_prob - row_delta.T[:, :, None]) * scale_factor).astype(
            jnp.bfloat16
        )
        query_grads.append(
            jnp.einsum("qtw,wd->tqd", grad_scores, key_group, preferred_element_type=jnp.float32)
        )
        key_grads.append(
            jnp.einsum("qtw,tqd->wd", grad_scores, query_group, preferred_element_type=jnp.float32)
        )
        value_grads.append(
            jnp.einsum(
                "qtw,tqd->wd",
                probability.astype(jnp.bfloat16),
                grad_group,
                preferred_element_type=jnp.float32,
            )
        )
    return (jnp.concatenate(query_grads, axis=1), jnp.concatenate(key_grads + value_grads, axis=1))


def shards(
    tokens, positions, gain_attn, w_query, w_kv, w_out, gain_ffn, w_gate_up, w_down, cotangent
):
    row_count = tokens.shape[0]
    width_kv = 2 * KVH * HD
    count = lax.axis_size("dev")
    attn_sizes = [w_query.shape[0], w_kv.shape[0], w_out.shape[0]]
    ffn_sizes = [w_gate_up.shape[0], w_down.shape[0]]
    attn_all = gather_all(jnp.concatenate([w_query, w_kv, w_out]).reshape(-1, 128), 2)
    attn_all = attn_all.reshape(count, -1)
    query_mat = attn_all[:, : attn_sizes[0]].reshape(D, H * HD)
    keyval_mat = attn_all[:, attn_sizes[0] : attn_sizes[0] + attn_sizes[1]].reshape(D, width_kv)
    out_mat = attn_all[:, attn_sizes[0] + attn_sizes[1] :].reshape(H * HD, D)
    ffn_all = gather_all(jnp.concatenate([w_gate_up, w_down]).reshape(-1, 128), 4)
    ffn_all = ffn_all.reshape(count, -1)
    gate_up_mat = ffn_all[:, : ffn_sizes[0]].reshape(D, 2 * FF)
    down_mat = ffn_all[:, ffn_sizes[0] :].reshape(FF, D)
    inputs = tokens.astype(jnp.float32)
    normed_attn, inverse_attn = norm_forward(inputs, gain_attn)
    normed_attn = normed_attn.astype(jnp.bfloat16)
    cos_table, sin_table = rope_angles(positions)
    query_rot, keyval_rot = project_heads(normed_attn, query_mat, keyval_mat, cos_table, sin_table)
    near_keys = passed_along(keyval_rot, "dev", 1)
    window = jnp.concatenate([near_keys, keyval_rot], axis=0)
    allowed = window_mask(positions, row_count)
    attended, totals = attend_forward(query_rot, window, allowed)
    residual = inputs + jnp.dot(attended, out_mat, preferred_element_type=jnp.float32)
    normed_ffn, inverse_ffn = norm_forward(residual, gain_ffn)
    normed_ffn = normed_ffn.astype(jnp.bfloat16)
    gate_up = jnp.dot(normed_ffn, gate_up_mat, preferred_element_type=jnp.float32)
    gate_part = gate_up[:, :FF]
    up_part = gate_up[:, FF:]
    activated = (jax.nn.silu(gate_part) * up_part).astype(jnp.bfloat16)
    mixed = (residual + jnp.dot(activated, down_mat, preferred_element_type=jnp.float32)).astype(
        jnp.bfloat16
    )
    grad_act = jnp.dot(cotangent, down_mat.T, preferred_element_type=jnp.float32)
    sigmoid_gate = jax.nn.sigmoid(gate_part)
    grad_gate_up_act = jnp.concatenate(
        [
            grad_act * up_part * sigmoid_gate * (1.0 + gate_part * (1.0 - sigmoid_gate)),
            grad_act * jax.nn.silu(gate_part),
        ],
        axis=1,
    ).astype(jnp.bfloat16)
    grad_down = jnp.dot(activated.T, cotangent, preferred_element_type=jnp.float32)
    grad_gate_up = jnp.dot(normed_ffn.T, grad_gate_up_act, preferred_element_type=jnp.float32)
    grad_normed_ffn = jnp.dot(grad_gate_up_act, gate_up_mat.T, preferred_element_type=jnp.float32)
    grad_norm_ffn, grad_gain_ffn = norm_backward(grad_normed_ffn, residual, inverse_ffn, gain_ffn)
    grad_residual = cotangent.astype(jnp.float32) + grad_norm_ffn
    grad_residual_b = grad_residual.astype(jnp.bfloat16)
    grad_out = jnp.dot(attended.T, grad_residual_b, preferred_element_type=jnp.float32)
    grad_attended = jnp.dot(grad_residual_b, out_mat.T, preferred_element_type=jnp.float32).astype(
        jnp.bfloat16
    )
    grad_query_rot, grad_window = attend_backward(
        query_rot, window, allowed, attended, grad_attended, totals
    )
    back_near = passed_along(grad_window[:row_count].astype(jnp.bfloat16), "dev", -1).astype(jnp.float32)
    grad_keyval_rot = grad_window[row_count:] + back_near
    key_part = rotate(
        grad_keyval_rot[:, : KVH * HD].reshape(row_count, KVH, HD), cos_table, -sin_table
    ).reshape(row_count, KVH * HD)
    grad_keyval_act = jnp.concatenate([key_part, grad_keyval_rot[:, KVH * HD :]], axis=1).astype(
        jnp.bfloat16
    )
    grad_query_act = (
        rotate(grad_query_rot, cos_table, -sin_table)
        .reshape(row_count, H * HD)
        .astype(jnp.bfloat16)
    )
    grad_query = jnp.dot(normed_attn.T, grad_query_act, preferred_element_type=jnp.float32)
    grad_keyval = jnp.dot(normed_attn.T, grad_keyval_act, preferred_element_type=jnp.float32)
    grad_normed_attn = jnp.dot(
        grad_query_act, query_mat.T, preferred_element_type=jnp.float32
    ) + jnp.dot(grad_keyval_act, keyval_mat.T, preferred_element_type=jnp.float32)
    grad_input, grad_gain_attn = norm_backward(grad_normed_attn, inputs, inverse_attn, gain_attn)
    token_grads = grad_residual + grad_input
    ffn_parts = jnp.concatenate(
        [
            grad_gate_up.reshape(count, -1).astype(jnp.bfloat16),
            grad_down.reshape(count, -1).astype(jnp.bfloat16),
            grad_out.reshape(count, -1).astype(jnp.bfloat16),
        ],
        axis=1,
    )
    ffn_parts = jnp.pad(ffn_parts, ((0, 0), (0, -ffn_parts.shape[1] % 128)))
    ffn_share = scatter_sum(ffn_parts.reshape(count, -1, 128), 4).reshape(-1)
    share_gate_up = ffn_share[: ffn_sizes[0]]
    share_down = ffn_share[ffn_sizes[0] : ffn_sizes[0] + ffn_sizes[1]]
    share_out = ffn_share[ffn_sizes[0] + ffn_sizes[1] : sum(ffn_sizes) + attn_sizes[2]]
    attn_parts = jnp.concatenate(
        [
            grad_query.reshape(count, -1).astype(jnp.bfloat16),
            grad_keyval.reshape(count, -1).astype(jnp.bfloat16),
        ],
        axis=1,
    )
    attn_rows = attn_parts.shape[1]
    attn_parts = jnp.pad(attn_parts, ((0, 0), (0, -attn_rows % 128)))
    attn_share = scatter_sum(attn_parts.reshape(count, -1, 128), 2).reshape(-1)
    share_query = attn_share[: attn_sizes[0]]
    share_keyval = attn_share[attn_sizes[0] : attn_sizes[0] + attn_sizes[1]]
    gain_sums = sum_all(jnp.stack([grad_gain_attn, grad_gain_ffn]))
    gain_attn_sum = gain_sums[0]
    gain_ffn_sum = gain_sums[1]
    return (
        mixed,
        token_grads,
        gain_attn_sum,
        share_query,
        share_keyval,
        share_out,
        gain_ffn_sum,
        share_gate_up,
        share_down,
    )


def solution(mesh):
    in_specs = (
        P("dev", None),
        P("dev"),
        P(),
        P("dev"),
        P("dev"),
        P("dev"),
        P(),
        P("dev"),
        P("dev"),
        P("dev", None),
    )
    out_specs = (
        P("dev", None),
        P("dev", None),
        P(),
        P("dev"),
        P("dev"),
        P("dev"),
        P(),
        P("dev"),
        P("dev"),
    )
    return jax.shard_map(shards, mesh=mesh, in_specs=in_specs, out_specs=out_specs, check_vma=False)
```

```python
import math

import jax
import jax.numpy as jnp
from jax import lax
from jax.experimental import pallas as pl
from jax.experimental.pallas import tpu as pltpu
from jax.sharding import PartitionSpec as P

D = 576
H = 9
KVH = 3
HD = 64
FF = 1536


norm_epsilon = 1e-05
theta_base = 100000.0


def passed_along(value, axis, steps):
    count = lax.axis_size(axis)
    first, last = (max(0, -steps), min(count, count - steps))
    return lax.ppermute(value, axis, [(source, source + steps) for source in range(first, last)])


def link_masks(count):
    bits = [1 << b for b in range(count.bit_length() - 1)]
    if count == 32:
        bits = [1, 2, 4, 8, 24]
    return bits[0], bits[1:]


def swapped(value, mask):
    count = lax.axis_size("dev")
    return lax.ppermute(value, "dev", [(i, i ^ mask) for i in range(count)])


def color_orders(count, colors):
    first, rest = link_masks(count)
    if colors == 1:
        return [rest + [first]]
    step = len(rest) // colors
    return [rest[c * step :] + rest[: c * step] + [first] for c in range(colors)]


def slot_masks(order):
    slots = [0]
    for mask in order:
        slots = slots + [s ^ mask for s in slots]
    return slots


def cut_rows(rows, colors):
    edges = [rows * c // colors for c in range(colors + 1)]
    return list(zip(edges[:-1], edges[1:]))


def gather_all(block, colors):
    count = lax.axis_size("dev")
    me = lax.axis_index("dev")
    orders = color_orders(count, colors)
    held = [block[a:b][None] for a, b in cut_rows(block.shape[0], colors)]
    for t in range(len(orders[0])):
        got = [swapped(h, order[t]) for h, order in zip(held, orders)]
        held = [jnp.concatenate([h, g], axis=0) for h, g in zip(held, got)]
    whole = []
    for h, order in zip(held, orders):
        slots = slot_masks(order)
        where = [0] * count
        for place, mask in enumerate(slots):
            where[mask] = place
        index = jnp.asarray(where, jnp.int32)[me ^ jnp.arange(count, dtype=jnp.int32)]
        whole.append(jnp.take(h, index, axis=0, mode="clip"))
    return jnp.concatenate(whole, axis=1)


def scatter_sum(parts, colors):
    count = lax.axis_size("dev")
    me = lax.axis_index("dev")
    orders = color_orders(count, colors)
    held = []
    for (a, b), order in zip(cut_rows(parts.shape[1], colors), orders):
        slots = jnp.asarray(slot_masks(order), jnp.int32)
        held.append(jnp.take(parts[:, a:b], me ^ slots, axis=0, mode="clip"))
    for t in range(len(orders[0])):
        half = held[0].shape[0] // 2
        masks = [order[-1 - t] for order in orders]
        got = [swapped(h[half:].astype(jnp.bfloat16), m) for h, m in zip(held, masks)]
        held = [h[:half].astype(jnp.float32) + g.astype(jnp.float32) for h, g in zip(held, got)]
    return jnp.concatenate([h[0] for h in held], axis=0)


def sum_all(value):
    first, rest = link_masks(lax.axis_size("dev"))
    for mask in [first] + rest:
        value = value + swapped(value, mask)
    return value


def norm_forward(values, scale_gain):
    inverse = lax.rsqrt(jnp.mean(values * values, axis=-1, keepdims=True) + norm_epsilon)
    return (values * inverse * scale_gain, inverse)


def norm_backward(grad_output, values, inverse, scale_gain):
    unit_rows = values * inverse
    scaled = grad_output * scale_gain
    grad_gain = jnp.sum(grad_output * unit_rows, axis=0)
    grad_input = inverse * (
        scaled - unit_rows * jnp.mean(scaled * unit_rows, axis=-1, keepdims=True)
    )
    return (grad_input, grad_gain)


def rope_angles(position_block):
    half_dim = HD // 2
    frequency = jnp.exp(
        jnp.arange(half_dim, dtype=jnp.float32) * (-2.0 * math.log(theta_base) / HD)
    )
    angles = position_block.astype(jnp.float32)[:, None] * frequency[None, :]
    return (jnp.cos(angles)[:, None, :], jnp.sin(angles)[:, None, :])


def rotate(values, cos_table, sin_table):
    half_dim = values.shape[-1] // 2
    first_half = values[..., :half_dim]
    second_half = values[..., half_dim:]
    return jnp.concatenate(
        [
            first_half * cos_table - second_half * sin_table,
            second_half * cos_table + first_half * sin_table,
        ],
        axis=-1,
    )


def project_heads(normed, query_mat, keyval_mat, cos_table, sin_table):
    row_count = normed.shape[0]
    queries = jnp.dot(normed, query_mat, preferred_element_type=jnp.float32).reshape(
        row_count, H, HD
    )
    keyvals = jnp.dot(normed, keyval_mat, preferred_element_type=jnp.float32)
    keys_rot = rotate(
        keyvals[:, : KVH * HD].reshape(row_count, KVH, HD), cos_table, sin_table
    ).reshape(row_count, KVH * HD)
    query_rot = (
        rotate(queries, cos_table, sin_table).reshape(row_count, H * HD).astype(jnp.bfloat16)
    )
    keyval_rot = jnp.concatenate([keys_rot, keyvals[:, KVH * HD :]], axis=1).astype(jnp.bfloat16)
    return (query_rot, keyval_rot)


def window_mask(position_block, row_count):
    query_at = jnp.arange(row_count, dtype=jnp.int32)[:, None] + row_count
    key_at = jnp.arange(2 * row_count, dtype=jnp.int32)[None, :]
    return (key_at <= query_at) & (key_at >= query_at - position_block[:, None])


def masked_scores(query_group, key_group, allowed):
    scale_factor = 1.0 / math.sqrt(HD)
    scores = (
        jnp.einsum("tqd,wd->qtw", query_group, key_group, preferred_element_type=jnp.float32)
        * scale_factor
    )
    return jnp.where(allowed[None], scores, -1e30)


def attend_forward(query_rot, window, allowed):
    row_count = query_rot.shape[0]
    grouped = H // KVH
    queries = query_rot.reshape(row_count, H, HD)
    outputs = []
    totals = []
    for group_index in range(KVH):
        query_group = queries[:, group_index * grouped : (group_index + 1) * grouped]
        key_group = window[:, group_index * HD : (group_index + 1) * HD]
        value_group = window[:, (KVH + group_index) * HD : (KVH + group_index + 1) * HD]
        scores = masked_scores(query_group, key_group, allowed)
        highest = jnp.max(scores, axis=-1, keepdims=True)
        log_total = highest + jnp.log(jnp.sum(jnp.exp(scores - highest), axis=-1, keepdims=True))
        probability = jnp.exp(scores - log_total).astype(jnp.bfloat16)
        head_out = jnp.einsum(
            "qtw,wd->tqd", probability, value_group, preferred_element_type=jnp.float32
        )
        outputs.append(head_out.astype(jnp.bfloat16))
        totals.append(log_total)
    return (jnp.concatenate(outputs, axis=1).reshape(row_count, H * HD), totals)


def attend_backward(query_rot, window, allowed, attended, grad_attended, totals):
    row_count = query_rot.shape[0]
    grouped = H // KVH
    scale_factor = 1.0 / math.sqrt(HD)
    queries = query_rot.reshape(row_count, H, HD)
    attended_heads = attended.reshape(row_count, H, HD)
    grad_heads = grad_attended.reshape(row_count, H, HD)
    query_grads = []
    key_grads = []
    value_grads = []
    for group_index in range(KVH):
        head_slice = slice(group_index * grouped, (group_index + 1) * grouped)
        query_group = queries[:, head_slice]
        key_group = window[:, group_index * HD : (group_index + 1) * HD]
        value_group = window[:, (KVH + group_index) * HD : (KVH + group_index + 1) * HD]
        scores = masked_scores(query_group, key_group, allowed)
        probability = jnp.exp(scores - totals[group_index])
        grad_group = grad_heads[:, head_slice]
        row_delta = jnp.sum(
            grad_group.astype(jnp.float32) * attended_heads[:, head_slice].astype(jnp.float32),
            axis=-1,
        )
        grad_prob = jnp.einsum(
            "tqd,wd->qtw", grad_group, value_group, preferred_element_type=jnp.float32
        )
        grad_scores = (probability * (grad_prob - row_delta.T[:, :, None]) * scale_factor).astype(
            jnp.bfloat16
        )
        query_grads.append(
            jnp.einsum("qtw,wd->tqd", grad_scores, key_group, preferred_element_type=jnp.float32)
        )
        key_grads.append(
            jnp.einsum("qtw,tqd->wd", grad_scores, query_group, preferred_element_type=jnp.float32)
        )
        value_grads.append(
            jnp.einsum(
                "qtw,tqd->wd",
                probability.astype(jnp.bfloat16),
                grad_group,
                preferred_element_type=jnp.float32,
            )
        )
    return (jnp.concatenate(query_grads, axis=1), jnp.concatenate(key_grads + value_grads, axis=1))


def shards_general(
    tokens, positions, gain_attn, w_query, w_kv, w_out, gain_ffn, w_gate_up, w_down, cotangent
):
    row_count = tokens.shape[0]
    width_kv = 2 * KVH * HD
    count = lax.axis_size("dev")
    attn_sizes = [w_query.shape[0], w_kv.shape[0], w_out.shape[0]]
    ffn_sizes = [w_gate_up.shape[0], w_down.shape[0]]
    attn_all = gather_all(jnp.concatenate([w_query, w_kv, w_out]).reshape(-1, 128), 2)
    attn_all = attn_all.reshape(count, -1)
    query_mat = attn_all[:, : attn_sizes[0]].reshape(D, H * HD)
    keyval_mat = attn_all[:, attn_sizes[0] : attn_sizes[0] + attn_sizes[1]].reshape(D, width_kv)
    out_mat = attn_all[:, attn_sizes[0] + attn_sizes[1] :].reshape(H * HD, D)
    ffn_all = gather_all(jnp.concatenate([w_gate_up, w_down]).reshape(-1, 128), 4)
    ffn_all = ffn_all.reshape(count, -1)
    gate_up_mat = ffn_all[:, : ffn_sizes[0]].reshape(D, 2 * FF)
    down_mat = ffn_all[:, ffn_sizes[0] :].reshape(FF, D)
    inputs = tokens.astype(jnp.float32)
    normed_attn, inverse_attn = norm_forward(inputs, gain_attn)
    normed_attn = normed_attn.astype(jnp.bfloat16)
    cos_table, sin_table = rope_angles(positions)
    query_rot, keyval_rot = project_heads(normed_attn, query_mat, keyval_mat, cos_table, sin_table)
    near_keys = passed_along(keyval_rot, "dev", 1)
    window = jnp.concatenate([near_keys, keyval_rot], axis=0)
    allowed = window_mask(positions, row_count)
    attended, totals = attend_forward(query_rot, window, allowed)
    residual = inputs + jnp.dot(attended, out_mat, preferred_element_type=jnp.float32)
    normed_ffn, inverse_ffn = norm_forward(residual, gain_ffn)
    normed_ffn = normed_ffn.astype(jnp.bfloat16)
    gate_up = jnp.dot(normed_ffn, gate_up_mat, preferred_element_type=jnp.float32)
    gate_part = gate_up[:, :FF]
    up_part = gate_up[:, FF:]
    activated = (jax.nn.silu(gate_part) * up_part).astype(jnp.bfloat16)
    mixed = (residual + jnp.dot(activated, down_mat, preferred_element_type=jnp.float32)).astype(
        jnp.bfloat16
    )
    grad_act = jnp.dot(cotangent, down_mat.T, preferred_element_type=jnp.float32)
    sigmoid_gate = jax.nn.sigmoid(gate_part)
    grad_gate_up_act = jnp.concatenate(
        [
            grad_act * up_part * sigmoid_gate * (1.0 + gate_part * (1.0 - sigmoid_gate)),
            grad_act * jax.nn.silu(gate_part),
        ],
        axis=1,
    ).astype(jnp.bfloat16)
    grad_down = jnp.dot(activated.T, cotangent, preferred_element_type=jnp.float32)
    grad_gate_up = jnp.dot(normed_ffn.T, grad_gate_up_act, preferred_element_type=jnp.float32)
    grad_normed_ffn = jnp.dot(grad_gate_up_act, gate_up_mat.T, preferred_element_type=jnp.float32)
    grad_norm_ffn, grad_gain_ffn = norm_backward(grad_normed_ffn, residual, inverse_ffn, gain_ffn)
    grad_residual = cotangent.astype(jnp.float32) + grad_norm_ffn
    grad_residual_b = grad_residual.astype(jnp.bfloat16)
    grad_out = jnp.dot(attended.T, grad_residual_b, preferred_element_type=jnp.float32)
    grad_attended = jnp.dot(grad_residual_b, out_mat.T, preferred_element_type=jnp.float32).astype(
        jnp.bfloat16
    )
    grad_query_rot, grad_window = attend_backward(
        query_rot, window, allowed, attended, grad_attended, totals
    )
    back_near = passed_along(grad_window[:row_count].astype(jnp.bfloat16), "dev", -1).astype(jnp.float32)
    grad_keyval_rot = grad_window[row_count:] + back_near
    key_part = rotate(
        grad_keyval_rot[:, : KVH * HD].reshape(row_count, KVH, HD), cos_table, -sin_table
    ).reshape(row_count, KVH * HD)
    grad_keyval_act = jnp.concatenate([key_part, grad_keyval_rot[:, KVH * HD :]], axis=1).astype(
        jnp.bfloat16
    )
    grad_query_act = (
        rotate(grad_query_rot, cos_table, -sin_table)
        .reshape(row_count, H * HD)
        .astype(jnp.bfloat16)
    )
    grad_query = jnp.dot(normed_attn.T, grad_query_act, preferred_element_type=jnp.float32)
    grad_keyval = jnp.dot(normed_attn.T, grad_keyval_act, preferred_element_type=jnp.float32)
    grad_normed_attn = jnp.dot(
        grad_query_act, query_mat.T, preferred_element_type=jnp.float32
    ) + jnp.dot(grad_keyval_act, keyval_mat.T, preferred_element_type=jnp.float32)
    grad_input, grad_gain_attn = norm_backward(grad_normed_attn, inputs, inverse_attn, gain_attn)
    token_grads = grad_residual + grad_input
    ffn_parts = jnp.concatenate(
        [
            grad_gate_up.reshape(count, -1).astype(jnp.bfloat16),
            grad_down.reshape(count, -1).astype(jnp.bfloat16),
            grad_out.reshape(count, -1).astype(jnp.bfloat16),
        ],
        axis=1,
    )
    ffn_parts = jnp.pad(ffn_parts, ((0, 0), (0, -ffn_parts.shape[1] % 128)))
    ffn_share = scatter_sum(ffn_parts.reshape(count, -1, 128), 4).reshape(-1)
    share_gate_up = ffn_share[: ffn_sizes[0]]
    share_down = ffn_share[ffn_sizes[0] : ffn_sizes[0] + ffn_sizes[1]]
    share_out = ffn_share[ffn_sizes[0] + ffn_sizes[1] : sum(ffn_sizes) + attn_sizes[2]]
    attn_parts = jnp.concatenate(
        [
            grad_query.reshape(count, -1).astype(jnp.bfloat16),
            grad_keyval.reshape(count, -1).astype(jnp.bfloat16),
        ],
        axis=1,
    )
    attn_rows = attn_parts.shape[1]
    attn_parts = jnp.pad(attn_parts, ((0, 0), (0, -attn_rows % 128)))
    attn_share = scatter_sum(attn_parts.reshape(count, -1, 128), 2).reshape(-1)
    share_query = attn_share[: attn_sizes[0]]
    share_keyval = attn_share[attn_sizes[0] : attn_sizes[0] + attn_sizes[1]]
    gain_sums = sum_all(jnp.stack([grad_gain_attn, grad_gain_ffn]))
    gain_attn_sum = gain_sums[0]
    gain_ffn_sum = gain_sums[1]
    return (
        mixed,
        token_grads,
        gain_attn_sum,
        share_query,
        share_keyval,
        share_out,
        gain_ffn_sum,
        share_gate_up,
        share_down,
    )


PAD = 24
CHUNK = 128
bf16 = jnp.bfloat16
f32 = jnp.float32


def dot_nn(a, b):
    return lax.dot_general(a, b, (((1,), (0,)), ((), ())), preferred_element_type=f32)


def dot_nt(a, b):
    return lax.dot_general(a, b, (((1,), (1,)), ((), ())), preferred_element_type=f32)


def split_two(value):
    high = value.astype(bf16)
    return high, (value - high.astype(f32)).astype(bf16)


def spread_wide(source_row):
    rows = lax.broadcasted_iota(jnp.int32, (D, source_row.shape[1]), 0)
    return jnp.where(rows == source_row, 1.0, 0.0).astype(bf16)


def spread_tall(source_col):
    lanes = lax.broadcasted_iota(jnp.int32, (source_col.shape[0], D), 1)
    return jnp.where(lanes == source_col, 1.0, 0.0).astype(bf16)


def turn(a, b, cos_table, sin_table):
    return a * cos_table - b * sin_table, b * cos_table + a * sin_table


def project_kernel(tok, gain, cos, sin, src_a, src_b, wa0, wa1, wb0, wb1, q_out, kv_out):
    x = tok[...].astype(f32)
    inverse = lax.rsqrt(jnp.mean(x * x, axis=0, keepdims=True) + norm_epsilon)
    normed = (x * inverse * gain[...]).astype(bf16).T
    cos_table, sin_table = cos[...], sin[...]
    wa = jnp.concatenate([wa0[...], wa1[...]], axis=0)
    wb = jnp.concatenate([wb0[...], wb1[...]], axis=0)
    wide_a = dot_nn(normed, spread_wide(src_a[...])).astype(bf16)
    wide_b = dot_nn(normed, spread_wide(src_b[...])).astype(bf16)
    qk = dot_nn(wide_a, wa).T
    v = dot_nn(wide_b, wb).T[H * HD :]
    half = HD // 2
    for h in range(H + KVH):
        a = qk[h * HD : h * HD + half]
        b = qk[h * HD + half : (h + 1) * HD]
        ra, rb = turn(a, b, cos_table, sin_table)
        out, row = (q_out, h * HD) if h < H else (kv_out, (h - H) * HD)
        out[row : row + half, :] = ra.astype(bf16)
        out[row + half : row + HD, :] = rb.astype(bf16)
    kv_out[KVH * HD :, :] = v.astype(bf16)


def attend_kernel(q, near, own, pos, prob_out, att_out):
    tokens = q.shape[1]
    group = H // KVH
    scale = 1.0 / math.sqrt(HD)
    span = tokens + CHUNK
    rows = lax.broadcasted_iota(jnp.int32, (span, CHUNK), 0)
    lanes = lax.broadcasted_iota(jnp.int32, (span, CHUNK), 1) + tokens
    for g in range(KVH):
        kw = jnp.concatenate(
            [near[g * HD : (g + 1) * HD, :], own[g * HD : (g + 1) * HD, :]], axis=1
        ).T
        low = (KVH + g) * HD
        vw = jnp.concatenate([near[low : low + HD, :], own[low : low + HD, :]], axis=1)
        for c in range(tokens // CHUNK):
            base = c * CHUNK
            position = pos[:, base : base + CHUNK]
            allowed = (rows <= lanes) & (rows >= lanes - position)
            for i in range(group):
                h = g * group + i
                qh = q[h * HD : (h + 1) * HD, base : base + CHUNK]
                scores = dot_nn(kw[base : base + span], qh) * scale
                scores = jnp.where(allowed, scores, -1e30)
                highest = jnp.max(scores, axis=0, keepdims=True)
                e = jnp.exp(scores - highest)
                total = jnp.sum(e, axis=0, keepdims=True)
                p = (e * (1.0 / total)).astype(bf16)
                prob_out[g, c, :, i * CHUNK : (i + 1) * CHUNK] = p
                att_out[h * HD : (h + 1) * HD, base : base + CHUNK] = dot_nn(
                    vw[:, base : base + span], p
                ).astype(bf16)


def attend_back_kernel(
    q, near, own, prob, att, grad_att, cos, sin, dq_out, dnear_out, down_out, dk, dv
):
    tokens = q.shape[1]
    group = H // KVH
    scale = 1.0 / math.sqrt(HD)
    span = tokens + CHUNK
    half = HD // 2
    for g in range(KVH):
        low = (KVH + g) * HD
        kw = jnp.concatenate(
            [near[g * HD : (g + 1) * HD, :], own[g * HD : (g + 1) * HD, :]], axis=1
        )
        vw = jnp.concatenate([near[low : low + HD, :], own[low : low + HD, :]], axis=1).T
        dk[...] = jnp.zeros_like(dk)
        dv[...] = jnp.zeros_like(dv)
        for c in range(tokens // CHUNK):
            base = c * CHUNK
            cut = slice(base, base + CHUNK)
            heads = [g * group + i for i in range(group)]
            q_all = jnp.concatenate([q[h * HD : (h + 1) * HD, cut] for h in heads], axis=1)
            g_all = jnp.concatenate([grad_att[h * HD : (h + 1) * HD, cut] for h in heads], axis=1)
            a_all = jnp.concatenate([att[h * HD : (h + 1) * HD, cut] for h in heads], axis=1)
            delta = jnp.sum(g_all.astype(f32) * a_all.astype(f32), axis=0, keepdims=True)
            p = prob[g, c]
            grad_prob = dot_nn(vw[base : base + span], g_all)
            ds = (p.astype(f32) * (grad_prob - delta) * scale).astype(bf16)
            dq = dot_nn(kw[:, base : base + span], ds)
            dk[:, base : base + span] += dot_nt(q_all, ds)
            dv[:, base : base + span] += dot_nt(g_all, p)
            for i, h in enumerate(heads):
                part = dq[:, i * CHUNK : (i + 1) * CHUNK]
                ra, rb = turn(part[:half], part[half:], cos[:, cut], -sin[:, cut])
                dq_out[h * HD : h * HD + half, cut] = ra.astype(bf16)
                dq_out[h * HD + half : (h + 1) * HD, cut] = rb.astype(bf16)
        dnear_out[g * HD : (g + 1) * HD, :] = dk[:, :tokens].astype(bf16)
        dnear_out[low : low + HD, :] = dv[:, :tokens].astype(bf16)
        down_out[g * HD : (g + 1) * HD, :] = dk[:, tokens:]
        down_out[low : low + HD, :] = dv[:, tokens:]


def feed_kernel(
    slots,
    att,
    tok,
    cot,
    gain,
    src_b,
    src_g,
    src_u,
    src_d,
    wb0,
    wb1,
    wg0,
    wg1,
    wu0,
    wu1,
    wd0,
    wd1,
    mixed_out,
    gres_out,
    gatt_out,
    dgain_out,
    dg_out,
    du_out,
    dd_out,
    wd,
    act,
    dgate,
    dup,
    wide_g,
    wide_u,
):
    count = slots.shape[0]
    rows_d = FF // count
    for p in range(count):
        half, at = (wd0, p) if p < count // 2 else (wd1, p - count // 2)
        target = pl.multiple_of(slots[p] * rows_d, rows_d)
        wd[pl.ds(target, rows_d), :] = half[at * rows_d : (at + 1) * rows_d, :]
    wb = jnp.concatenate([wb0[...], wb1[...]], axis=0)
    spread_b = spread_wide(src_b[...])
    spread_g = spread_wide(src_g[...])
    spread_u = spread_wide(src_u[...])
    cot_tok = cot[...].T
    att_wide = dot_nn(att[...].T, spread_b).astype(bf16)
    residual = tok[...].astype(f32).T + dot_nn(att_wide, wb)[:, :D]
    inverse = lax.rsqrt(jnp.mean(residual * residual, axis=-1, keepdims=True) + norm_epsilon)
    normed = (residual * inverse * gain[...]).astype(bf16)
    wide_g[...] = dot_nn(normed, spread_g).astype(bf16)
    wide_u[...] = dot_nn(normed, spread_u).astype(bf16)
    block = 256

    def ff_step(j, carry):
        cut = pl.ds(pl.multiple_of(j * block, block), block)
        gate = dot_nn(wide_g[...], jnp.concatenate([wg0[:, cut], wg1[:, cut]], axis=0))
        up = dot_nn(wide_u[...], jnp.concatenate([wu0[:, cut], wu1[:, cut]], axis=0))
        grad_act = dot_nt(cot_tok, wd[cut, :])
        sig = jax.nn.sigmoid(gate)
        silu = gate * sig
        act[:, cut] = (silu * up).astype(bf16)
        dgate[:, cut] = (grad_act * up * sig * (1.0 + gate * (1.0 - sig))).astype(bf16)
        dup[:, cut] = (grad_act * silu).astype(bf16)
        return carry

    lax.fori_loop(0, FF // block, ff_step, 0)
    mixed = residual + dot_nn(act[...], wd[...])
    mixed_out[...] = mixed.T.astype(bf16)
    dn_g = dot_nt(dgate[...], jnp.concatenate([wg0[...], wg1[...]], axis=0))
    dn_u = dot_nt(dup[...], jnp.concatenate([wu0[...], wu1[...]], axis=0))
    grad_normed = sum(dot_nt(part, spread_g) for part in split_two(dn_g)) + sum(
        dot_nt(part, spread_u) for part in split_two(dn_u)
    )
    unit = residual * inverse
    scaled = grad_normed * gain[...]
    dgain_out[...] = jnp.sum(grad_normed * unit, axis=0, keepdims=True)
    grad_res = cot_tok.astype(f32) + inverse * (
        scaled - unit * jnp.mean(scaled * unit, axis=-1, keepdims=True)
    )
    gres_out[...] = grad_res.T
    grad_res_b = grad_res.astype(bf16)
    gatt_wide = dot_nt(wb[:, :D], grad_res_b).astype(bf16)
    gatt_out[...] = dot_nn(spread_b, gatt_wide).astype(bf16)
    dg_out[...] = dot_nn(wide_g[...].T, dgate[...]).astype(bf16)
    du_out[...] = dot_nn(wide_u[...].T, dup[...]).astype(bf16)
    d_out = dot_nn(dot_nn(spread_tall(src_d[...]), att[...]).astype(bf16), grad_res_b).astype(bf16)
    wd[...] = dot_nn(act[...].T, cot_tok).astype(bf16)
    rows_all = rows_d + PAD
    for p in range(count):
        source = pl.multiple_of(slots[p] * rows_d, rows_d)
        dd_out[p * rows_all : p * rows_all + rows_d, :] = wd[pl.ds(source, rows_d), :]
        dd_out[p * rows_all + rows_d : (p + 1) * rows_all, :] = d_out[p * PAD : (p + 1) * PAD]


def finish_kernel(
    dq,
    own,
    back,
    tok,
    gain,
    cos,
    sin,
    gres,
    src_a,
    src_b,
    tall_a,
    tall_b,
    wa0,
    wa1,
    wb0,
    wb1,
    dtok_out,
    dgain_out,
    da_out,
    dv_out,
):
    x = tok[...].astype(f32)
    inverse = lax.rsqrt(jnp.mean(x * x, axis=0, keepdims=True) + norm_epsilon)
    unit = x * inverse
    normed = (unit * gain[...]).astype(bf16)
    total = own[...] + back[...].astype(f32)
    half = HD // 2
    parts = [dq[...]]
    for g in range(KVH):
        ra, rb = turn(
            total[g * HD : g * HD + half],
            total[g * HD + half : (g + 1) * HD],
            cos[...],
            -sin[...],
        )
        parts += [ra.astype(bf16), rb.astype(bf16)]
    dqk = jnp.concatenate(parts, axis=0)
    dv = total[KVH * HD :].astype(bf16)
    wa = jnp.concatenate([wa0[...], wa1[...]], axis=0)
    wb = jnp.concatenate([wb0[...], wb1[...]], axis=0)
    dvx = jnp.concatenate([jnp.zeros((H * HD, dv.shape[1]), bf16), dv], axis=0)
    dn_a = dot_nn(wa, dqk)
    dn_b = dot_nn(wb, dvx)
    spread_a = spread_wide(src_a[...])
    spread_b = spread_wide(src_b[...])
    grad_normed = sum(dot_nn(spread_a, part) for part in split_two(dn_a)) + sum(
        dot_nn(spread_b, part) for part in split_two(dn_b)
    )
    scaled = grad_normed * gain[...]
    dgain_out[...] = jnp.sum(grad_normed * unit, axis=1, keepdims=True)
    dtok_out[...] = gres[...] + inverse * (
        scaled - unit * jnp.mean(scaled * unit, axis=0, keepdims=True)
    )
    wide_a = dot_nn(spread_tall(tall_a[...]), normed).astype(bf16)
    wide_b = dot_nn(spread_tall(tall_b[...]), normed).astype(bf16)
    da_out[...] = dot_nt(wide_a, dqk).astype(bf16)
    dv_out[...] = dot_nt(wide_b, dv).astype(bf16)


def call_whole(kernel, outs, operands, scratch=(), scalars=()):
    vmem = pl.BlockSpec(memory_space=pltpu.VMEM)
    smem = pl.BlockSpec(memory_space=pltpu.SMEM)
    return pl.pallas_call(
        kernel,
        out_shape=[jax.ShapeDtypeStruct(s, d) for s, d in outs],
        in_specs=[smem] * len(scalars) + [vmem] * len(operands),
        out_specs=[vmem] * len(outs),
        scratch_shapes=list(scratch),
        compiler_params=pltpu.CompilerParams(vmem_limit_bytes=60 * 1024 * 1024),
    )(*scalars, *operands)


def doubled(streams, orders):
    held = list(streams)
    got = None
    for t in range(len(orders[0])):
        got = [swapped(h, order[t]) for h, order in zip(held, orders)]
        if t < len(orders[0]) - 1:
            held = [jnp.concatenate([h, g], axis=0) for h, g in zip(held, got)]
    return list(zip(held, got))


def halved(streams, orders):
    held = list(streams)
    for t in range(len(orders[0])):
        half = held[0].shape[0] // 2
        halves = [h.shape[0] // 2 for h in held]
        got = [
            swapped(h[k:].astype(bf16), order[-1 - t])
            for h, k, order in zip(held, halves, orders)
        ]
        held = [h[:k].astype(f32) + g.astype(f32) for h, k, g in zip(held, halves, got)]
    return held


def sources(order, count, per_slot):
    me = lax.axis_index("dev")
    owner = me ^ jnp.asarray(slot_masks(order), jnp.int32)
    inner = jnp.arange(PAD, dtype=jnp.int32)[None, :]
    value = jnp.where(inner < per_slot, owner[:, None] * per_slot + inner, -1)
    return value.reshape(-1)


def padded_rows(value):
    return jnp.pad(value, ((0, PAD - value.shape[0]), (0, 0)))


def shards(
    tokens, positions, gain_attn, w_query, w_kv, w_out, gain_ffn, w_gate_up, w_down, cotangent
):
    count = lax.axis_size("dev")
    me = lax.axis_index("dev")
    row_count = tokens.shape[0]
    per = D // count
    per_d = FF // count
    first, rest = link_masks(count)
    order_of = [rest[k:] + rest[:k] + [first] for k in range(len(rest))]
    ord_a, ord_b = order_of[0], order_of[2]
    ord_g, ord_u, ord_d = order_of[1], order_of[2], order_of[3]
    src_a, src_b = sources(ord_a, count, per), sources(ord_b, count, per)
    src_g, src_u = sources(ord_g, count, per), sources(ord_u, count, per)
    src_d = sources(ord_d, count, per)
    slots = me ^ jnp.asarray(slot_masks(ord_d), jnp.int32)
    w_qs, w_kvs = w_query.reshape(per, H * HD), w_kv.reshape(per, 2 * KVH * HD)
    w_gs = w_gate_up.reshape(per, 2 * FF)
    kv_cut = KVH * HD
    stream_a = padded_rows(jnp.concatenate([w_qs, w_kvs[:, :kv_cut]], axis=1))
    stream_b = padded_rows(jnp.concatenate([w_out.reshape(per, D), w_kvs[:, kv_cut:]], axis=1))
    (wa0, wa1), (wb0, wb1) = doubled([stream_a, stream_b], [ord_a, ord_b])
    stream_g, stream_u = padded_rows(w_gs[:, :FF]), padded_rows(w_gs[:, FF:])
    stream_d = w_down.reshape(per_d, D)
    (wg0, wg1), (wu0, wu1), (wd0, wd1) = doubled(
        [stream_g, stream_u, stream_d], [ord_g, ord_u, ord_d]
    )
    half_dim = HD // 2
    frequency = jnp.exp(jnp.arange(half_dim, dtype=f32) * (-2.0 * math.log(theta_base) / HD))
    angles = frequency[:, None] * positions.astype(f32)[None, :]
    cos, sin = jnp.cos(angles), jnp.sin(angles)
    tok_t, cot_t = tokens.T, cotangent.T
    gain_col = gain_attn.reshape(D, 1)
    q_t, kv_t = call_whole(
        project_kernel,
        [((H * HD, row_count), bf16), ((2 * kv_cut, row_count), bf16)],
        [tok_t, gain_col, cos, sin, src_a[None], src_b[None], wa0, wa1, wb0, wb1],
    )
    near = passed_along(kv_t, "dev", 1)
    chunks = row_count // CHUNK
    prob, att_t = call_whole(
        attend_kernel,
        [
            ((KVH, chunks, row_count + CHUNK, H // KVH * CHUNK), bf16),
            ((H * HD, row_count), bf16),
        ],
        [q_t, near, kv_t, positions[None]],
    )
    wide = count * PAD
    mixed_t, gres_t, gatt_t, dgain_ffn, dg, du, dd = call_whole(
        feed_kernel,
        [
            ((D, row_count), bf16),
            ((D, row_count), f32),
            ((H * HD, row_count), bf16),
            ((1, D), f32),
            ((wide, FF), bf16),
            ((wide, FF), bf16),
            ((count * (per_d + PAD), D), bf16),
        ],
        [
            att_t,
            tok_t,
            cot_t,
            gain_ffn[None],
            src_b[None],
            src_g[None],
            src_u[None],
            src_d[:, None],
            wb0,
            wb1,
            wg0,
            wg1,
            wu0,
            wu1,
            wd0,
            wd1,
        ],
        scratch=[
            pltpu.VMEM((FF, D), bf16),
            pltpu.VMEM((row_count, FF), bf16),
            pltpu.VMEM((row_count, FF), bf16),
            pltpu.VMEM((row_count, FF), bf16),
            pltpu.VMEM((row_count, wide), bf16),
            pltpu.VMEM((row_count, wide), bf16),
        ],
        scalars=[slots],
    )
    share_g, share_u, share_d = halved([dg, du, dd], [ord_g, ord_u, ord_d])
    dq_t, dnear, down = call_whole(
        attend_back_kernel,
        [
            ((H * HD, row_count), bf16),
            ((2 * kv_cut, row_count), bf16),
            ((2 * kv_cut, row_count), f32),
        ],
        [q_t, near, kv_t, prob, att_t, gatt_t, cos, sin],
        scratch=[pltpu.VMEM((HD, 2 * row_count), f32)] * 2,
    )
    back = passed_along(dnear, "dev", -1)
    dtok_t, dgain_attn, da, dv = call_whole(
        finish_kernel,
        [
            ((D, row_count), f32),
            ((D, 1), f32),
            ((wide, H * HD + kv_cut), bf16),
            ((wide, kv_cut), bf16),
        ],
        [
            dq_t,
            down,
            back,
            tok_t,
            gain_col,
            cos,
            sin,
            gres_t,
            src_a[None],
            src_b[None],
            src_a[:, None],
            src_b[:, None],
            wa0,
            wa1,
            wb0,
            wb1,
        ],
    )
    share_a, share_v = halved([da, dv], [ord_a, ord_b])
    gain_sums = sum_all(jnp.concatenate([dgain_attn.reshape(1, D), dgain_ffn], axis=0))
    share_kv = jnp.concatenate([share_a[:per, H * HD :], share_v[:per]], axis=1)
    share_gu = jnp.concatenate([share_g[:per], share_u[:per]], axis=1)
    return (
        mixed_t.T,
        dtok_t.T,
        gain_sums[0],
        share_a[:per, : H * HD].reshape(-1),
        share_kv.reshape(-1),
        share_d[per_d : per_d + per].reshape(-1),
        gain_sums[1],
        share_gu.reshape(-1),
        share_d[:per_d].reshape(-1),
    )


def fits_whole_rows(count):
    per = D // count
    return D % count == 0 and FF % count == 0 and (FF // count) % 16 == 0 and 16 <= per <= PAD


def solution(mesh):
    in_specs = (
        P("dev", None),
        P("dev"),
        P(),
        P("dev"),
        P("dev"),
        P("dev"),
        P(),
        P("dev"),
        P("dev"),
        P("dev", None),
    )
    out_specs = (
        P("dev", None),
        P("dev", None),
        P(),
        P("dev"),
        P("dev"),
        P("dev"),
        P(),
        P("dev"),
        P("dev"),
    )
    return jax.shard_map(
        shards if fits_whole_rows(mesh.shape["dev"]) else shards_general, mesh=mesh, in_specs=in_specs, out_specs=out_specs, check_vma=False)
```

```python
import math

import jax
import jax.numpy as jnp
from jax import lax
from jax.experimental import pallas as pl
from jax.experimental.pallas import tpu as pltpu
from jax.sharding import PartitionSpec as P


D = 576
H = 9
KVH = 3
HD = 64
FF = 1536


norm_epsilon = 1e-05
theta_base = 100000.0


def passed_along(value, axis, steps):
    count = lax.axis_size(axis)
    first, last = (max(0, -steps), min(count, count - steps))
    return lax.ppermute(value, axis, [(source, source + steps) for source in range(first, last)])


def link_masks(count):
    bits = [1 << b for b in range(count.bit_length() - 1)]
    if count == 32:
        bits = [1, 2, 4, 8, 24]
    return bits[0], bits[1:]


def swapped(value, mask):
    count = lax.axis_size("dev")
    return lax.ppermute(value, "dev", [(i, i ^ mask) for i in range(count)])


def color_orders(count, colors):
    first, rest = link_masks(count)
    if colors == 1:
        return [rest + [first]]
    step = len(rest) // colors
    return [rest[c * step :] + rest[: c * step] + [first] for c in range(colors)]


def slot_masks(order):
    slots = [0]
    for mask in order:
        slots = slots + [s ^ mask for s in slots]
    return slots


def cut_rows(rows, colors):
    edges = [rows * c // colors for c in range(colors + 1)]
    return list(zip(edges[:-1], edges[1:]))


def gather_all(block, colors):
    count = lax.axis_size("dev")
    me = lax.axis_index("dev")
    orders = color_orders(count, colors)
    held = [block[a:b][None] for a, b in cut_rows(block.shape[0], colors)]
    for t in range(len(orders[0])):
        got = [swapped(h, order[t]) for h, order in zip(held, orders)]
        held = [jnp.concatenate([h, g], axis=0) for h, g in zip(held, got)]
    whole = []
    for h, order in zip(held, orders):
        slots = slot_masks(order)
        where = [0] * count
        for place, mask in enumerate(slots):
            where[mask] = place
        index = jnp.asarray(where, jnp.int32)[me ^ jnp.arange(count, dtype=jnp.int32)]
        whole.append(jnp.take(h, index, axis=0, mode="clip"))
    return jnp.concatenate(whole, axis=1)


def scatter_sum(parts, colors):
    count = lax.axis_size("dev")
    me = lax.axis_index("dev")
    orders = color_orders(count, colors)
    held = []
    for (a, b), order in zip(cut_rows(parts.shape[1], colors), orders):
        slots = jnp.asarray(slot_masks(order), jnp.int32)
        held.append(jnp.take(parts[:, a:b], me ^ slots, axis=0, mode="clip"))
    for t in range(len(orders[0])):
        half = held[0].shape[0] // 2
        masks = [order[-1 - t] for order in orders]
        got = [swapped(h[half:].astype(jnp.bfloat16), m) for h, m in zip(held, masks)]
        held = [h[:half].astype(jnp.float32) + g.astype(jnp.float32) for h, g in zip(held, got)]
    return jnp.concatenate([h[0] for h in held], axis=0)


def sum_all(value):
    first, rest = link_masks(lax.axis_size("dev"))
    for mask in [first] + rest:
        value = value + swapped(value, mask)
    return value


def norm_forward(values, scale_gain):
    inverse = lax.rsqrt(jnp.mean(values * values, axis=-1, keepdims=True) + norm_epsilon)
    return (values * inverse * scale_gain, inverse)


def norm_backward(grad_output, values, inverse, scale_gain):
    unit_rows = values * inverse
    scaled = grad_output * scale_gain
    grad_gain = jnp.sum(grad_output * unit_rows, axis=0)
    grad_input = inverse * (
        scaled - unit_rows * jnp.mean(scaled * unit_rows, axis=-1, keepdims=True)
    )
    return (grad_input, grad_gain)


def rope_angles(position_block):
    half_dim = HD // 2
    frequency = jnp.exp(
        jnp.arange(half_dim, dtype=jnp.float32) * (-2.0 * math.log(theta_base) / HD)
    )
    angles = position_block.astype(jnp.float32)[:, None] * frequency[None, :]
    return (jnp.cos(angles)[:, None, :], jnp.sin(angles)[:, None, :])


def rotate(values, cos_table, sin_table):
    half_dim = values.shape[-1] // 2
    first_half = values[..., :half_dim]
    second_half = values[..., half_dim:]
    return jnp.concatenate(
        [
            first_half * cos_table - second_half * sin_table,
            second_half * cos_table + first_half * sin_table,
        ],
        axis=-1,
    )


def project_heads(normed, query_mat, keyval_mat, cos_table, sin_table):
    row_count = normed.shape[0]
    queries = jnp.dot(normed, query_mat, preferred_element_type=jnp.float32).reshape(
        row_count, H, HD
    )
    keyvals = jnp.dot(normed, keyval_mat, preferred_element_type=jnp.float32)
    keys_rot = rotate(
        keyvals[:, : KVH * HD].reshape(row_count, KVH, HD), cos_table, sin_table
    ).reshape(row_count, KVH * HD)
    query_rot = (
        rotate(queries, cos_table, sin_table).reshape(row_count, H * HD).astype(jnp.bfloat16)
    )
    keyval_rot = jnp.concatenate([keys_rot, keyvals[:, KVH * HD :]], axis=1).astype(jnp.bfloat16)
    return (query_rot, keyval_rot)


def window_mask(position_block, row_count):
    query_at = jnp.arange(row_count, dtype=jnp.int32)[:, None] + row_count
    key_at = jnp.arange(2 * row_count, dtype=jnp.int32)[None, :]
    return (key_at <= query_at) & (key_at >= query_at - position_block[:, None])


def masked_scores(query_group, key_group, allowed):
    scale_factor = 1.0 / math.sqrt(HD)
    scores = (
        jnp.einsum("tqd,wd->qtw", query_group, key_group, preferred_element_type=jnp.float32)
        * scale_factor
    )
    return jnp.where(allowed[None], scores, -1e30)


def attend_forward(query_rot, window, allowed):
    row_count = query_rot.shape[0]
    grouped = H // KVH
    queries = query_rot.reshape(row_count, H, HD)
    outputs = []
    totals = []
    for group_index in range(KVH):
        query_group = queries[:, group_index * grouped : (group_index + 1) * grouped]
        key_group = window[:, group_index * HD : (group_index + 1) * HD]
        value_group = window[:, (KVH + group_index) * HD : (KVH + group_index + 1) * HD]
        scores = masked_scores(query_group, key_group, allowed)
        highest = jnp.max(scores, axis=-1, keepdims=True)
        log_total = highest + jnp.log(jnp.sum(jnp.exp(scores - highest), axis=-1, keepdims=True))
        probability = jnp.exp(scores - log_total).astype(jnp.bfloat16)
        head_out = jnp.einsum(
            "qtw,wd->tqd", probability, value_group, preferred_element_type=jnp.float32
        )
        outputs.append(head_out.astype(jnp.bfloat16))
        totals.append(log_total)
    return (jnp.concatenate(outputs, axis=1).reshape(row_count, H * HD), totals)


def attend_backward(query_rot, window, allowed, attended, grad_attended, totals):
    row_count = query_rot.shape[0]
    grouped = H // KVH
    scale_factor = 1.0 / math.sqrt(HD)
    queries = query_rot.reshape(row_count, H, HD)
    attended_heads = attended.reshape(row_count, H, HD)
    grad_heads = grad_attended.reshape(row_count, H, HD)
    query_grads = []
    key_grads = []
    value_grads = []
    for group_index in range(KVH):
        head_slice = slice(group_index * grouped, (group_index + 1) * grouped)
        query_group = queries[:, head_slice]
        key_group = window[:, group_index * HD : (group_index + 1) * HD]
        value_group = window[:, (KVH + group_index) * HD : (KVH + group_index + 1) * HD]
        scores = masked_scores(query_group, key_group, allowed)
        probability = jnp.exp(scores - totals[group_index])
        grad_group = grad_heads[:, head_slice]
        row_delta = jnp.sum(
            grad_group.astype(jnp.float32) * attended_heads[:, head_slice].astype(jnp.float32),
            axis=-1,
        )
        grad_prob = jnp.einsum(
            "tqd,wd->qtw", grad_group, value_group, preferred_element_type=jnp.float32
        )
        grad_scores = (probability * (grad_prob - row_delta.T[:, :, None]) * scale_factor).astype(
            jnp.bfloat16
        )
        query_grads.append(
            jnp.einsum("qtw,wd->tqd", grad_scores, key_group, preferred_element_type=jnp.float32)
        )
        key_grads.append(
            jnp.einsum("qtw,tqd->wd", grad_scores, query_group, preferred_element_type=jnp.float32)
        )
        value_grads.append(
            jnp.einsum(
                "qtw,tqd->wd",
                probability.astype(jnp.bfloat16),
                grad_group,
                preferred_element_type=jnp.float32,
            )
        )
    return (jnp.concatenate(query_grads, axis=1), jnp.concatenate(key_grads + value_grads, axis=1))


def shards_general(
    tokens, positions, gain_attn, w_query, w_kv, w_out, gain_ffn, w_gate_up, w_down, cotangent
):
    row_count = tokens.shape[0]
    width_kv = 2 * KVH * HD
    count = lax.axis_size("dev")
    attn_sizes = [w_query.shape[0], w_kv.shape[0], w_out.shape[0]]
    ffn_sizes = [w_gate_up.shape[0], w_down.shape[0]]
    attn_all = gather_all(jnp.concatenate([w_query, w_kv, w_out]).reshape(-1, 128), 2)
    attn_all = attn_all.reshape(count, -1)
    query_mat = attn_all[:, : attn_sizes[0]].reshape(D, H * HD)
    keyval_mat = attn_all[:, attn_sizes[0] : attn_sizes[0] + attn_sizes[1]].reshape(D, width_kv)
    out_mat = attn_all[:, attn_sizes[0] + attn_sizes[1] :].reshape(H * HD, D)
    ffn_all = gather_all(jnp.concatenate([w_gate_up, w_down]).reshape(-1, 128), 4)
    ffn_all = ffn_all.reshape(count, -1)
    gate_up_mat = ffn_all[:, : ffn_sizes[0]].reshape(D, 2 * FF)
    down_mat = ffn_all[:, ffn_sizes[0] :].reshape(FF, D)
    inputs = tokens.astype(jnp.float32)
    normed_attn, inverse_attn = norm_forward(inputs, gain_attn)
    normed_attn = normed_attn.astype(jnp.bfloat16)
    cos_table, sin_table = rope_angles(positions)
    query_rot, keyval_rot = project_heads(normed_attn, query_mat, keyval_mat, cos_table, sin_table)
    near_keys = passed_along(keyval_rot, "dev", 1)
    window = jnp.concatenate([near_keys, keyval_rot], axis=0)
    allowed = window_mask(positions, row_count)
    attended, totals = attend_forward(query_rot, window, allowed)
    residual = inputs + jnp.dot(attended, out_mat, preferred_element_type=jnp.float32)
    normed_ffn, inverse_ffn = norm_forward(residual, gain_ffn)
    normed_ffn = normed_ffn.astype(jnp.bfloat16)
    gate_up = jnp.dot(normed_ffn, gate_up_mat, preferred_element_type=jnp.float32)
    gate_part = gate_up[:, :FF]
    up_part = gate_up[:, FF:]
    activated = (jax.nn.silu(gate_part) * up_part).astype(jnp.bfloat16)
    mixed = (residual + jnp.dot(activated, down_mat, preferred_element_type=jnp.float32)).astype(
        jnp.bfloat16
    )
    grad_act = jnp.dot(cotangent, down_mat.T, preferred_element_type=jnp.float32)
    sigmoid_gate = jax.nn.sigmoid(gate_part)
    grad_gate_up_act = jnp.concatenate(
        [
            grad_act * up_part * sigmoid_gate * (1.0 + gate_part * (1.0 - sigmoid_gate)),
            grad_act * jax.nn.silu(gate_part),
        ],
        axis=1,
    ).astype(jnp.bfloat16)
    grad_down = jnp.dot(activated.T, cotangent, preferred_element_type=jnp.float32)
    grad_gate_up = jnp.dot(normed_ffn.T, grad_gate_up_act, preferred_element_type=jnp.float32)
    grad_normed_ffn = jnp.dot(grad_gate_up_act, gate_up_mat.T, preferred_element_type=jnp.float32)
    grad_norm_ffn, grad_gain_ffn = norm_backward(grad_normed_ffn, residual, inverse_ffn, gain_ffn)
    grad_residual = cotangent.astype(jnp.float32) + grad_norm_ffn
    grad_residual_b = grad_residual.astype(jnp.bfloat16)
    grad_out = jnp.dot(attended.T, grad_residual_b, preferred_element_type=jnp.float32)
    grad_attended = jnp.dot(grad_residual_b, out_mat.T, preferred_element_type=jnp.float32).astype(
        jnp.bfloat16
    )
    grad_query_rot, grad_window = attend_backward(
        query_rot, window, allowed, attended, grad_attended, totals
    )
    back_near = passed_along(grad_window[:row_count].astype(jnp.bfloat16), "dev", -1).astype(jnp.float32)
    grad_keyval_rot = grad_window[row_count:] + back_near
    key_part = rotate(
        grad_keyval_rot[:, : KVH * HD].reshape(row_count, KVH, HD), cos_table, -sin_table
    ).reshape(row_count, KVH * HD)
    grad_keyval_act = jnp.concatenate([key_part, grad_keyval_rot[:, KVH * HD :]], axis=1).astype(
        jnp.bfloat16
    )
    grad_query_act = (
        rotate(grad_query_rot, cos_table, -sin_table)
        .reshape(row_count, H * HD)
        .astype(jnp.bfloat16)
    )
    grad_query = jnp.dot(normed_attn.T, grad_query_act, preferred_element_type=jnp.float32)
    grad_keyval = jnp.dot(normed_attn.T, grad_keyval_act, preferred_element_type=jnp.float32)
    grad_normed_attn = jnp.dot(
        grad_query_act, query_mat.T, preferred_element_type=jnp.float32
    ) + jnp.dot(grad_keyval_act, keyval_mat.T, preferred_element_type=jnp.float32)
    grad_input, grad_gain_attn = norm_backward(grad_normed_attn, inputs, inverse_attn, gain_attn)
    token_grads = grad_residual + grad_input
    ffn_parts = jnp.concatenate(
        [
            grad_gate_up.reshape(count, -1).astype(jnp.bfloat16),
            grad_down.reshape(count, -1).astype(jnp.bfloat16),
            grad_out.reshape(count, -1).astype(jnp.bfloat16),
        ],
        axis=1,
    )
    ffn_parts = jnp.pad(ffn_parts, ((0, 0), (0, -ffn_parts.shape[1] % 128)))
    ffn_share = scatter_sum(ffn_parts.reshape(count, -1, 128), 4).reshape(-1)
    share_gate_up = ffn_share[: ffn_sizes[0]]
    share_down = ffn_share[ffn_sizes[0] : ffn_sizes[0] + ffn_sizes[1]]
    share_out = ffn_share[ffn_sizes[0] + ffn_sizes[1] : sum(ffn_sizes) + attn_sizes[2]]
    attn_parts = jnp.concatenate(
        [
            grad_query.reshape(count, -1).astype(jnp.bfloat16),
            grad_keyval.reshape(count, -1).astype(jnp.bfloat16),
        ],
        axis=1,
    )
    attn_rows = attn_parts.shape[1]
    attn_parts = jnp.pad(attn_parts, ((0, 0), (0, -attn_rows % 128)))
    attn_share = scatter_sum(attn_parts.reshape(count, -1, 128), 2).reshape(-1)
    share_query = attn_share[: attn_sizes[0]]
    share_keyval = attn_share[attn_sizes[0] : attn_sizes[0] + attn_sizes[1]]
    gain_sums = sum_all(jnp.stack([grad_gain_attn, grad_gain_ffn]))
    gain_attn_sum = gain_sums[0]
    gain_ffn_sum = gain_sums[1]
    return (
        mixed,
        token_grads,
        gain_attn_sum,
        share_query,
        share_keyval,
        share_out,
        gain_ffn_sum,
        share_gate_up,
        share_down,
    )


PAD = 24
CHUNK = 128
bf16 = jnp.bfloat16
f32 = jnp.float32


def dot_nn(a, b):
    return lax.dot_general(a, b, (((1,), (0,)), ((), ())), preferred_element_type=f32)


def dot_nt(a, b):
    return lax.dot_general(a, b, (((1,), (1,)), ((), ())), preferred_element_type=f32)


def split_two(value):
    high = value.astype(bf16)
    return high, (value - high.astype(f32)).astype(bf16)


def spread_wide(source_row):
    rows = lax.broadcasted_iota(jnp.int32, (D, source_row.shape[1]), 0)
    return jnp.where(rows == source_row, 1.0, 0.0).astype(bf16)


def spread_tall(source_col):
    lanes = lax.broadcasted_iota(jnp.int32, (source_col.shape[0], D), 1)
    return jnp.where(lanes == source_col, 1.0, 0.0).astype(bf16)


def turn(a, b, cos_table, sin_table):
    return a * cos_table - b * sin_table, b * cos_table + a * sin_table


def project_kernel(tok, gain, cos, sin, src_a, src_b, wa0, wa1, wb0, wb1, q_out, kv_out):
    x = tok[...].astype(f32)
    inverse = lax.rsqrt(jnp.mean(x * x, axis=0, keepdims=True) + norm_epsilon)
    normed = (x * inverse * gain[...]).astype(bf16).T
    cos_table, sin_table = cos[...], sin[...]
    wa = jnp.concatenate([wa0[...], wa1[...]], axis=0)
    wb = jnp.concatenate([wb0[...], wb1[...]], axis=0)
    wide_a = dot_nn(normed, spread_wide(src_a[...])).astype(bf16)
    wide_b = dot_nn(normed, spread_wide(src_b[...])).astype(bf16)
    qk = dot_nn(wide_a, wa).T
    v = dot_nn(wide_b, wb).T[H * HD :]
    half = HD // 2
    for h in range(H + KVH):
        a = qk[h * HD : h * HD + half]
        b = qk[h * HD + half : (h + 1) * HD]
        ra, rb = turn(a, b, cos_table, sin_table)
        out, row = (q_out, h * HD) if h < H else (kv_out, (h - H) * HD)
        out[row : row + half, :] = ra.astype(bf16)
        out[row + half : row + HD, :] = rb.astype(bf16)
    kv_out[KVH * HD :, :] = v.astype(bf16)


def attend_kernel(q, near, own, pos, prob_out, att_out):
    tokens = q.shape[1]
    group = H // KVH
    scale = 1.0 / math.sqrt(HD)
    span = tokens + CHUNK
    rows = lax.broadcasted_iota(jnp.int32, (span, CHUNK), 0)
    lanes = lax.broadcasted_iota(jnp.int32, (span, CHUNK), 1) + tokens
    for g in range(KVH):
        kw = jnp.concatenate(
            [near[g * HD : (g + 1) * HD, :], own[g * HD : (g + 1) * HD, :]], axis=1
        ).T
        low = (KVH + g) * HD
        vw = jnp.concatenate([near[low : low + HD, :], own[low : low + HD, :]], axis=1)
        for c in range(tokens // CHUNK):
            base = c * CHUNK
            position = pos[:, base : base + CHUNK]
            allowed = (rows <= lanes) & (rows >= lanes - position)
            for i in range(group):
                h = g * group + i
                qh = q[h * HD : (h + 1) * HD, base : base + CHUNK]
                scores = dot_nn(kw[base : base + span], qh) * scale
                scores = jnp.where(allowed, scores, -1e30)
                highest = jnp.max(scores, axis=0, keepdims=True)
                e = jnp.exp(scores - highest)
                total = jnp.sum(e, axis=0, keepdims=True)
                p = (e * (1.0 / total)).astype(bf16)
                prob_out[g, c, :, i * CHUNK : (i + 1) * CHUNK] = p
                att_out[h * HD : (h + 1) * HD, base : base + CHUNK] = dot_nn(
                    vw[:, base : base + span], p
                ).astype(bf16)


def attend_back_kernel(
    q, near, own, prob, att, grad_att, cos, sin, dq_out, dnear_out, down_out, dk, dv
):
    tokens = q.shape[1]
    group = H // KVH
    scale = 1.0 / math.sqrt(HD)
    span = tokens + CHUNK
    half = HD // 2
    for g in range(KVH):
        low = (KVH + g) * HD
        kw = jnp.concatenate(
            [near[g * HD : (g + 1) * HD, :], own[g * HD : (g + 1) * HD, :]], axis=1
        )
        vw = jnp.concatenate([near[low : low + HD, :], own[low : low + HD, :]], axis=1).T
        dk[...] = jnp.zeros_like(dk)
        dv[...] = jnp.zeros_like(dv)
        for c in range(tokens // CHUNK):
            base = c * CHUNK
            cut = slice(base, base + CHUNK)
            heads = [g * group + i for i in range(group)]
            q_all = jnp.concatenate([q[h * HD : (h + 1) * HD, cut] for h in heads], axis=1)
            g_all = jnp.concatenate([grad_att[h * HD : (h + 1) * HD, cut] for h in heads], axis=1)
            a_all = jnp.concatenate([att[h * HD : (h + 1) * HD, cut] for h in heads], axis=1)
            delta = jnp.sum(g_all.astype(f32) * a_all.astype(f32), axis=0, keepdims=True)
            p = prob[g, c]
            grad_prob = dot_nn(vw[base : base + span], g_all)
            ds = (p.astype(f32) * (grad_prob - delta) * scale).astype(bf16)
            dq = dot_nn(kw[:, base : base + span], ds)
            dk[:, base : base + span] += dot_nt(q_all, ds)
            dv[:, base : base + span] += dot_nt(g_all, p)
            for i, h in enumerate(heads):
                part = dq[:, i * CHUNK : (i + 1) * CHUNK]
                ra, rb = turn(part[:half], part[half:], cos[:, cut], -sin[:, cut])
                dq_out[h * HD : h * HD + half, cut] = ra.astype(bf16)
                dq_out[h * HD + half : (h + 1) * HD, cut] = rb.astype(bf16)
        dnear_out[g * HD : (g + 1) * HD, :] = dk[:, :tokens].astype(bf16)
        dnear_out[low : low + HD, :] = dv[:, :tokens].astype(bf16)
        down_out[g * HD : (g + 1) * HD, :] = dk[:, tokens:]
        down_out[low : low + HD, :] = dv[:, tokens:]


def feed_kernel(
    slots,
    att,
    tok,
    cot,
    gain,
    src_b,
    src_g,
    src_u,
    wb0,
    wb1,
    wg0,
    wg1,
    wu0,
    wu1,
    wd0,
    wd1,
    mixed_out,
    res_out,
    dgate,
    dup,
    dg_out,
    du_out,
    dd_out,
    wd,
    act,
    wide_g,
    wide_u,
):
    count = slots.shape[0]
    rows_d = FF // count
    for p in range(count):
        half, at = (wd0, p) if p < count // 2 else (wd1, p - count // 2)
        target = pl.multiple_of(slots[p] * rows_d, rows_d)
        wd[pl.ds(target, rows_d), :] = half[at * rows_d : (at + 1) * rows_d, :]
    wb = jnp.concatenate([wb0[...], wb1[...]], axis=0)
    cot_tok = cot[...].T
    att_wide = dot_nn(att[...].T, spread_wide(src_b[...])).astype(bf16)
    residual = tok[...].astype(f32).T + dot_nn(att_wide, wb)[:, :D]
    res_out[...] = residual
    inverse = lax.rsqrt(jnp.mean(residual * residual, axis=-1, keepdims=True) + norm_epsilon)
    normed = (residual * inverse * gain[...]).astype(bf16)
    wide_g[...] = dot_nn(normed, spread_wide(src_g[...])).astype(bf16)
    wide_u[...] = dot_nn(normed, spread_wide(src_u[...])).astype(bf16)
    block = 256

    def ff_step(j, carry):
        cut = pl.ds(pl.multiple_of(j * block, block), block)
        gate = dot_nn(wide_g[...], jnp.concatenate([wg0[:, cut], wg1[:, cut]], axis=0))
        up = dot_nn(wide_u[...], jnp.concatenate([wu0[:, cut], wu1[:, cut]], axis=0))
        grad_act = dot_nt(cot_tok, wd[cut, :])
        sig = jax.nn.sigmoid(gate)
        silu = gate * sig
        act[:, cut] = (silu * up).astype(bf16)
        dgate[:, cut] = (grad_act * up * sig * (1.0 + gate * (1.0 - sig))).astype(bf16)
        dup[:, cut] = (grad_act * silu).astype(bf16)
        return carry

    lax.fori_loop(0, FF // block, ff_step, 0)
    mixed = residual + dot_nn(act[...], wd[...])
    mixed_out[...] = mixed.T.astype(bf16)
    dg_out[...] = dot_nn(wide_g[...].T, dgate[...]).astype(bf16)
    du_out[...] = dot_nn(wide_u[...].T, dup[...]).astype(bf16)
    wd[...] = dot_nn(act[...].T, cot_tok).astype(bf16)
    for p in range(count):
        source = pl.multiple_of(slots[p] * rows_d, rows_d)
        dd_out[p * rows_d : (p + 1) * rows_d, :] = wd[pl.ds(source, rows_d), :]


def feed_back_kernel(
    residual_in,
    cot,
    gain,
    src_b,
    src_g,
    src_u,
    dgate,
    dup,
    wb0,
    wb1,
    wg0,
    wg1,
    wu0,
    wu1,
    gres_out,
    gatt_out,
    dgain_out,
):
    residual = residual_in[...]
    spread_b = spread_wide(src_b[...])
    spread_g = spread_wide(src_g[...])
    spread_u = spread_wide(src_u[...])
    inverse = lax.rsqrt(jnp.mean(residual * residual, axis=-1, keepdims=True) + norm_epsilon)
    dn_g = dot_nt(dgate[...], jnp.concatenate([wg0[...], wg1[...]], axis=0))
    dn_u = dot_nt(dup[...], jnp.concatenate([wu0[...], wu1[...]], axis=0))
    grad_normed = sum(dot_nt(part, spread_g) for part in split_two(dn_g)) + sum(
        dot_nt(part, spread_u) for part in split_two(dn_u)
    )
    unit = residual * inverse
    scaled = grad_normed * gain[...]
    dgain_out[...] = jnp.sum(grad_normed * unit, axis=0, keepdims=True)
    grad_res = cot[...].T.astype(f32) + inverse * (
        scaled - unit * jnp.mean(scaled * unit, axis=-1, keepdims=True)
    )
    gres_out[...] = grad_res.T
    wb = jnp.concatenate([wb0[:, :D], wb1[:, :D]], axis=0)
    gatt_wide = dot_nt(wb, grad_res.astype(bf16)).astype(bf16)
    gatt_out[...] = dot_nn(spread_b, gatt_wide).astype(bf16)


def finish_kernel(
    dq,
    own,
    back,
    tok,
    gain,
    cos,
    sin,
    gres,
    att,
    dgain_ffn,
    src_a,
    src_b,
    tall_a,
    tall_b,
    wa0,
    wa1,
    wb0,
    wb1,
    dtok_out,
    da_out,
    db_out,
):
    x = tok[...].astype(f32)
    inverse = lax.rsqrt(jnp.mean(x * x, axis=0, keepdims=True) + norm_epsilon)
    unit = x * inverse
    normed = (unit * gain[...]).astype(bf16)
    total = own[...] + back[...].astype(f32)
    half = HD // 2
    parts = [dq[...]]
    for g in range(KVH):
        ra, rb = turn(
            total[g * HD : g * HD + half],
            total[g * HD + half : (g + 1) * HD],
            cos[...],
            -sin[...],
        )
        parts += [ra.astype(bf16), rb.astype(bf16)]
    dqk = jnp.concatenate(parts, axis=0)
    dv = total[KVH * HD :].astype(bf16)
    wa = jnp.concatenate([wa0[...], wa1[...]], axis=0)
    wb = jnp.concatenate([wb0[...], wb1[...]], axis=0)
    dvx = jnp.concatenate([jnp.zeros((H * HD, dv.shape[1]), bf16), dv], axis=0)
    dn_a = dot_nn(wa, dqk)
    dn_b = dot_nn(wb, dvx)
    spread_a = spread_wide(src_a[...])
    spread_b = spread_wide(src_b[...])
    grad_normed = sum(dot_nn(spread_a, part) for part in split_two(dn_a)) + sum(
        dot_nn(spread_b, part) for part in split_two(dn_b)
    )
    scaled = grad_normed * gain[...]
    dtok_out[...] = gres[...] + inverse * (
        scaled - unit * jnp.mean(scaled * unit, axis=0, keepdims=True)
    )
    dgain = jnp.sum(grad_normed * unit, axis=1, keepdims=True)
    dgain = jnp.broadcast_to(dgain, (D, CHUNK)).T[:1]
    tall_spread_b = spread_tall(tall_b[...])
    wide_a = dot_nn(spread_tall(tall_a[...]), normed).astype(bf16)
    wide_b = dot_nn(tall_spread_b, normed).astype(bf16)
    wide_att = dot_nn(tall_spread_b, att[...]).astype(bf16)
    extra_a = tall_a[...] < 0
    extra_b = tall_b[...] < 0
    fill_a = jnp.concatenate([dgain, jnp.zeros((1, KVH * HD), f32)], axis=1)
    da_out[...] = jnp.where(extra_a, fill_a, dot_nt(wide_a, dqk)).astype(bf16)
    d_out = dot_nt(wide_att, gres[...].astype(bf16))
    db_out[:, :D] = jnp.where(extra_b, dgain_ffn[...], d_out).astype(bf16)
    db_out[:, D:] = dot_nt(wide_b, dv).astype(bf16)


def call_whole(kernel, outs, operands, scratch=(), scalars=()):
    vmem = pl.BlockSpec(memory_space=pltpu.VMEM)
    smem = pl.BlockSpec(memory_space=pltpu.SMEM)
    return pl.pallas_call(
        kernel,
        out_shape=[jax.ShapeDtypeStruct(s, d) for s, d in outs],
        in_specs=[smem] * len(scalars) + [vmem] * len(operands),
        out_specs=[vmem] * len(outs),
        scratch_shapes=list(scratch),
        compiler_params=pltpu.CompilerParams(vmem_limit_bytes=60 * 1024 * 1024),
    )(*scalars, *operands)


def step_double(held, orders, t):
    got = []
    for h, order in zip(held, orders):
        got.append(swapped(h, order[t]))
    return got


def joined(held, got):
    return [jnp.concatenate([h, g], axis=0) for h, g in zip(held, got)]


def step_halve(held, orders, t, even=False):
    halves = [h.shape[0] // 2 for h in held]
    out = []
    for h, k, order in zip(held, halves, orders):
        g = swapped(h[k:].astype(bf16), order[-1 - t])
        kept = h[:k].astype(f32)
        if even:
            kept = lax.reduce_precision(kept, 8, 7)
        out.append(kept + g.astype(f32))
    return out


def sources(order, per_slot):
    me = lax.axis_index("dev")
    owner = me ^ jnp.asarray(slot_masks(order), jnp.int32)
    inner = jnp.arange(PAD, dtype=jnp.int32)[None, :]
    value = jnp.where(inner < per_slot, owner[:, None] * per_slot + inner, -1)
    return value.reshape(-1)


def padded_rows(value):
    return jnp.pad(value, ((0, PAD - value.shape[0]), (0, 0)))


def shards(
    tokens, positions, gain_attn, w_query, w_kv, w_out, gain_ffn, w_gate_up, w_down, cotangent
):
    count = lax.axis_size("dev")
    me = lax.axis_index("dev")
    row_count = tokens.shape[0]
    per = D // count
    per_d = FF // count
    first, rest = link_masks(count)
    order_of = [rest[k:] + rest[:k] + [first] for k in range(len(rest))]
    ord_a, ord_b = order_of[0], order_of[2]
    ord_g, ord_u, ord_d = order_of[1], order_of[2], order_of[3]
    src_a, src_b = sources(ord_a, per), sources(ord_b, per)
    src_g, src_u = sources(ord_g, per), sources(ord_u, per)
    slots = me ^ jnp.asarray(slot_masks(ord_d), jnp.int32)
    w_qs, w_kvs = w_query.reshape(per, H * HD), w_kv.reshape(per, 2 * KVH * HD)
    kv_cut = KVH * HD
    stream_a = padded_rows(jnp.concatenate([w_qs, w_kvs[:, :kv_cut]], axis=1))
    stream_b = padded_rows(jnp.concatenate([w_out.reshape(per, D), w_kvs[:, kv_cut:]], axis=1))
    half_dim = HD // 2
    frequency = jnp.exp(jnp.arange(half_dim, dtype=f32) * (-2.0 * math.log(theta_base) / HD))
    angles = frequency[:, None] * positions.astype(f32)[None, :]
    cos, sin = jnp.cos(angles), jnp.sin(angles)
    tok_t, cot_t = tokens.T, cotangent.T
    gain_col = gain_attn.reshape(D, 1)
    orders_ab, orders_gud = [ord_a, ord_b], [ord_g, ord_u, ord_d]
    steps = len(ord_a)
    hold = lax.optimization_barrier
    held = [stream_a, stream_b]
    ffn = None
    early = (src_a[None], src_b[None], src_a[:, None], src_b[:, None])
    early = early + (src_g[None], src_u[None], slots, cos, sin, gain_col)
    for t in range(steps):
        if t == 2:
            held, w_gate_up, w_down = hold((held, w_gate_up, w_down))
            w_gs = w_gate_up.reshape(per, 2 * FF)
            ffn = [padded_rows(w_gs[:, :FF]), padded_rows(w_gs[:, FF:]), w_down.reshape(per_d, D)]
        if t == 3:
            held, early = hold((held, early))
        got = step_double(held, orders_ab, t)
        if t < steps - 1:
            held = joined(held, got)
        if t >= 2:
            ffn = joined(ffn, step_double(ffn, orders_gud, t - 2))
        if t == 3:
            held, ffn = hold((held, ffn))
    (wa0, wb0), (wa1, wb1) = held, got
    row_a, row_b, tall_a, tall_b, row_g, row_u, slots, cos, sin, gain_col = early
    q_t, kv_t = call_whole(
        project_kernel,
        [((H * HD, row_count), bf16), ((2 * kv_cut, row_count), bf16)],
        [tok_t, gain_col, cos, sin, row_a, row_b, wa0, wa1, wb0, wb1],
    )
    for t in range(steps - 2, steps):
        got = step_double(ffn, orders_gud, t)
        if t < steps - 1:
            ffn = joined(ffn, got)
    (wg0, wu0, wd0), (wg1, wu1, wd1) = ffn, got
    near = passed_along(kv_t, "dev", 1)
    chunks = row_count // CHUNK
    prob, att_t = call_whole(
        attend_kernel,
        [
            ((KVH, chunks, row_count + CHUNK, H // KVH * CHUNK), bf16),
            ((H * HD, row_count), bf16),
        ],
        [q_t, near, kv_t, positions[None]],
    )
    wide = count * PAD
    mixed_t, residual, dgate, dup, dg, du, dd = call_whole(
        feed_kernel,
        [
            ((D, row_count), bf16),
            ((row_count, D), f32),
            ((row_count, FF), bf16),
            ((row_count, FF), bf16),
            ((wide, FF), bf16),
            ((wide, FF), bf16),
            ((FF, D), bf16),
        ],
        [att_t, tok_t, cot_t, gain_ffn[None], row_b, row_g, row_u]
        + [wb0, wb1, wg0, wg1, wu0, wu1, wd0, wd1],
        scratch=[
            pltpu.VMEM((FF, D), bf16),
            pltpu.VMEM((row_count, FF), bf16),
            pltpu.VMEM((row_count, wide), bf16),
            pltpu.VMEM((row_count, wide), bf16),
        ],
        scalars=[slots],
    )
    sums = [dg, du, dd]
    gres_t, gatt_t, dgain_ffn = call_whole(
        feed_back_kernel,
        [((D, row_count), f32), ((H * HD, row_count), bf16), ((1, D), f32)],
        [residual, cot_t, gain_ffn[None], row_b, row_g, row_u, dgate, dup]
        + [wb0, wb1, wg0, wg1, wu0, wu1],
    )
    for t in range(3):
        sums = step_halve(sums, orders_gud, t)
    dq_t, dnear, down = call_whole(
        attend_back_kernel,
        [
            ((H * HD, row_count), bf16),
            ((2 * kv_cut, row_count), bf16),
            ((2 * kv_cut, row_count), f32),
        ],
        [q_t, near, kv_t, prob, att_t, gatt_t, cos, sin],
        scratch=[pltpu.VMEM((HD, 2 * row_count), f32)] * 2,
    )
    back = passed_along(dnear, "dev", -1)
    dtok_t, da, db = call_whole(
        finish_kernel,
        [
            ((D, row_count), f32),
            ((wide, H * HD + kv_cut), bf16),
            ((wide, D + kv_cut), bf16),
        ],
        [dq_t, down, back, tok_t, gain_col, cos, sin, gres_t, att_t, dgain_ffn]
        + [row_a, row_b, tall_a, tall_b, wa0, wa1, wb0, wb1],
    )
    last = [da, db]
    for t in range(steps):
        last = step_halve(last, orders_ab, t, even=True)
        if t + 3 < steps:
            sums = step_halve(sums, orders_gud, t + 3)
    share_g, share_u, share_d = sums
    share_a, share_b = last
    share_kv = jnp.concatenate([share_a[:per, H * HD :], share_b[:per, D:]], axis=1)
    share_gu = jnp.concatenate([share_g[:per], share_u[:per]], axis=1)
    return (
        mixed_t.T,
        dtok_t.T,
        share_a[per, :D],
        share_a[:per, : H * HD].reshape(-1),
        share_kv.reshape(-1),
        share_b[:per, :D].reshape(-1),
        share_b[per, :D],
        share_gu.reshape(-1),
        share_d.reshape(-1),
    )


def fits_whole_rows(count):
    per = D // count
    return D % count == 0 and FF % count == 0 and (FF // count) % 16 == 0 and 16 <= per <= PAD


def solution(mesh):
    in_specs = (
        P("dev", None),
        P("dev"),
        P(),
        P("dev"),
        P("dev"),
        P("dev"),
        P(),
        P("dev"),
        P("dev"),
        P("dev", None),
    )
    out_specs = (
        P("dev", None),
        P("dev", None),
        P(),
        P("dev"),
        P("dev"),
        P("dev"),
        P(),
        P("dev"),
        P("dev"),
    )
    whole_rows = fits_whole_rows(mesh.shape["dev"])

    def layer(*args):
        return shards(*args)

    return jax.shard_map(
        layer if whole_rows else shards_general,
        mesh=mesh,
        in_specs=in_specs,
        out_specs=out_specs,
        check_vma=False,
    )
```

```python
import functools
import math

import jax
import jax.numpy as jnp
from jax import lax
from jax.experimental import pallas as pl
from jax.experimental.pallas import tpu as pltpu
from jax.sharding import PartitionSpec as P


D = 576
H = 9
KVH = 3
HD = 64
FF = 1536


norm_epsilon = 1e-05
theta_base = 100000.0


def passed_along(value, axis, steps):
    count = lax.axis_size(axis)
    first, last = (max(0, -steps), min(count, count - steps))
    return lax.ppermute(value, axis, [(source, source + steps) for source in range(first, last)])


def link_masks(count):
    bits = [1 << b for b in range(count.bit_length() - 1)]
    if count == 32:
        bits = [1, 2, 4, 8, 24]
    return bits[0], bits[1:]


def swapped(value, mask):
    count = lax.axis_size("dev")
    return lax.ppermute(value, "dev", [(i, i ^ mask) for i in range(count)])


def color_orders(count, colors):
    first, rest = link_masks(count)
    if colors == 1:
        return [rest + [first]]
    step = len(rest) // colors
    return [rest[c * step :] + rest[: c * step] + [first] for c in range(colors)]


def slot_masks(order):
    slots = [0]
    for mask in order:
        slots = slots + [s ^ mask for s in slots]
    return slots


def cut_rows(rows, colors):
    edges = [rows * c // colors for c in range(colors + 1)]
    return list(zip(edges[:-1], edges[1:]))


def gather_all(block, colors):
    count = lax.axis_size("dev")
    me = lax.axis_index("dev")
    orders = color_orders(count, colors)
    held = [block[a:b][None] for a, b in cut_rows(block.shape[0], colors)]
    for t in range(len(orders[0])):
        got = [swapped(h, order[t]) for h, order in zip(held, orders)]
        held = [jnp.concatenate([h, g], axis=0) for h, g in zip(held, got)]
    whole = []
    for h, order in zip(held, orders):
        slots = slot_masks(order)
        where = [0] * count
        for place, mask in enumerate(slots):
            where[mask] = place
        index = jnp.asarray(where, jnp.int32)[me ^ jnp.arange(count, dtype=jnp.int32)]
        whole.append(jnp.take(h, index, axis=0, mode="clip"))
    return jnp.concatenate(whole, axis=1)


def scatter_sum(parts, colors):
    count = lax.axis_size("dev")
    me = lax.axis_index("dev")
    orders = color_orders(count, colors)
    held = []
    for (a, b), order in zip(cut_rows(parts.shape[1], colors), orders):
        slots = jnp.asarray(slot_masks(order), jnp.int32)
        held.append(jnp.take(parts[:, a:b], me ^ slots, axis=0, mode="clip"))
    for t in range(len(orders[0])):
        half = held[0].shape[0] // 2
        masks = [order[-1 - t] for order in orders]
        got = [swapped(h[half:].astype(jnp.bfloat16), m) for h, m in zip(held, masks)]
        held = [h[:half].astype(jnp.float32) + g.astype(jnp.float32) for h, g in zip(held, got)]
    return jnp.concatenate([h[0] for h in held], axis=0)


def sum_all(value):
    first, rest = link_masks(lax.axis_size("dev"))
    for mask in [first] + rest:
        value = value + swapped(value, mask)
    return value


def norm_forward(values, scale_gain):
    inverse = lax.rsqrt(jnp.mean(values * values, axis=-1, keepdims=True) + norm_epsilon)
    return (values * inverse * scale_gain, inverse)


def norm_backward(grad_output, values, inverse, scale_gain):
    unit_rows = values * inverse
    scaled = grad_output * scale_gain
    grad_gain = jnp.sum(grad_output * unit_rows, axis=0)
    grad_input = inverse * (
        scaled - unit_rows * jnp.mean(scaled * unit_rows, axis=-1, keepdims=True)
    )
    return (grad_input, grad_gain)


def rope_angles(position_block):
    half_dim = HD // 2
    frequency = jnp.exp(
        jnp.arange(half_dim, dtype=jnp.float32) * (-2.0 * math.log(theta_base) / HD)
    )
    angles = position_block.astype(jnp.float32)[:, None] * frequency[None, :]
    return (jnp.cos(angles)[:, None, :], jnp.sin(angles)[:, None, :])


def rotate(values, cos_table, sin_table):
    half_dim = values.shape[-1] // 2
    first_half = values[..., :half_dim]
    second_half = values[..., half_dim:]
    return jnp.concatenate(
        [
            first_half * cos_table - second_half * sin_table,
            second_half * cos_table + first_half * sin_table,
        ],
        axis=-1,
    )


def project_heads(normed, query_mat, keyval_mat, cos_table, sin_table):
    row_count = normed.shape[0]
    queries = jnp.dot(normed, query_mat, preferred_element_type=jnp.float32).reshape(
        row_count, H, HD
    )
    keyvals = jnp.dot(normed, keyval_mat, preferred_element_type=jnp.float32)
    keys_rot = rotate(
        keyvals[:, : KVH * HD].reshape(row_count, KVH, HD), cos_table, sin_table
    ).reshape(row_count, KVH * HD)
    query_rot = (
        rotate(queries, cos_table, sin_table).reshape(row_count, H * HD).astype(jnp.bfloat16)
    )
    keyval_rot = jnp.concatenate([keys_rot, keyvals[:, KVH * HD :]], axis=1).astype(jnp.bfloat16)
    return (query_rot, keyval_rot)


def window_mask(position_block, row_count):
    query_at = jnp.arange(row_count, dtype=jnp.int32)[:, None] + row_count
    key_at = jnp.arange(2 * row_count, dtype=jnp.int32)[None, :]
    return (key_at <= query_at) & (key_at >= query_at - position_block[:, None])


def masked_scores(query_group, key_group, allowed):
    scale_factor = 1.0 / math.sqrt(HD)
    scores = (
        jnp.einsum("tqd,wd->qtw", query_group, key_group, preferred_element_type=jnp.float32)
        * scale_factor
    )
    return jnp.where(allowed[None], scores, -1e30)


def attend_forward(query_rot, window, allowed):
    row_count = query_rot.shape[0]
    grouped = H // KVH
    queries = query_rot.reshape(row_count, H, HD)
    outputs = []
    totals = []
    for group_index in range(KVH):
        query_group = queries[:, group_index * grouped : (group_index + 1) * grouped]
        key_group = window[:, group_index * HD : (group_index + 1) * HD]
        value_group = window[:, (KVH + group_index) * HD : (KVH + group_index + 1) * HD]
        scores = masked_scores(query_group, key_group, allowed)
        highest = jnp.max(scores, axis=-1, keepdims=True)
        log_total = highest + jnp.log(jnp.sum(jnp.exp(scores - highest), axis=-1, keepdims=True))
        probability = jnp.exp(scores - log_total).astype(jnp.bfloat16)
        head_out = jnp.einsum(
            "qtw,wd->tqd", probability, value_group, preferred_element_type=jnp.float32
        )
        outputs.append(head_out.astype(jnp.bfloat16))
        totals.append(log_total)
    return (jnp.concatenate(outputs, axis=1).reshape(row_count, H * HD), totals)


def attend_backward(query_rot, window, allowed, attended, grad_attended, totals):
    row_count = query_rot.shape[0]
    grouped = H // KVH
    scale_factor = 1.0 / math.sqrt(HD)
    queries = query_rot.reshape(row_count, H, HD)
    attended_heads = attended.reshape(row_count, H, HD)
    grad_heads = grad_attended.reshape(row_count, H, HD)
    query_grads = []
    key_grads = []
    value_grads = []
    for group_index in range(KVH):
        head_slice = slice(group_index * grouped, (group_index + 1) * grouped)
        query_group = queries[:, head_slice]
        key_group = window[:, group_index * HD : (group_index + 1) * HD]
        value_group = window[:, (KVH + group_index) * HD : (KVH + group_index + 1) * HD]
        scores = masked_scores(query_group, key_group, allowed)
        probability = jnp.exp(scores - totals[group_index])
        grad_group = grad_heads[:, head_slice]
        row_delta = jnp.sum(
            grad_group.astype(jnp.float32) * attended_heads[:, head_slice].astype(jnp.float32),
            axis=-1,
        )
        grad_prob = jnp.einsum(
            "tqd,wd->qtw", grad_group, value_group, preferred_element_type=jnp.float32
        )
        grad_scores = (probability * (grad_prob - row_delta.T[:, :, None]) * scale_factor).astype(
            jnp.bfloat16
        )
        query_grads.append(
            jnp.einsum("qtw,wd->tqd", grad_scores, key_group, preferred_element_type=jnp.float32)
        )
        key_grads.append(
            jnp.einsum("qtw,tqd->wd", grad_scores, query_group, preferred_element_type=jnp.float32)
        )
        value_grads.append(
            jnp.einsum(
                "qtw,tqd->wd",
                probability.astype(jnp.bfloat16),
                grad_group,
                preferred_element_type=jnp.float32,
            )
        )
    return (jnp.concatenate(query_grads, axis=1), jnp.concatenate(key_grads + value_grads, axis=1))


def shards_general(
    tokens, positions, gain_attn, w_query, w_kv, w_out, gain_ffn, w_gate_up, w_down, cotangent
):
    row_count = tokens.shape[0]
    width_kv = 2 * KVH * HD
    count = lax.axis_size("dev")
    attn_sizes = [w_query.shape[0], w_kv.shape[0], w_out.shape[0]]
    ffn_sizes = [w_gate_up.shape[0], w_down.shape[0]]
    attn_all = gather_all(jnp.concatenate([w_query, w_kv, w_out]).reshape(-1, 128), 2)
    attn_all = attn_all.reshape(count, -1)
    query_mat = attn_all[:, : attn_sizes[0]].reshape(D, H * HD)
    keyval_mat = attn_all[:, attn_sizes[0] : attn_sizes[0] + attn_sizes[1]].reshape(D, width_kv)
    out_mat = attn_all[:, attn_sizes[0] + attn_sizes[1] :].reshape(H * HD, D)
    ffn_all = gather_all(jnp.concatenate([w_gate_up, w_down]).reshape(-1, 128), 4)
    ffn_all = ffn_all.reshape(count, -1)
    gate_up_mat = ffn_all[:, : ffn_sizes[0]].reshape(D, 2 * FF)
    down_mat = ffn_all[:, ffn_sizes[0] :].reshape(FF, D)
    inputs = tokens.astype(jnp.float32)
    normed_attn, inverse_attn = norm_forward(inputs, gain_attn)
    normed_attn = normed_attn.astype(jnp.bfloat16)
    cos_table, sin_table = rope_angles(positions)
    query_rot, keyval_rot = project_heads(normed_attn, query_mat, keyval_mat, cos_table, sin_table)
    near_keys = passed_along(keyval_rot, "dev", 1)
    window = jnp.concatenate([near_keys, keyval_rot], axis=0)
    allowed = window_mask(positions, row_count)
    attended, totals = attend_forward(query_rot, window, allowed)
    residual = inputs + jnp.dot(attended, out_mat, preferred_element_type=jnp.float32)
    normed_ffn, inverse_ffn = norm_forward(residual, gain_ffn)
    normed_ffn = normed_ffn.astype(jnp.bfloat16)
    gate_up = jnp.dot(normed_ffn, gate_up_mat, preferred_element_type=jnp.float32)
    gate_part = gate_up[:, :FF]
    up_part = gate_up[:, FF:]
    activated = (jax.nn.silu(gate_part) * up_part).astype(jnp.bfloat16)
    mixed = (residual + jnp.dot(activated, down_mat, preferred_element_type=jnp.float32)).astype(
        jnp.bfloat16
    )
    grad_act = jnp.dot(cotangent, down_mat.T, preferred_element_type=jnp.float32)
    sigmoid_gate = jax.nn.sigmoid(gate_part)
    grad_gate_up_act = jnp.concatenate(
        [
            grad_act * up_part * sigmoid_gate * (1.0 + gate_part * (1.0 - sigmoid_gate)),
            grad_act * jax.nn.silu(gate_part),
        ],
        axis=1,
    ).astype(jnp.bfloat16)
    grad_down = jnp.dot(activated.T, cotangent, preferred_element_type=jnp.float32)
    grad_gate_up = jnp.dot(normed_ffn.T, grad_gate_up_act, preferred_element_type=jnp.float32)
    grad_normed_ffn = jnp.dot(grad_gate_up_act, gate_up_mat.T, preferred_element_type=jnp.float32)
    grad_norm_ffn, grad_gain_ffn = norm_backward(grad_normed_ffn, residual, inverse_ffn, gain_ffn)
    grad_residual = cotangent.astype(jnp.float32) + grad_norm_ffn
    grad_residual_b = grad_residual.astype(jnp.bfloat16)
    grad_out = jnp.dot(attended.T, grad_residual_b, preferred_element_type=jnp.float32)
    grad_attended = jnp.dot(grad_residual_b, out_mat.T, preferred_element_type=jnp.float32).astype(
        jnp.bfloat16
    )
    grad_query_rot, grad_window = attend_backward(
        query_rot, window, allowed, attended, grad_attended, totals
    )
    back_near = passed_along(grad_window[:row_count].astype(jnp.bfloat16), "dev", -1).astype(jnp.float32)
    grad_keyval_rot = grad_window[row_count:] + back_near
    key_part = rotate(
        grad_keyval_rot[:, : KVH * HD].reshape(row_count, KVH, HD), cos_table, -sin_table
    ).reshape(row_count, KVH * HD)
    grad_keyval_act = jnp.concatenate([key_part, grad_keyval_rot[:, KVH * HD :]], axis=1).astype(
        jnp.bfloat16
    )
    grad_query_act = (
        rotate(grad_query_rot, cos_table, -sin_table)
        .reshape(row_count, H * HD)
        .astype(jnp.bfloat16)
    )
    grad_query = jnp.dot(normed_attn.T, grad_query_act, preferred_element_type=jnp.float32)
    grad_keyval = jnp.dot(normed_attn.T, grad_keyval_act, preferred_element_type=jnp.float32)
    grad_normed_attn = jnp.dot(
        grad_query_act, query_mat.T, preferred_element_type=jnp.float32
    ) + jnp.dot(grad_keyval_act, keyval_mat.T, preferred_element_type=jnp.float32)
    grad_input, grad_gain_attn = norm_backward(grad_normed_attn, inputs, inverse_attn, gain_attn)
    token_grads = grad_residual + grad_input
    ffn_parts = jnp.concatenate(
        [
            grad_gate_up.reshape(count, -1).astype(jnp.bfloat16),
            grad_down.reshape(count, -1).astype(jnp.bfloat16),
            grad_out.reshape(count, -1).astype(jnp.bfloat16),
        ],
        axis=1,
    )
    ffn_parts = jnp.pad(ffn_parts, ((0, 0), (0, -ffn_parts.shape[1] % 128)))
    ffn_share = scatter_sum(ffn_parts.reshape(count, -1, 128), 4).reshape(-1)
    share_gate_up = ffn_share[: ffn_sizes[0]]
    share_down = ffn_share[ffn_sizes[0] : ffn_sizes[0] + ffn_sizes[1]]
    share_out = ffn_share[ffn_sizes[0] + ffn_sizes[1] : sum(ffn_sizes) + attn_sizes[2]]
    attn_parts = jnp.concatenate(
        [
            grad_query.reshape(count, -1).astype(jnp.bfloat16),
            grad_keyval.reshape(count, -1).astype(jnp.bfloat16),
        ],
        axis=1,
    )
    attn_rows = attn_parts.shape[1]
    attn_parts = jnp.pad(attn_parts, ((0, 0), (0, -attn_rows % 128)))
    attn_share = scatter_sum(attn_parts.reshape(count, -1, 128), 2).reshape(-1)
    share_query = attn_share[: attn_sizes[0]]
    share_keyval = attn_share[attn_sizes[0] : attn_sizes[0] + attn_sizes[1]]
    gain_sums = sum_all(jnp.stack([grad_gain_attn, grad_gain_ffn]))
    gain_attn_sum = gain_sums[0]
    gain_ffn_sum = gain_sums[1]
    return (
        mixed,
        token_grads,
        gain_attn_sum,
        share_query,
        share_keyval,
        share_out,
        gain_ffn_sum,
        share_gate_up,
        share_down,
    )


PAD = 24
CHUNK = 128
bf16 = jnp.bfloat16
f32 = jnp.float32


def dot_nn(a, b):
    return lax.dot_general(a, b, (((1,), (0,)), ((), ())), preferred_element_type=f32)


def dot_nt(a, b):
    return lax.dot_general(a, b, (((1,), (1,)), ((), ())), preferred_element_type=f32)


def split_two(value):
    high = value.astype(bf16)
    return high, (value - high.astype(f32)).astype(bf16)


def spread_wide(source_row):
    rows = lax.broadcasted_iota(jnp.int32, (D, source_row.shape[1]), 0)
    return jnp.where(rows == source_row, 1.0, 0.0).astype(bf16)


def spread_tall(source_col):
    lanes = lax.broadcasted_iota(jnp.int32, (source_col.shape[0], D), 1)
    return jnp.where(lanes == source_col, 1.0, 0.0).astype(bf16)


def turn(a, b, cos_table, sin_table):
    return a * cos_table - b * sin_table, b * cos_table + a * sin_table


def project_kernel(tok, gain, cos, sin, src_a, src_b, wa0, wa1, wb0, wb1, q_out, kv_out):
    x = tok[...].astype(f32)
    inverse = lax.rsqrt(jnp.mean(x * x, axis=0, keepdims=True) + norm_epsilon)
    normed = (x * inverse * gain[...]).astype(bf16).T
    cos_table, sin_table = cos[...], sin[...]
    wa = jnp.concatenate([wa0[...], wa1[...]], axis=0)
    wb = jnp.concatenate([wb0[...], wb1[...]], axis=0)
    wide_a = dot_nn(normed, spread_wide(src_a[...])).astype(bf16)
    wide_b = dot_nn(normed, spread_wide(src_b[...])).astype(bf16)
    qk = dot_nn(wide_a, wa).T
    v = dot_nn(wide_b, wb).T[H * HD :]
    half = HD // 2
    for h in range(H + KVH):
        a = qk[h * HD : h * HD + half]
        b = qk[h * HD + half : (h + 1) * HD]
        ra, rb = turn(a, b, cos_table, sin_table)
        out, row = (q_out, h * HD) if h < H else (kv_out, (h - H) * HD)
        out[row : row + half, :] = ra.astype(bf16)
        out[row + half : row + HD, :] = rb.astype(bf16)
    kv_out[KVH * HD :, :] = v.astype(bf16)


def attend_kernel(q, near, own, pos, prob_out, att_out):
    tokens = q.shape[1]
    group = H // KVH
    scale = 1.0 / math.sqrt(HD)
    span = tokens + CHUNK
    rows = lax.broadcasted_iota(jnp.int32, (span, CHUNK), 0)
    lanes = lax.broadcasted_iota(jnp.int32, (span, CHUNK), 1) + tokens
    for g in range(KVH):
        kw = jnp.concatenate(
            [near[g * HD : (g + 1) * HD, :], own[g * HD : (g + 1) * HD, :]], axis=1
        ).T
        low = (KVH + g) * HD
        vw = jnp.concatenate([near[low : low + HD, :], own[low : low + HD, :]], axis=1)
        for c in range(tokens // CHUNK):
            base = c * CHUNK
            position = pos[:, base : base + CHUNK]
            allowed = (rows <= lanes) & (rows >= lanes - position)
            for i in range(group):
                h = g * group + i
                qh = q[h * HD : (h + 1) * HD, base : base + CHUNK]
                scores = dot_nn(kw[base : base + span], qh) * scale
                scores = jnp.where(allowed, scores, -1e30)
                highest = jnp.max(scores, axis=0, keepdims=True)
                e = jnp.exp(scores - highest)
                total = jnp.sum(e, axis=0, keepdims=True)
                p = (e * (1.0 / total)).astype(bf16)
                prob_out[g, c, :, i * CHUNK : (i + 1) * CHUNK] = p
                att_out[h * HD : (h + 1) * HD, base : base + CHUNK] = dot_nn(
                    vw[:, base : base + span], p
                ).astype(bf16)


def attend_back_kernel(
    q, near, own, prob, att, grad_att, cos, sin, dq_out, dnear_out, down_out, dk, dv
):
    tokens = q.shape[1]
    group = H // KVH
    scale = 1.0 / math.sqrt(HD)
    span = tokens + CHUNK
    half = HD // 2
    for g in range(KVH):
        low = (KVH + g) * HD
        kw = jnp.concatenate(
            [near[g * HD : (g + 1) * HD, :], own[g * HD : (g + 1) * HD, :]], axis=1
        )
        vw = jnp.concatenate([near[low : low + HD, :], own[low : low + HD, :]], axis=1).T
        dk[...] = jnp.zeros_like(dk)
        dv[...] = jnp.zeros_like(dv)
        for c in range(tokens // CHUNK):
            base = c * CHUNK
            cut = slice(base, base + CHUNK)
            heads = [g * group + i for i in range(group)]
            q_all = jnp.concatenate([q[h * HD : (h + 1) * HD, cut] for h in heads], axis=1)
            g_all = jnp.concatenate([grad_att[h * HD : (h + 1) * HD, cut] for h in heads], axis=1)
            a_all = jnp.concatenate([att[h * HD : (h + 1) * HD, cut] for h in heads], axis=1)
            delta = jnp.sum(g_all.astype(f32) * a_all.astype(f32), axis=0, keepdims=True)
            p = prob[g, c]
            grad_prob = dot_nn(vw[base : base + span], g_all)
            ds = (p.astype(f32) * (grad_prob - delta) * scale).astype(bf16)
            dq = dot_nn(kw[:, base : base + span], ds)
            dk[:, base : base + span] += dot_nt(q_all, ds)
            dv[:, base : base + span] += dot_nt(g_all, p)
            for i, h in enumerate(heads):
                part = dq[:, i * CHUNK : (i + 1) * CHUNK]
                ra, rb = turn(part[:half], part[half:], cos[:, cut], -sin[:, cut])
                dq_out[h * HD : h * HD + half, cut] = ra.astype(bf16)
                dq_out[h * HD + half : (h + 1) * HD, cut] = rb.astype(bf16)
        dnear_out[g * HD : (g + 1) * HD, :] = dk[:, :tokens].astype(bf16)
        dnear_out[low : low + HD, :] = dv[:, :tokens].astype(bf16)
        down_out[g * HD : (g + 1) * HD, :] = dk[:, tokens:]
        down_out[low : low + HD, :] = dv[:, tokens:]


def feed_kernel(
    slots,
    att,
    tok,
    cot,
    gain,
    src_b,
    src_n,
    tall_g,
    tall_u,
    wb0,
    wb1,
    wgu,
    wd,
    mixed_out,
    res_out,
    dgate,
    dup,
    dg_low,
    du_low,
    dd_low,
    dg_high,
    du_high,
    dd_high,
    act,
    wide_n,
    dd,
):
    count = slots.shape[0]
    rows_d = FF // count
    wb = jnp.concatenate([wb0[...], wb1[...]], axis=0)
    cot_tok = cot[...].T
    att_wide = dot_nn(att[...].T, spread_wide(src_b[...])).astype(bf16)
    residual = tok[...].astype(f32).T + dot_nn(att_wide, wb)[:, :D]
    res_out[...] = residual
    inverse = lax.rsqrt(jnp.mean(residual * residual, axis=-1, keepdims=True) + norm_epsilon)
    normed = (residual * inverse * gain[...]).astype(bf16)
    wide_n[...] = dot_nn(normed, spread_wide(src_n[...])).astype(bf16)
    normed_t = normed.T
    block = 256

    def ff_step(j, carry):
        cut = pl.ds(pl.multiple_of(j * block, block), block)
        cut_up = pl.ds(pl.multiple_of(j * block + FF, block), block)
        gate = dot_nn(wide_n[...], wgu[:, cut])
        up = dot_nn(wide_n[...], wgu[:, cut_up])
        grad_act = dot_nt(cot_tok, wd[cut, :])
        sig = jax.nn.sigmoid(gate)
        silu = gate * sig
        act[:, cut] = (silu * up).astype(bf16)
        dgate[:, cut] = (grad_act * up * sig * (1.0 + gate * (1.0 - sig))).astype(bf16)
        dup[:, cut] = (grad_act * silu).astype(bf16)
        return carry

    lax.fori_loop(0, FF // block, ff_step, 0)
    mixed = residual + dot_nn(act[...], wd[...])
    mixed_out[...] = mixed.T.astype(bf16)
    for tall, grad, low, high in ((tall_g, dgate, dg_low, dg_high), (tall_u, dup, du_low, du_high)):
        wide_t = dot_nn(spread_tall(tall[...]), normed_t).astype(bf16)
        half = wide_t.shape[0] // 2
        low[...] = dot_nn(wide_t[:half], grad[...]).astype(bf16)
        high[...] = dot_nn(wide_t[half:], grad[...]).astype(bf16)
    dd[...] = dot_nn(act[...].T, cot_tok).astype(bf16)
    for p in range(count):
        source = pl.multiple_of(slots[p] * rows_d, rows_d)
        out, at = (dd_low, p) if p < count // 2 else (dd_high, p - count // 2)
        out[at * rows_d : (at + 1) * rows_d, :] = dd[pl.ds(source, rows_d), :]


def feed_back_kernel(
    residual_in,
    cot,
    gain,
    src_b,
    src_n,
    dgate,
    dup,
    wb0,
    wb1,
    wgu,
    gres_out,
    gatt_out,
    dgain_out,
):
    residual = residual_in[...]
    spread_b = spread_wide(src_b[...])
    spread_n = spread_wide(src_n[...])
    inverse = lax.rsqrt(jnp.mean(residual * residual, axis=-1, keepdims=True) + norm_epsilon)
    dn = dot_nt(dgate[...], wgu[:, :FF]) + dot_nt(dup[...], wgu[:, FF:])
    grad_normed = sum(dot_nt(part, spread_n) for part in split_two(dn))
    unit = residual * inverse
    scaled = grad_normed * gain[...]
    dgain_out[...] = jnp.sum(grad_normed * unit, axis=0, keepdims=True)
    grad_res = cot[...].T.astype(f32) + inverse * (
        scaled - unit * jnp.mean(scaled * unit, axis=-1, keepdims=True)
    )
    gres_out[...] = grad_res.T
    wb = jnp.concatenate([wb0[:, :D], wb1[:, :D]], axis=0)
    gatt_wide = dot_nt(wb, grad_res.astype(bf16)).astype(bf16)
    gatt_out[...] = dot_nn(spread_b, gatt_wide).astype(bf16)


def finish_kernel(
    dq,
    own,
    back,
    tok,
    gain,
    cos,
    sin,
    gres,
    att,
    dgain_ffn,
    src_a,
    src_b,
    tall_a,
    tall_b,
    wa0,
    wa1,
    wb0,
    wb1,
    dtok_out,
    da_low,
    db_low,
    da_high,
    db_high,
):
    x = tok[...].astype(f32)
    inverse = lax.rsqrt(jnp.mean(x * x, axis=0, keepdims=True) + norm_epsilon)
    unit = x * inverse
    normed = (unit * gain[...]).astype(bf16)
    total = own[...] + back[...].astype(f32)
    half = HD // 2
    parts = [dq[...]]
    for g in range(KVH):
        ra, rb = turn(
            total[g * HD : g * HD + half],
            total[g * HD + half : (g + 1) * HD],
            cos[...],
            -sin[...],
        )
        parts += [ra.astype(bf16), rb.astype(bf16)]
    dqk = jnp.concatenate(parts, axis=0)
    dv = total[KVH * HD :].astype(bf16)
    wa = jnp.concatenate([wa0[...], wa1[...]], axis=0)
    wb = jnp.concatenate([wb0[...], wb1[...]], axis=0)
    dvx = jnp.concatenate([jnp.zeros((H * HD, dv.shape[1]), bf16), dv], axis=0)
    dn_a = dot_nn(wa, dqk)
    dn_b = dot_nn(wb, dvx)
    spread_a = spread_wide(src_a[...])
    spread_b = spread_wide(src_b[...])
    grad_normed = sum(dot_nn(spread_a, part) for part in split_two(dn_a)) + sum(
        dot_nn(spread_b, part) for part in split_two(dn_b)
    )
    scaled = grad_normed * gain[...]
    dtok_out[...] = gres[...] + inverse * (
        scaled - unit * jnp.mean(scaled * unit, axis=0, keepdims=True)
    )
    dgain = jnp.sum(grad_normed * unit, axis=1, keepdims=True)
    dgain = jnp.broadcast_to(dgain, (D, CHUNK)).T[:1]
    tall_spread_b = spread_tall(tall_b[...])
    wide_a = dot_nn(spread_tall(tall_a[...]), normed).astype(bf16)
    wide_b = dot_nn(tall_spread_b, normed).astype(bf16)
    wide_att = dot_nn(tall_spread_b, att[...]).astype(bf16)
    fill_a = jnp.concatenate([dgain, jnp.zeros((1, KVH * HD), f32)], axis=1)
    gres_b = gres[...].astype(bf16)
    half = wide_a.shape[0] // 2
    for cut, da_out, db_out in ((slice(0, half), da_low, db_low), (slice(half, None), da_high, db_high)):
        da_out[...] = jnp.where(tall_a[cut] < 0, fill_a, dot_nt(wide_a[cut], dqk)).astype(bf16)
        d_out = dot_nt(wide_att[cut], gres_b)
        db_out[:, :D] = jnp.where(tall_b[cut] < 0, dgain_ffn[...], d_out).astype(bf16)
        db_out[:, D:] = dot_nt(wide_b[cut], dv).astype(bf16)


def merge_kernel(streams, final, *refs):
    kept, got, outs = refs[:streams], refs[streams : 2 * streams], refs[2 * streams :]
    for i in range(streams):
        total = kept[i][...].astype(f32) + got[i][...].astype(f32)
        if final:
            outs[i][...] = total
        else:
            half = total.shape[0] // 2
            outs[i][...] = total[:half].astype(bf16)
            outs[streams + i][...] = total[half:].astype(bf16)


def call_whole(kernel, outs, operands, scratch=(), scalars=()):
    vmem = pl.BlockSpec(memory_space=pltpu.VMEM)
    smem = pl.BlockSpec(memory_space=pltpu.SMEM)
    return pl.pallas_call(
        kernel,
        out_shape=[jax.ShapeDtypeStruct(s, d) for s, d in outs],
        in_specs=[smem] * len(scalars) + [vmem] * len(operands),
        out_specs=[vmem] * len(outs),
        scratch_shapes=list(scratch),
        compiler_params=pltpu.CompilerParams(vmem_limit_bytes=60 * 1024 * 1024),
    )(*scalars, *operands)


def step_double(held, orders, t):
    got = []
    for h, order in zip(held, orders):
        got.append(swapped(h, order[t]))
    return got


def joined(held, got):
    return [jnp.concatenate([h, g], axis=0) for h, g in zip(held, got)]


def step_halve(pair, orders, t):
    kept, send = pair
    streams = len(kept)
    got = []
    for value, order in zip(send, orders):
        got.append(swapped(value, order[-1 - t]))
    final = t == len(orders[0]) - 1
    if final:
        outs = [(k.shape, f32) for k in kept]
    else:
        outs = [((k.shape[0] // 2, k.shape[1]), bf16) for k in kept] * 2
    merged = call_whole(functools.partial(merge_kernel, streams, final), outs, list(kept) + got)
    return merged if final else (merged[:streams], merged[streams:])


def sources(order, count, per_slot):
    me = lax.axis_index("dev")
    owner = jnp.arange(count, dtype=jnp.int32)
    if order is not None:
        owner = me ^ jnp.asarray(slot_masks(order), jnp.int32)
    inner = jnp.arange(PAD, dtype=jnp.int32)[None, :]
    value = jnp.where(inner < per_slot, owner[:, None] * per_slot + inner, -1)
    return value.reshape(-1)


def padded_rows(value):
    return jnp.pad(value, ((0, PAD - value.shape[0]), (0, 0)))


def shards(
    tokens, positions, gain_attn, w_query, w_kv, w_out, gain_ffn, w_gate_up, w_down, cotangent
):
    count = lax.axis_size("dev")
    me = lax.axis_index("dev")
    row_count = tokens.shape[0]
    per = D // count
    per_d = FF // count
    first, rest = link_masks(count)
    order_of = [rest[k:] + rest[:k] + [first] for k in range(len(rest))]
    ord_a, ord_b = order_of[0], order_of[2]
    ord_g, ord_u, ord_d = order_of[1], order_of[2], order_of[3]
    src_a, src_b = sources(ord_a, count, per), sources(ord_b, count, per)
    src_n = sources(None, count, per)
    src_g, src_u = sources(ord_g, count, per), sources(ord_u, count, per)
    slots = me ^ jnp.asarray(slot_masks(ord_d), jnp.int32)
    w_qs, w_kvs = w_query.reshape(per, H * HD), w_kv.reshape(per, 2 * KVH * HD)
    kv_cut = KVH * HD
    stream_gu = padded_rows(w_gate_up.reshape(per, 2 * FF))
    stream_d = w_down.reshape(per_d, D)
    wgu = lax.all_gather(stream_gu, "dev", axis=0, tiled=True)
    wd = lax.all_gather(stream_d, "dev", axis=0, tiled=True)
    stream_a = padded_rows(jnp.concatenate([w_qs, w_kvs[:, :kv_cut]], axis=1))
    stream_b = padded_rows(jnp.concatenate([w_out.reshape(per, D), w_kvs[:, kv_cut:]], axis=1))
    half_dim = HD // 2
    frequency = jnp.exp(jnp.arange(half_dim, dtype=f32) * (-2.0 * math.log(theta_base) / HD))
    angles = frequency[:, None] * positions.astype(f32)[None, :]
    cos, sin = jnp.cos(angles), jnp.sin(angles)
    tok_t, cot_t = tokens.T, cotangent.T
    gain_col = gain_attn.reshape(D, 1)
    orders_ab, orders_gud = [ord_a, ord_b], [ord_g, ord_u, ord_d]
    steps = len(ord_a)
    hold = lax.optimization_barrier
    held = [stream_a, stream_b]
    early = (src_a[None], src_b[None], src_a[:, None], src_b[:, None])
    early = early + (src_n[None], src_g[:, None], src_u[:, None], slots, cos, sin, gain_col)
    for t in range(steps):
        if t == 2:
            held, early = hold((held, early))
        got = step_double(held, orders_ab, t)
        if t < steps - 1:
            held = joined(held, got)
    (wa0, wb0), (wa1, wb1) = held, got
    row_a, row_b, tall_a, tall_b, row_n, tall_g, tall_u, slots, cos, sin, gain_col = early
    q_t, kv_t = call_whole(
        project_kernel,
        [((H * HD, row_count), bf16), ((2 * kv_cut, row_count), bf16)],
        [tok_t, gain_col, cos, sin, row_a, row_b, wa0, wa1, wb0, wb1],
    )
    near = passed_along(kv_t, "dev", 1)
    chunks = row_count // CHUNK
    prob, att_t = call_whole(
        attend_kernel,
        [
            ((KVH, chunks, row_count + CHUNK, H // KVH * CHUNK), bf16),
            ((H * HD, row_count), bf16),
        ],
        [q_t, near, kv_t, positions[None]],
    )
    wide = count * PAD
    mixed_t, residual, dgate, dup, *sums = call_whole(
        feed_kernel,
        [
            ((D, row_count), bf16),
            ((row_count, D), f32),
            ((row_count, FF), bf16),
            ((row_count, FF), bf16),
        ]
        + [((wide // 2, FF), bf16), ((wide // 2, FF), bf16), ((FF // 2, D), bf16)] * 2,
        [att_t, tok_t, cot_t, gain_ffn[None], row_b, row_n, tall_g, tall_u, wb0, wb1, wgu, wd],
        scratch=[
            pltpu.VMEM((row_count, FF), bf16),
            pltpu.VMEM((row_count, wide), bf16),
            pltpu.VMEM((FF, D), bf16),
        ],
        scalars=[slots],
    )
    sums = (sums[:3], sums[3:])
    gres_t, gatt_t, dgain_ffn = call_whole(
        feed_back_kernel,
        [((D, row_count), f32), ((H * HD, row_count), bf16), ((1, D), f32)],
        [residual, cot_t, gain_ffn[None], row_b, row_n, dgate, dup, wb0, wb1, wgu],
    )
    for t in range(3):
        sums = step_halve(sums, orders_gud, t)
    dq_t, dnear, down = call_whole(
        attend_back_kernel,
        [
            ((H * HD, row_count), bf16),
            ((2 * kv_cut, row_count), bf16),
            ((2 * kv_cut, row_count), f32),
        ],
        [q_t, near, kv_t, prob, att_t, gatt_t, cos, sin],
        scratch=[pltpu.VMEM((HD, 2 * row_count), f32)] * 2,
    )
    back = passed_along(dnear, "dev", -1)
    dtok_t, *last = call_whole(
        finish_kernel,
        [
            ((D, row_count), f32),
        ]
        + [((wide // 2, H * HD + kv_cut), bf16), ((wide // 2, D + kv_cut), bf16)] * 2,
        [dq_t, down, back, tok_t, gain_col, cos, sin, gres_t, att_t, dgain_ffn]
        + [row_a, row_b, tall_a, tall_b, wa0, wa1, wb0, wb1],
    )
    last = (last[:2], last[2:])
    for t in range(steps):
        last = step_halve(last, orders_ab, t)
        if t + 3 < steps:
            sums = step_halve(sums, orders_gud, t + 3)
            last, sums = hold((last, sums))
    share_g, share_u, share_d = sums
    share_a, share_b = last
    share_kv = jnp.concatenate([share_a[:per, H * HD :], share_b[:per, D:]], axis=1)
    share_gu = jnp.concatenate([share_g[:per], share_u[:per]], axis=1)
    return (
        mixed_t.T,
        dtok_t.T,
        share_a[per, :D],
        share_a[:per, : H * HD].reshape(-1),
        share_kv.reshape(-1),
        share_b[:per, :D].reshape(-1),
        share_b[per, :D],
        share_gu.reshape(-1),
        share_d.reshape(-1),
    )


def fits_whole_rows(count):
    per = D // count
    return D % count == 0 and FF % count == 0 and (FF // count) % 16 == 0 and 16 <= per <= PAD


def solution(mesh):
    in_specs = (
        P("dev", None),
        P("dev"),
        P(),
        P("dev"),
        P("dev"),
        P("dev"),
        P(),
        P("dev"),
        P("dev"),
        P("dev", None),
    )
    out_specs = (
        P("dev", None),
        P("dev", None),
        P(),
        P("dev"),
        P("dev"),
        P("dev"),
        P(),
        P("dev"),
        P("dev"),
    )
    whole_rows = fits_whole_rows(mesh.shape["dev"])

    def layer(*args):
        return shards(*args)

    return jax.shard_map(
        layer if whole_rows else shards_general,
        mesh=mesh,
        in_specs=in_specs,
        out_specs=out_specs,
        check_vma=False,
    )
```

```python
import math

import jax
import jax.numpy as jnp
from jax import lax
from jax.experimental import pallas as pl
from jax.experimental.pallas import tpu as pltpu
from jax.sharding import PartitionSpec as P


D = 576
H = 9
KVH = 3
HD = 64
FF = 1536


norm_epsilon = 1e-05
theta_base = 100000.0


def passed_along(value, axis, steps):
    count = lax.axis_size(axis)
    first, last = (max(0, -steps), min(count, count - steps))
    return lax.ppermute(value, axis, [(source, source + steps) for source in range(first, last)])


def link_masks(count):
    bits = [1 << b for b in range(count.bit_length() - 1)]
    if count == 32:
        bits = [1, 2, 4, 8, 24]
    return bits[0], bits[1:]


def swapped(value, mask):
    count = lax.axis_size("dev")
    return lax.ppermute(value, "dev", [(i, i ^ mask) for i in range(count)])


def color_orders(count, colors):
    first, rest = link_masks(count)
    if colors == 1:
        return [rest + [first]]
    step = len(rest) // colors
    return [rest[c * step :] + rest[: c * step] + [first] for c in range(colors)]


def slot_masks(order):
    slots = [0]
    for mask in order:
        slots = slots + [s ^ mask for s in slots]
    return slots


def cut_rows(rows, colors):
    edges = [rows * c // colors for c in range(colors + 1)]
    return list(zip(edges[:-1], edges[1:]))


def gather_all(block, colors):
    count = lax.axis_size("dev")
    me = lax.axis_index("dev")
    orders = color_orders(count, colors)
    held = [block[a:b][None] for a, b in cut_rows(block.shape[0], colors)]
    for t in range(len(orders[0])):
        got = [swapped(h, order[t]) for h, order in zip(held, orders)]
        held = [jnp.concatenate([h, g], axis=0) for h, g in zip(held, got)]
    whole = []
    for h, order in zip(held, orders):
        slots = slot_masks(order)
        where = [0] * count
        for place, mask in enumerate(slots):
            where[mask] = place
        index = jnp.asarray(where, jnp.int32)[me ^ jnp.arange(count, dtype=jnp.int32)]
        whole.append(jnp.take(h, index, axis=0, mode="clip"))
    return jnp.concatenate(whole, axis=1)


def scatter_sum(parts, colors):
    count = lax.axis_size("dev")
    me = lax.axis_index("dev")
    orders = color_orders(count, colors)
    held = []
    for (a, b), order in zip(cut_rows(parts.shape[1], colors), orders):
        slots = jnp.asarray(slot_masks(order), jnp.int32)
        held.append(jnp.take(parts[:, a:b], me ^ slots, axis=0, mode="clip"))
    for t in range(len(orders[0])):
        half = held[0].shape[0] // 2
        masks = [order[-1 - t] for order in orders]
        got = [swapped(h[half:].astype(jnp.bfloat16), m) for h, m in zip(held, masks)]
        held = [h[:half].astype(jnp.float32) + g.astype(jnp.float32) for h, g in zip(held, got)]
    return jnp.concatenate([h[0] for h in held], axis=0)


def sum_all(value):
    first, rest = link_masks(lax.axis_size("dev"))
    for mask in [first] + rest:
        value = value + swapped(value, mask)
    return value


def norm_forward(values, scale_gain):
    inverse = lax.rsqrt(jnp.mean(values * values, axis=-1, keepdims=True) + norm_epsilon)
    return (values * inverse * scale_gain, inverse)


def norm_backward(grad_output, values, inverse, scale_gain):
    unit_rows = values * inverse
    scaled = grad_output * scale_gain
    grad_gain = jnp.sum(grad_output * unit_rows, axis=0)
    grad_input = inverse * (
        scaled - unit_rows * jnp.mean(scaled * unit_rows, axis=-1, keepdims=True)
    )
    return (grad_input, grad_gain)


def rope_angles(position_block):
    half_dim = HD // 2
    frequency = jnp.exp(
        jnp.arange(half_dim, dtype=jnp.float32) * (-2.0 * math.log(theta_base) / HD)
    )
    angles = position_block.astype(jnp.float32)[:, None] * frequency[None, :]
    return (jnp.cos(angles)[:, None, :], jnp.sin(angles)[:, None, :])


def rotate(values, cos_table, sin_table):
    half_dim = values.shape[-1] // 2
    first_half = values[..., :half_dim]
    second_half = values[..., half_dim:]
    return jnp.concatenate(
        [
            first_half * cos_table - second_half * sin_table,
            second_half * cos_table + first_half * sin_table,
        ],
        axis=-1,
    )


def project_heads(normed, query_mat, keyval_mat, cos_table, sin_table):
    row_count = normed.shape[0]
    queries = jnp.dot(normed, query_mat, preferred_element_type=jnp.float32).reshape(
        row_count, H, HD
    )
    keyvals = jnp.dot(normed, keyval_mat, preferred_element_type=jnp.float32)
    keys_rot = rotate(
        keyvals[:, : KVH * HD].reshape(row_count, KVH, HD), cos_table, sin_table
    ).reshape(row_count, KVH * HD)
    query_rot = (
        rotate(queries, cos_table, sin_table).reshape(row_count, H * HD).astype(jnp.bfloat16)
    )
    keyval_rot = jnp.concatenate([keys_rot, keyvals[:, KVH * HD :]], axis=1).astype(jnp.bfloat16)
    return (query_rot, keyval_rot)


def window_mask(position_block, row_count):
    query_at = jnp.arange(row_count, dtype=jnp.int32)[:, None] + row_count
    key_at = jnp.arange(2 * row_count, dtype=jnp.int32)[None, :]
    return (key_at <= query_at) & (key_at >= query_at - position_block[:, None])


def masked_scores(query_group, key_group, allowed):
    scale_factor = 1.0 / math.sqrt(HD)
    scores = (
        jnp.einsum("tqd,wd->qtw", query_group, key_group, preferred_element_type=jnp.float32)
        * scale_factor
    )
    return jnp.where(allowed[None], scores, -1e30)


def attend_forward(query_rot, window, allowed):
    row_count = query_rot.shape[0]
    grouped = H // KVH
    queries = query_rot.reshape(row_count, H, HD)
    outputs = []
    totals = []
    for group_index in range(KVH):
        query_group = queries[:, group_index * grouped : (group_index + 1) * grouped]
        key_group = window[:, group_index * HD : (group_index + 1) * HD]
        value_group = window[:, (KVH + group_index) * HD : (KVH + group_index + 1) * HD]
        scores = masked_scores(query_group, key_group, allowed)
        highest = jnp.max(scores, axis=-1, keepdims=True)
        log_total = highest + jnp.log(jnp.sum(jnp.exp(scores - highest), axis=-1, keepdims=True))
        probability = jnp.exp(scores - log_total).astype(jnp.bfloat16)
        head_out = jnp.einsum(
            "qtw,wd->tqd", probability, value_group, preferred_element_type=jnp.float32
        )
        outputs.append(head_out.astype(jnp.bfloat16))
        totals.append(log_total)
    return (jnp.concatenate(outputs, axis=1).reshape(row_count, H * HD), totals)


def attend_backward(query_rot, window, allowed, attended, grad_attended, totals):
    row_count = query_rot.shape[0]
    grouped = H // KVH
    scale_factor = 1.0 / math.sqrt(HD)
    queries = query_rot.reshape(row_count, H, HD)
    attended_heads = attended.reshape(row_count, H, HD)
    grad_heads = grad_attended.reshape(row_count, H, HD)
    query_grads = []
    key_grads = []
    value_grads = []
    for group_index in range(KVH):
        head_slice = slice(group_index * grouped, (group_index + 1) * grouped)
        query_group = queries[:, head_slice]
        key_group = window[:, group_index * HD : (group_index + 1) * HD]
        value_group = window[:, (KVH + group_index) * HD : (KVH + group_index + 1) * HD]
        scores = masked_scores(query_group, key_group, allowed)
        probability = jnp.exp(scores - totals[group_index])
        grad_group = grad_heads[:, head_slice]
        row_delta = jnp.sum(
            grad_group.astype(jnp.float32) * attended_heads[:, head_slice].astype(jnp.float32),
            axis=-1,
        )
        grad_prob = jnp.einsum(
            "tqd,wd->qtw", grad_group, value_group, preferred_element_type=jnp.float32
        )
        grad_scores = (probability * (grad_prob - row_delta.T[:, :, None]) * scale_factor).astype(
            jnp.bfloat16
        )
        query_grads.append(
            jnp.einsum("qtw,wd->tqd", grad_scores, key_group, preferred_element_type=jnp.float32)
        )
        key_grads.append(
            jnp.einsum("qtw,tqd->wd", grad_scores, query_group, preferred_element_type=jnp.float32)
        )
        value_grads.append(
            jnp.einsum(
                "qtw,tqd->wd",
                probability.astype(jnp.bfloat16),
                grad_group,
                preferred_element_type=jnp.float32,
            )
        )
    return (jnp.concatenate(query_grads, axis=1), jnp.concatenate(key_grads + value_grads, axis=1))


def shards_general(
    tokens, positions, gain_attn, w_query, w_kv, w_out, gain_ffn, w_gate_up, w_down, cotangent
):
    row_count = tokens.shape[0]
    width_kv = 2 * KVH * HD
    count = lax.axis_size("dev")
    attn_sizes = [w_query.shape[0], w_kv.shape[0], w_out.shape[0]]
    ffn_sizes = [w_gate_up.shape[0], w_down.shape[0]]
    attn_all = gather_all(jnp.concatenate([w_query, w_kv, w_out]).reshape(-1, 128), 2)
    attn_all = attn_all.reshape(count, -1)
    query_mat = attn_all[:, : attn_sizes[0]].reshape(D, H * HD)
    keyval_mat = attn_all[:, attn_sizes[0] : attn_sizes[0] + attn_sizes[1]].reshape(D, width_kv)
    out_mat = attn_all[:, attn_sizes[0] + attn_sizes[1] :].reshape(H * HD, D)
    ffn_all = gather_all(jnp.concatenate([w_gate_up, w_down]).reshape(-1, 128), 4)
    ffn_all = ffn_all.reshape(count, -1)
    gate_up_mat = ffn_all[:, : ffn_sizes[0]].reshape(D, 2 * FF)
    down_mat = ffn_all[:, ffn_sizes[0] :].reshape(FF, D)
    inputs = tokens.astype(jnp.float32)
    normed_attn, inverse_attn = norm_forward(inputs, gain_attn)
    normed_attn = normed_attn.astype(jnp.bfloat16)
    cos_table, sin_table = rope_angles(positions)
    query_rot, keyval_rot = project_heads(normed_attn, query_mat, keyval_mat, cos_table, sin_table)
    near_keys = passed_along(keyval_rot, "dev", 1)
    window = jnp.concatenate([near_keys, keyval_rot], axis=0)
    allowed = window_mask(positions, row_count)
    attended, totals = attend_forward(query_rot, window, allowed)
    residual = inputs + jnp.dot(attended, out_mat, preferred_element_type=jnp.float32)
    normed_ffn, inverse_ffn = norm_forward(residual, gain_ffn)
    normed_ffn = normed_ffn.astype(jnp.bfloat16)
    gate_up = jnp.dot(normed_ffn, gate_up_mat, preferred_element_type=jnp.float32)
    gate_part = gate_up[:, :FF]
    up_part = gate_up[:, FF:]
    activated = (jax.nn.silu(gate_part) * up_part).astype(jnp.bfloat16)
    mixed = (residual + jnp.dot(activated, down_mat, preferred_element_type=jnp.float32)).astype(
        jnp.bfloat16
    )
    grad_act = jnp.dot(cotangent, down_mat.T, preferred_element_type=jnp.float32)
    sigmoid_gate = jax.nn.sigmoid(gate_part)
    grad_gate_up_act = jnp.concatenate(
        [
            grad_act * up_part * sigmoid_gate * (1.0 + gate_part * (1.0 - sigmoid_gate)),
            grad_act * jax.nn.silu(gate_part),
        ],
        axis=1,
    ).astype(jnp.bfloat16)
    grad_down = jnp.dot(activated.T, cotangent, preferred_element_type=jnp.float32)
    grad_gate_up = jnp.dot(normed_ffn.T, grad_gate_up_act, preferred_element_type=jnp.float32)
    grad_normed_ffn = jnp.dot(grad_gate_up_act, gate_up_mat.T, preferred_element_type=jnp.float32)
    grad_norm_ffn, grad_gain_ffn = norm_backward(grad_normed_ffn, residual, inverse_ffn, gain_ffn)
    grad_residual = cotangent.astype(jnp.float32) + grad_norm_ffn
    grad_residual_b = grad_residual.astype(jnp.bfloat16)
    grad_out = jnp.dot(attended.T, grad_residual_b, preferred_element_type=jnp.float32)
    grad_attended = jnp.dot(grad_residual_b, out_mat.T, preferred_element_type=jnp.float32).astype(
        jnp.bfloat16
    )
    grad_query_rot, grad_window = attend_backward(
        query_rot, window, allowed, attended, grad_attended, totals
    )
    back_near = passed_along(grad_window[:row_count].astype(jnp.bfloat16), "dev", -1).astype(jnp.float32)
    grad_keyval_rot = grad_window[row_count:] + back_near
    key_part = rotate(
        grad_keyval_rot[:, : KVH * HD].reshape(row_count, KVH, HD), cos_table, -sin_table
    ).reshape(row_count, KVH * HD)
    grad_keyval_act = jnp.concatenate([key_part, grad_keyval_rot[:, KVH * HD :]], axis=1).astype(
        jnp.bfloat16
    )
    grad_query_act = (
        rotate(grad_query_rot, cos_table, -sin_table)
        .reshape(row_count, H * HD)
        .astype(jnp.bfloat16)
    )
    grad_query = jnp.dot(normed_attn.T, grad_query_act, preferred_element_type=jnp.float32)
    grad_keyval = jnp.dot(normed_attn.T, grad_keyval_act, preferred_element_type=jnp.float32)
    grad_normed_attn = jnp.dot(
        grad_query_act, query_mat.T, preferred_element_type=jnp.float32
    ) + jnp.dot(grad_keyval_act, keyval_mat.T, preferred_element_type=jnp.float32)
    grad_input, grad_gain_attn = norm_backward(grad_normed_attn, inputs, inverse_attn, gain_attn)
    token_grads = grad_residual + grad_input
    ffn_parts = jnp.concatenate(
        [
            grad_gate_up.reshape(count, -1).astype(jnp.bfloat16),
            grad_down.reshape(count, -1).astype(jnp.bfloat16),
            grad_out.reshape(count, -1).astype(jnp.bfloat16),
        ],
        axis=1,
    )
    ffn_parts = jnp.pad(ffn_parts, ((0, 0), (0, -ffn_parts.shape[1] % 128)))
    ffn_share = scatter_sum(ffn_parts.reshape(count, -1, 128), 4).reshape(-1)
    share_gate_up = ffn_share[: ffn_sizes[0]]
    share_down = ffn_share[ffn_sizes[0] : ffn_sizes[0] + ffn_sizes[1]]
    share_out = ffn_share[ffn_sizes[0] + ffn_sizes[1] : sum(ffn_sizes) + attn_sizes[2]]
    attn_parts = jnp.concatenate(
        [
            grad_query.reshape(count, -1).astype(jnp.bfloat16),
            grad_keyval.reshape(count, -1).astype(jnp.bfloat16),
        ],
        axis=1,
    )
    attn_rows = attn_parts.shape[1]
    attn_parts = jnp.pad(attn_parts, ((0, 0), (0, -attn_rows % 128)))
    attn_share = scatter_sum(attn_parts.reshape(count, -1, 128), 2).reshape(-1)
    share_query = attn_share[: attn_sizes[0]]
    share_keyval = attn_share[attn_sizes[0] : attn_sizes[0] + attn_sizes[1]]
    gain_sums = sum_all(jnp.stack([grad_gain_attn, grad_gain_ffn]))
    gain_attn_sum = gain_sums[0]
    gain_ffn_sum = gain_sums[1]
    return (
        mixed,
        token_grads,
        gain_attn_sum,
        share_query,
        share_keyval,
        share_out,
        gain_ffn_sum,
        share_gate_up,
        share_down,
    )


PAD = 24
FOLD_LANES = 640
CHUNK = 128
bf16 = jnp.bfloat16
f32 = jnp.float32


def dot_nn(a, b):
    return lax.dot_general(a, b, (((1,), (0,)), ((), ())), preferred_element_type=f32)


def dot_nt(a, b):
    return lax.dot_general(a, b, (((1,), (1,)), ((), ())), preferred_element_type=f32)


def spread_wide(source_row):
    rows = lax.broadcasted_iota(jnp.int32, (D, source_row.shape[1]), 0)
    return jnp.where(rows == source_row, 1.0, 0.0).astype(bf16)


def spread_tall(source_col):
    lanes = lax.broadcasted_iota(jnp.int32, (source_col.shape[0], D), 1)
    return jnp.where(lanes == source_col, 1.0, 0.0).astype(bf16)


def turn(a, b, cos_table, sin_table):
    return a * cos_table - b * sin_table, b * cos_table + a * sin_table


def project_kernel(tok, gain, cos, sin, src_a, src_b, wa0, wa1, wb0, wb1, q_out, kv_out):
    x = tok[...].astype(f32)
    inverse = lax.rsqrt(jnp.mean(x * x, axis=0, keepdims=True) + norm_epsilon)
    normed = (x * inverse * gain[...]).astype(bf16).T
    cos_table, sin_table = cos[...], sin[...]
    wa = jnp.concatenate([wa0[...], wa1[...]], axis=0)
    wb = jnp.concatenate([wb0[...], wb1[...]], axis=0)
    wide_a = dot_nn(normed, spread_wide(src_a[...])).astype(bf16)
    wide_b = dot_nn(normed, spread_wide(src_b[...])).astype(bf16)
    qk = dot_nn(wide_a, wa).T
    v = dot_nn(wide_b, wb).T[H * HD :]
    half = HD // 2
    for h in range(H + KVH):
        a = qk[h * HD : h * HD + half]
        b = qk[h * HD + half : (h + 1) * HD]
        ra, rb = turn(a, b, cos_table, sin_table)
        out, row = (q_out, h * HD) if h < H else (kv_out, (h - H) * HD)
        out[row : row + half, :] = ra.astype(bf16)
        out[row + half : row + HD, :] = rb.astype(bf16)
    kv_out[KVH * HD :, :] = v.astype(bf16)


def attend_kernel(q, near, own, pos, prob_out, att_out):
    tokens = q.shape[1]
    group = H // KVH
    scale = 1.0 / math.sqrt(HD)
    span = tokens + CHUNK
    rows = lax.broadcasted_iota(jnp.int32, (span, CHUNK), 0)
    lanes = lax.broadcasted_iota(jnp.int32, (span, CHUNK), 1) + tokens
    for g in range(KVH):
        kw = jnp.concatenate(
            [near[g * HD : (g + 1) * HD, :], own[g * HD : (g + 1) * HD, :]], axis=1
        ).T
        low = (KVH + g) * HD
        vw = jnp.concatenate([near[low : low + HD, :], own[low : low + HD, :]], axis=1)
        for c in range(tokens // CHUNK):
            base = c * CHUNK
            position = pos[:, base : base + CHUNK]
            allowed = (rows <= lanes) & (rows >= lanes - position)
            for i in range(group):
                h = g * group + i
                qh = q[h * HD : (h + 1) * HD, base : base + CHUNK]
                scores = dot_nn(kw[base : base + span], qh) * scale
                scores = jnp.where(allowed, scores, -1e30)
                highest = jnp.max(scores, axis=0, keepdims=True)
                e = jnp.exp(scores - highest)
                total = jnp.sum(e, axis=0, keepdims=True)
                p = (e * (1.0 / total)).astype(bf16)
                prob_out[g, c, :, i * CHUNK : (i + 1) * CHUNK] = p
                att_out[h * HD : (h + 1) * HD, base : base + CHUNK] = dot_nn(
                    vw[:, base : base + span], p
                ).astype(bf16)


def attend_back_kernel(
    q, near, own, prob, att, grad_att, cos, sin, dq_out, dnear_out, down_out, dk, dv
):
    tokens = q.shape[1]
    group = H // KVH
    scale = 1.0 / math.sqrt(HD)
    span = tokens + CHUNK
    half = HD // 2
    for g in range(KVH):
        low = (KVH + g) * HD
        kw = jnp.concatenate(
            [near[g * HD : (g + 1) * HD, :], own[g * HD : (g + 1) * HD, :]], axis=1
        )
        vw = jnp.concatenate([near[low : low + HD, :], own[low : low + HD, :]], axis=1).T
        dk[...] = jnp.zeros_like(dk)
        dv[...] = jnp.zeros_like(dv)
        for c in range(tokens // CHUNK):
            base = c * CHUNK
            cut = slice(base, base + CHUNK)
            heads = [g * group + i for i in range(group)]
            q_all = jnp.concatenate([q[h * HD : (h + 1) * HD, cut] for h in heads], axis=1)
            g_all = jnp.concatenate([grad_att[h * HD : (h + 1) * HD, cut] for h in heads], axis=1)
            a_all = jnp.concatenate([att[h * HD : (h + 1) * HD, cut] for h in heads], axis=1)
            delta = jnp.sum(g_all.astype(f32) * a_all.astype(f32), axis=0, keepdims=True)
            p = prob[g, c]
            grad_prob = dot_nn(vw[base : base + span], g_all)
            ds = (p.astype(f32) * (grad_prob - delta) * scale).astype(bf16)
            dq = dot_nn(kw[:, base : base + span], ds)
            dk[:, base : base + span] += dot_nt(q_all, ds)
            dv[:, base : base + span] += dot_nt(g_all, p)
            for i, h in enumerate(heads):
                part = dq[:, i * CHUNK : (i + 1) * CHUNK]
                ra, rb = turn(part[:half], part[half:], cos[:, cut], -sin[:, cut])
                dq_out[h * HD : h * HD + half, cut] = ra.astype(bf16)
                dq_out[h * HD + half : (h + 1) * HD, cut] = rb.astype(bf16)
        dnear_out[g * HD : (g + 1) * HD, :] = dk[:, :tokens].astype(bf16)
        dnear_out[low : low + HD, :] = dv[:, :tokens].astype(bf16)
        down_out[g * HD : (g + 1) * HD, :] = dk[:, tokens:]
        down_out[low : low + HD, :] = dv[:, tokens:]


def prepare_kernel(
    att,
    tok,
    gain_in,
    gain,
    row_b,
    row_n,
    tall_g,
    tall_u,
    tall_a,
    tall_b,
    wb0,
    wb1,
    res_out,
    wide_n,
    tall_wide_g,
    tall_wide_u,
    tall_wide_a,
    tall_wide_b,
    tall_wide_att,
):
    wb = jnp.concatenate([wb0[...], wb1[...]], axis=0)
    x = tok[...].astype(f32)
    att_wide = dot_nn(att[...].T, spread_wide(row_b[...])).astype(bf16)
    residual = x.T + dot_nn(att_wide, wb)[:, :D]
    res_out[...] = residual
    inverse = lax.rsqrt(jnp.mean(residual * residual, axis=-1, keepdims=True) + norm_epsilon)
    normed = (residual * inverse * gain[...]).astype(bf16)
    wide_n[...] = dot_nn(normed, spread_wide(row_n[...])).astype(bf16)
    normed_t = normed.T
    tall_wide_g[...] = dot_nn(spread_tall(tall_g[...]), normed_t).astype(bf16)
    tall_wide_u[...] = dot_nn(spread_tall(tall_u[...]), normed_t).astype(bf16)
    inverse_in = lax.rsqrt(jnp.mean(x * x, axis=0, keepdims=True) + norm_epsilon)
    normed_in = (x * inverse_in * gain_in[...]).astype(bf16)
    spread_b = spread_tall(tall_b[...])
    tall_wide_a[...] = dot_nn(spread_tall(tall_a[...]), normed_in).astype(bf16)
    tall_wide_b[...] = dot_nn(spread_b, normed_in).astype(bf16)
    tall_wide_att[...] = dot_nn(spread_b, att[...]).astype(bf16)


def feed_kernel(
    slots,
    residual,
    cot,
    wide_n,
    tall_wide_g,
    tall_wide_u,
    wall,
    mixed_out,
    dgate,
    dup,
    dg_low,
    du_low,
    dd_low,
    dg_high,
    du_high,
    dd_high,
    act,
    wd,
):
    count = slots.shape[0]
    rows_d = FF // count
    fold = rows_d // 2
    for j in range(count):
        for k in range(2):
            at = 2 * FF + k * FOLD_LANES
            wd[j * rows_d + k * fold : j * rows_d + (k + 1) * fold, :] = wall[
                j * PAD : j * PAD + fold, at : at + D
            ]
    cot_tok = cot[...].T
    block = 256

    def ff_step(j, carry):
        cut = pl.ds(pl.multiple_of(j * block, block), block)
        cut_up = pl.ds(pl.multiple_of(j * block + FF, block), block)
        gate = dot_nn(wide_n[...], wall[:, cut])
        up = dot_nn(wide_n[...], wall[:, cut_up])
        grad_act = dot_nt(cot_tok, wd[cut, :])
        sig = jax.nn.sigmoid(gate)
        silu = gate * sig
        act[:, cut] = (silu * up).astype(bf16)
        dgate[:, cut] = (grad_act * up * sig * (1.0 + gate * (1.0 - sig))).astype(bf16)
        dup[:, cut] = (grad_act * silu).astype(bf16)
        return carry

    lax.fori_loop(0, FF // block, ff_step, 0)
    mixed = residual[...] + dot_nn(act[...], wd[...])
    mixed_out[...] = mixed.T.astype(bf16)
    half = tall_wide_g.shape[0] // 2
    dg_low[...] = dot_nn(tall_wide_g[:half, :], dgate[...]).astype(bf16)
    dg_high[...] = dot_nn(tall_wide_g[half:, :], dgate[...]).astype(bf16)
    du_low[...] = dot_nn(tall_wide_u[:half, :], dup[...]).astype(bf16)
    du_high[...] = dot_nn(tall_wide_u[half:, :], dup[...]).astype(bf16)
    wd[...] = dot_nn(act[...].T, cot_tok).astype(bf16)
    for p in range(count):
        source = pl.multiple_of(slots[p] * rows_d, rows_d)
        out, at = (dd_low, p) if p < count // 2 else (dd_high, p - count // 2)
        out[at * rows_d : (at + 1) * rows_d, :] = wd[pl.ds(source, rows_d), :]


def feed_back_kernel(
    residual_in,
    cot,
    gain,
    src_b,
    src_n,
    dgate,
    dup,
    wb0,
    wb1,
    wall,
    gres_out,
    gatt_out,
    dgain_out,
):
    residual = residual_in[...]
    spread_b = spread_wide(src_b[...])
    spread_n = spread_wide(src_n[...])
    inverse = lax.rsqrt(jnp.mean(residual * residual, axis=-1, keepdims=True) + norm_epsilon)
    dn = dot_nt(dgate[...], wall[:, :FF]) + dot_nt(dup[...], wall[:, FF : 2 * FF])
    grad_normed = dot_nt(dn.astype(bf16), spread_n)
    unit = residual * inverse
    scaled = grad_normed * gain[...]
    dgain_out[...] = jnp.sum(grad_normed * unit, axis=0, keepdims=True)
    grad_res = cot[...].T.astype(f32) + inverse * (
        scaled - unit * jnp.mean(scaled * unit, axis=-1, keepdims=True)
    )
    gres_out[...] = grad_res.T
    wb = jnp.concatenate([wb0[:, :D], wb1[:, :D]], axis=0)
    gatt_wide = dot_nt(wb, grad_res.astype(bf16)).astype(bf16)
    gatt_out[...] = dot_nn(spread_b, gatt_wide).astype(bf16)


def finish_kernel(
    dq,
    own,
    back,
    tok,
    gain,
    cos,
    sin,
    gres,
    wide_a,
    wide_b,
    wide_att,
    dgain_ffn,
    src_a,
    src_b,
    tall_a,
    tall_b,
    wa0,
    wa1,
    wb0,
    wb1,
    dtok_out,
    da_low,
    db_low,
    da_high,
    db_high,
):
    x = tok[...].astype(f32)
    inverse = lax.rsqrt(jnp.mean(x * x, axis=0, keepdims=True) + norm_epsilon)
    unit = x * inverse
    total = own[...] + back[...].astype(f32)
    half = HD // 2
    parts = [dq[...]]
    for g in range(KVH):
        ra, rb = turn(
            total[g * HD : g * HD + half],
            total[g * HD + half : (g + 1) * HD],
            cos[...],
            -sin[...],
        )
        parts += [ra.astype(bf16), rb.astype(bf16)]
    dqk = jnp.concatenate(parts, axis=0)
    dv = total[KVH * HD :].astype(bf16)
    wa = jnp.concatenate([wa0[...], wa1[...]], axis=0)
    wb = jnp.concatenate([wb0[...], wb1[...]], axis=0)
    dvx = jnp.concatenate([jnp.zeros((H * HD, dv.shape[1]), bf16), dv], axis=0)
    dn_a = dot_nn(wa, dqk)
    dn_b = dot_nn(wb, dvx)
    spread_a = spread_wide(src_a[...])
    spread_b = spread_wide(src_b[...])
    grad_normed = dot_nn(spread_a, dn_a.astype(bf16)) + dot_nn(spread_b, dn_b.astype(bf16))
    scaled = grad_normed * gain[...]
    dtok_out[...] = gres[...] + inverse * (
        scaled - unit * jnp.mean(scaled * unit, axis=0, keepdims=True)
    )
    dgain = jnp.sum(grad_normed * unit, axis=1, keepdims=True)
    dgain = jnp.broadcast_to(dgain, (D, CHUNK)).T[:1]
    fill_a = jnp.concatenate([dgain, jnp.zeros((1, KVH * HD), f32)], axis=1)
    gres_b = gres[...].astype(bf16)
    half = wide_a.shape[0] // 2
    for cut, da_out, db_out in ((slice(0, half), da_low, db_low), (slice(half, None), da_high, db_high)):
        da_out[...] = jnp.where(tall_a[cut, :] < 0, fill_a, dot_nt(wide_a[cut, :], dqk)).astype(bf16)
        d_out = dot_nt(wide_att[cut, :], gres_b)
        db_out[:, :D] = jnp.where(tall_b[cut, :] < 0, dgain_ffn[...], d_out).astype(bf16)
        db_out[:, D:] = dot_nt(wide_b[cut, :], dv).astype(bf16)


def call_whole(kernel, outs, operands, scratch=(), scalars=()):
    vmem = pl.BlockSpec(memory_space=pltpu.VMEM)
    smem = pl.BlockSpec(memory_space=pltpu.SMEM)
    return pl.pallas_call(
        kernel,
        out_shape=[jax.ShapeDtypeStruct(s, d) for s, d in outs],
        in_specs=[smem] * len(scalars) + [vmem] * len(operands),
        out_specs=[vmem] * len(outs),
        scratch_shapes=list(scratch),
        compiler_params=pltpu.CompilerParams(vmem_limit_bytes=60 * 1024 * 1024),
    )(*scalars, *operands)


def step_double(held, orders, t):
    got = []
    for h, order in zip(held, orders):
        got.append(swapped(h, order[t]))
    return got


def joined(held, got):
    return [jnp.concatenate([h, g], axis=0) for h, g in zip(held, got)]


def step_halve(pair, orders, t, even=False):
    kept, send = pair
    final = t == len(orders[0]) - 1
    low, high = [], []
    for k, value, order in zip(kept, send, orders):
        g = swapped(value, order[-1 - t])
        if even:
            k = lax.reduce_precision(k.astype(f32), 8, 7)
        half = k.shape[0] if final else k.shape[0] // 2
        low.append(k[:half].astype(f32) + g[:half].astype(f32))
        high.append((k[half:].astype(f32) + g[half:].astype(f32)).astype(bf16))
    return low if final else (low, high)


def sources(order, count, per_slot):
    me = lax.axis_index("dev")
    owner = jnp.arange(count, dtype=jnp.int32)
    if order is not None:
        owner = me ^ jnp.asarray(slot_masks(order), jnp.int32)
    inner = jnp.arange(PAD, dtype=jnp.int32)[None, :]
    value = jnp.where(inner < per_slot, owner[:, None] * per_slot + inner, -1)
    return value.reshape(-1)


def padded_rows(value):
    return jnp.pad(value, ((0, PAD - value.shape[0]), (0, 0)))


def shards(
    tokens, positions, gain_attn, w_query, w_kv, w_out, gain_ffn, w_gate_up, w_down, cotangent
):
    count = lax.axis_size("dev")
    me = lax.axis_index("dev")
    row_count = tokens.shape[0]
    per = D // count
    per_d = FF // count
    first, rest = link_masks(count)
    order_of = [rest[k:] + rest[:k] + [first] for k in range(len(rest))]
    ord_a, ord_b = order_of[0], order_of[2]
    ord_g, ord_u, ord_d = order_of[1], order_of[2], order_of[3]
    src_a, src_b = sources(ord_a, count, per), sources(ord_b, count, per)
    src_n = sources(None, count, per)
    src_g, src_u = sources(ord_g, count, per), sources(ord_u, count, per)
    slots = me ^ jnp.asarray(slot_masks(ord_d), jnp.int32)
    w_qs, w_kvs = w_query.reshape(per, H * HD), w_kv.reshape(per, 2 * KVH * HD)
    kv_cut = KVH * HD
    stream_gu = padded_rows(w_gate_up.reshape(per, 2 * FF))
    folded = w_down.reshape(2, per_d // 2, D)
    folded = jnp.pad(folded, ((0, 0), (0, PAD - per_d // 2), (0, FOLD_LANES - D)))
    stream_ffn = jnp.concatenate([stream_gu, folded[0], folded[1]], axis=1)
    wall = lax.all_gather(stream_ffn, "dev", axis=0, tiled=True)
    stream_a = padded_rows(jnp.concatenate([w_qs, w_kvs[:, :kv_cut]], axis=1))
    stream_b = padded_rows(jnp.concatenate([w_out.reshape(per, D), w_kvs[:, kv_cut:]], axis=1))
    half_dim = HD // 2
    frequency = jnp.exp(jnp.arange(half_dim, dtype=f32) * (-2.0 * math.log(theta_base) / HD))
    angles = frequency[:, None] * positions.astype(f32)[None, :]
    cos, sin = jnp.cos(angles), jnp.sin(angles)
    tok_t, cot_t = tokens.T, cotangent.T
    gain_col = gain_attn.reshape(D, 1)
    orders_ab, orders_gud = [ord_a, ord_b], [ord_g, ord_u, ord_d]
    steps = len(ord_a)
    hold = lax.optimization_barrier
    held = [stream_a, stream_b]
    early = (src_a[None], src_b[None], src_a[:, None], src_b[:, None])
    early = early + (src_n[None], src_g[:, None], src_u[:, None], slots, cos, sin, gain_col)
    for t in range(steps):
        if t == 2:
            held, early = hold((held, early))
        got = step_double(held, orders_ab, t)
        if t < steps - 1:
            held = joined(held, got)
    (wa0, wb0), (wa1, wb1) = held, got
    row_a, row_b, tall_a, tall_b, row_n, tall_g, tall_u, slots, cos, sin, gain_col = early
    q_t, kv_t = call_whole(
        project_kernel,
        [((H * HD, row_count), bf16), ((2 * kv_cut, row_count), bf16)],
        [tok_t, gain_col, cos, sin, row_a, row_b, wa0, wa1, wb0, wb1],
    )
    near = passed_along(kv_t, "dev", 1)
    chunks = row_count // CHUNK
    prob, att_t = call_whole(
        attend_kernel,
        [
            ((KVH, chunks, row_count + CHUNK, H // KVH * CHUNK), bf16),
            ((H * HD, row_count), bf16),
        ],
        [q_t, near, kv_t, positions[None]],
    )
    wide = count * PAD
    tall_shape = ((wide, row_count), bf16)
    residual, wide_n, tall_wide_g, tall_wide_u, wide_a, wide_b, wide_att = call_whole(
        prepare_kernel,
        [((row_count, D), f32), ((row_count, wide), bf16)] + [tall_shape] * 5,
        [att_t, tok_t, gain_col, gain_ffn[None], row_b, row_n, tall_g, tall_u, tall_a, tall_b]
        + [wb0, wb1],
    )
    mixed_t, dgate, dup, *sums = call_whole(
        feed_kernel,
        [
            ((D, row_count), bf16),
            ((row_count, FF), bf16),
            ((row_count, FF), bf16),
        ]
        + [((wide // 2, FF), bf16), ((wide // 2, FF), bf16), ((FF // 2, D), bf16)] * 2,
        [residual, cot_t, wide_n, tall_wide_g, tall_wide_u, wall],
        scratch=[pltpu.VMEM((row_count, FF), bf16), pltpu.VMEM((FF, D), bf16)],
        scalars=[slots],
    )
    sums = (sums[:3], sums[3:])
    gres_t, gatt_t, dgain_ffn = call_whole(
        feed_back_kernel,
        [((D, row_count), f32), ((H * HD, row_count), bf16), ((1, D), f32)],
        [residual, cot_t, gain_ffn[None], row_b, row_n, dgate, dup, wb0, wb1, wall],
    )
    for t in range(3):
        sums = step_halve(sums, orders_gud, t)
    dq_t, dnear, down = call_whole(
        attend_back_kernel,
        [
            ((H * HD, row_count), bf16),
            ((2 * kv_cut, row_count), bf16),
            ((2 * kv_cut, row_count), f32),
        ],
        [q_t, near, kv_t, prob, att_t, gatt_t, cos, sin],
        scratch=[pltpu.VMEM((HD, 2 * row_count), f32)] * 2,
    )
    back = passed_along(dnear, "dev", -1)
    dtok_t, *last = call_whole(
        finish_kernel,
        [
            ((D, row_count), f32),
        ]
        + [((wide // 2, H * HD + kv_cut), bf16), ((wide // 2, D + kv_cut), bf16)] * 2,
        [dq_t, down, back, tok_t, gain_col, cos, sin, gres_t, wide_a, wide_b, wide_att, dgain_ffn]
        + [row_a, row_b, tall_a, tall_b, wa0, wa1, wb0, wb1],
    )
    last = (last[:2], last[2:])
    for t in range(steps):
        last = step_halve(last, orders_ab, t, even=True)
        if t + 3 < steps:
            sums = step_halve(sums, orders_gud, t + 3)
    share_g, share_u, share_d = sums
    share_a, share_b = last
    share_kv = jnp.concatenate([share_a[:per, H * HD :], share_b[:per, D:]], axis=1)
    share_gu = jnp.concatenate([share_g[:per], share_u[:per]], axis=1)
    return (
        mixed_t.T,
        dtok_t.T,
        share_a[per, :D],
        share_a[:per, : H * HD].reshape(-1),
        share_kv.reshape(-1),
        share_b[:per, :D].reshape(-1),
        share_b[per, :D],
        share_gu.reshape(-1),
        share_d.reshape(-1),
    )


def fits_whole_rows(count):
    per = D // count
    return D % count == 0 and FF % count == 0 and (FF // count) % 16 == 0 and 16 <= per < PAD and FF // count <= 2 * PAD


def solution(mesh):
    in_specs = (
        P("dev", None),
        P("dev"),
        P(),
        P("dev"),
        P("dev"),
        P("dev"),
        P(),
        P("dev"),
        P("dev"),
        P("dev", None),
    )
    out_specs = (
        P("dev", None),
        P("dev", None),
        P(),
        P("dev"),
        P("dev"),
        P("dev"),
        P(),
        P("dev"),
        P("dev"),
    )
    whole_rows = fits_whole_rows(mesh.shape["dev"])

    def layer(*args):
        return shards(*args)

    return jax.shard_map(
        layer if whole_rows else shards_general,
        mesh=mesh,
        in_specs=in_specs,
        out_specs=out_specs,
        check_vma=False,
    )
```

```python
import math

import jax
import jax.numpy as jnp
from jax import lax
from jax.experimental import pallas as pl
from jax.experimental.pallas import tpu as pltpu
from jax.sharding import PartitionSpec as P


D = 576
H = 9
KVH = 3
HD = 64
FF = 1536


norm_epsilon = 1e-05
theta_base = 100000.0


def passed_along(value, axis, steps):
    count = lax.axis_size(axis)
    first, last = (max(0, -steps), min(count, count - steps))
    return lax.ppermute(value, axis, [(source, source + steps) for source in range(first, last)])


def link_masks(count):
    bits = [1 << b for b in range(count.bit_length() - 1)]
    if count == 32:
        bits = [1, 2, 4, 8, 24]
    return bits[0], bits[1:]


def swapped(value, mask):
    count = lax.axis_size("dev")
    return lax.ppermute(value, "dev", [(i, i ^ mask) for i in range(count)])


def color_orders(count, colors):
    first, rest = link_masks(count)
    if colors == 1:
        return [rest + [first]]
    step = len(rest) // colors
    return [rest[c * step :] + rest[: c * step] + [first] for c in range(colors)]


def slot_masks(order):
    slots = [0]
    for mask in order:
        slots = slots + [s ^ mask for s in slots]
    return slots


def cut_rows(rows, colors):
    edges = [rows * c // colors for c in range(colors + 1)]
    return list(zip(edges[:-1], edges[1:]))


def gather_all(block, colors):
    count = lax.axis_size("dev")
    me = lax.axis_index("dev")
    orders = color_orders(count, colors)
    held = [block[a:b][None] for a, b in cut_rows(block.shape[0], colors)]
    for t in range(len(orders[0])):
        got = [swapped(h, order[t]) for h, order in zip(held, orders)]
        held = [jnp.concatenate([h, g], axis=0) for h, g in zip(held, got)]
    whole = []
    for h, order in zip(held, orders):
        slots = slot_masks(order)
        where = [0] * count
        for place, mask in enumerate(slots):
            where[mask] = place
        index = jnp.asarray(where, jnp.int32)[me ^ jnp.arange(count, dtype=jnp.int32)]
        whole.append(jnp.take(h, index, axis=0, mode="clip"))
    return jnp.concatenate(whole, axis=1)


def scatter_sum(parts, colors):
    count = lax.axis_size("dev")
    me = lax.axis_index("dev")
    orders = color_orders(count, colors)
    held = []
    for (a, b), order in zip(cut_rows(parts.shape[1], colors), orders):
        slots = jnp.asarray(slot_masks(order), jnp.int32)
        held.append(jnp.take(parts[:, a:b], me ^ slots, axis=0, mode="clip"))
    for t in range(len(orders[0])):
        half = held[0].shape[0] // 2
        masks = [order[-1 - t] for order in orders]
        got = [swapped(h[half:].astype(jnp.bfloat16), m) for h, m in zip(held, masks)]
        held = [h[:half].astype(jnp.float32) + g.astype(jnp.float32) for h, g in zip(held, got)]
    return jnp.concatenate([h[0] for h in held], axis=0)


def sum_all(value):
    first, rest = link_masks(lax.axis_size("dev"))
    for mask in [first] + rest:
        value = value + swapped(value, mask)
    return value


def norm_forward(values, scale_gain):
    inverse = lax.rsqrt(jnp.mean(values * values, axis=-1, keepdims=True) + norm_epsilon)
    return (values * inverse * scale_gain, inverse)


def norm_backward(grad_output, values, inverse, scale_gain):
    unit_rows = values * inverse
    scaled = grad_output * scale_gain
    grad_gain = jnp.sum(grad_output * unit_rows, axis=0)
    grad_input = inverse * (
        scaled - unit_rows * jnp.mean(scaled * unit_rows, axis=-1, keepdims=True)
    )
    return (grad_input, grad_gain)


def rope_angles(position_block):
    half_dim = HD // 2
    frequency = jnp.exp(
        jnp.arange(half_dim, dtype=jnp.float32) * (-2.0 * math.log(theta_base) / HD)
    )
    angles = position_block.astype(jnp.float32)[:, None] * frequency[None, :]
    return (jnp.cos(angles)[:, None, :], jnp.sin(angles)[:, None, :])


def rotate(values, cos_table, sin_table):
    half_dim = values.shape[-1] // 2
    first_half = values[..., :half_dim]
    second_half = values[..., half_dim:]
    return jnp.concatenate(
        [
            first_half * cos_table - second_half * sin_table,
            second_half * cos_table + first_half * sin_table,
        ],
        axis=-1,
    )


def project_heads(normed, query_mat, keyval_mat, cos_table, sin_table):
    row_count = normed.shape[0]
    queries = jnp.dot(normed, query_mat, preferred_element_type=jnp.float32).reshape(
        row_count, H, HD
    )
    keyvals = jnp.dot(normed, keyval_mat, preferred_element_type=jnp.float32)
    keys_rot = rotate(
        keyvals[:, : KVH * HD].reshape(row_count, KVH, HD), cos_table, sin_table
    ).reshape(row_count, KVH * HD)
    query_rot = (
        rotate(queries, cos_table, sin_table).reshape(row_count, H * HD).astype(jnp.bfloat16)
    )
    keyval_rot = jnp.concatenate([keys_rot, keyvals[:, KVH * HD :]], axis=1).astype(jnp.bfloat16)
    return (query_rot, keyval_rot)


def window_mask(position_block, row_count):
    query_at = jnp.arange(row_count, dtype=jnp.int32)[:, None] + row_count
    key_at = jnp.arange(2 * row_count, dtype=jnp.int32)[None, :]
    return (key_at <= query_at) & (key_at >= query_at - position_block[:, None])


def masked_scores(query_group, key_group, allowed):
    scale_factor = 1.0 / math.sqrt(HD)
    scores = (
        jnp.einsum("tqd,wd->qtw", query_group, key_group, preferred_element_type=jnp.float32)
        * scale_factor
    )
    return jnp.where(allowed[None], scores, -1e30)


def attend_forward(query_rot, window, allowed):
    row_count = query_rot.shape[0]
    grouped = H // KVH
    queries = query_rot.reshape(row_count, H, HD)
    outputs = []
    totals = []
    for group_index in range(KVH):
        query_group = queries[:, group_index * grouped : (group_index + 1) * grouped]
        key_group = window[:, group_index * HD : (group_index + 1) * HD]
        value_group = window[:, (KVH + group_index) * HD : (KVH + group_index + 1) * HD]
        scores = masked_scores(query_group, key_group, allowed)
        highest = jnp.max(scores, axis=-1, keepdims=True)
        log_total = highest + jnp.log(jnp.sum(jnp.exp(scores - highest), axis=-1, keepdims=True))
        probability = jnp.exp(scores - log_total).astype(jnp.bfloat16)
        head_out = jnp.einsum(
            "qtw,wd->tqd", probability, value_group, preferred_element_type=jnp.float32
        )
        outputs.append(head_out.astype(jnp.bfloat16))
        totals.append(log_total)
    return (jnp.concatenate(outputs, axis=1).reshape(row_count, H * HD), totals)


def attend_backward(query_rot, window, allowed, attended, grad_attended, totals):
    row_count = query_rot.shape[0]
    grouped = H // KVH
    scale_factor = 1.0 / math.sqrt(HD)
    queries = query_rot.reshape(row_count, H, HD)
    attended_heads = attended.reshape(row_count, H, HD)
    grad_heads = grad_attended.reshape(row_count, H, HD)
    query_grads = []
    key_grads = []
    value_grads = []
    for group_index in range(KVH):
        head_slice = slice(group_index * grouped, (group_index + 1) * grouped)
        query_group = queries[:, head_slice]
        key_group = window[:, group_index * HD : (group_index + 1) * HD]
        value_group = window[:, (KVH + group_index) * HD : (KVH + group_index + 1) * HD]
        scores = masked_scores(query_group, key_group, allowed)
        probability = jnp.exp(scores - totals[group_index])
        grad_group = grad_heads[:, head_slice]
        row_delta = jnp.sum(
            grad_group.astype(jnp.float32) * attended_heads[:, head_slice].astype(jnp.float32),
            axis=-1,
        )
        grad_prob = jnp.einsum(
            "tqd,wd->qtw", grad_group, value_group, preferred_element_type=jnp.float32
        )
        grad_scores = (probability * (grad_prob - row_delta.T[:, :, None]) * scale_factor).astype(
            jnp.bfloat16
        )
        query_grads.append(
            jnp.einsum("qtw,wd->tqd", grad_scores, key_group, preferred_element_type=jnp.float32)
        )
        key_grads.append(
            jnp.einsum("qtw,tqd->wd", grad_scores, query_group, preferred_element_type=jnp.float32)
        )
        value_grads.append(
            jnp.einsum(
                "qtw,tqd->wd",
                probability.astype(jnp.bfloat16),
                grad_group,
                preferred_element_type=jnp.float32,
            )
        )
    return (jnp.concatenate(query_grads, axis=1), jnp.concatenate(key_grads + value_grads, axis=1))


def shards_general(
    tokens, positions, gain_attn, w_query, w_kv, w_out, gain_ffn, w_gate_up, w_down, cotangent
):
    row_count = tokens.shape[0]
    width_kv = 2 * KVH * HD
    count = lax.axis_size("dev")
    attn_sizes = [w_query.shape[0], w_kv.shape[0], w_out.shape[0]]
    ffn_sizes = [w_gate_up.shape[0], w_down.shape[0]]
    attn_all = gather_all(jnp.concatenate([w_query, w_kv, w_out]).reshape(-1, 128), 2)
    attn_all = attn_all.reshape(count, -1)
    query_mat = attn_all[:, : attn_sizes[0]].reshape(D, H * HD)
    keyval_mat = attn_all[:, attn_sizes[0] : attn_sizes[0] + attn_sizes[1]].reshape(D, width_kv)
    out_mat = attn_all[:, attn_sizes[0] + attn_sizes[1] :].reshape(H * HD, D)
    ffn_all = gather_all(jnp.concatenate([w_gate_up, w_down]).reshape(-1, 128), 4)
    ffn_all = ffn_all.reshape(count, -1)
    gate_up_mat = ffn_all[:, : ffn_sizes[0]].reshape(D, 2 * FF)
    down_mat = ffn_all[:, ffn_sizes[0] :].reshape(FF, D)
    inputs = tokens.astype(jnp.float32)
    normed_attn, inverse_attn = norm_forward(inputs, gain_attn)
    normed_attn = normed_attn.astype(jnp.bfloat16)
    cos_table, sin_table = rope_angles(positions)
    query_rot, keyval_rot = project_heads(normed_attn, query_mat, keyval_mat, cos_table, sin_table)
    near_keys = passed_along(keyval_rot, "dev", 1)
    window = jnp.concatenate([near_keys, keyval_rot], axis=0)
    allowed = window_mask(positions, row_count)
    attended, totals = attend_forward(query_rot, window, allowed)
    residual = inputs + jnp.dot(attended, out_mat, preferred_element_type=jnp.float32)
    normed_ffn, inverse_ffn = norm_forward(residual, gain_ffn)
    normed_ffn = normed_ffn.astype(jnp.bfloat16)
    gate_up = jnp.dot(normed_ffn, gate_up_mat, preferred_element_type=jnp.float32)
    gate_part = gate_up[:, :FF]
    up_part = gate_up[:, FF:]
    activated = (jax.nn.silu(gate_part) * up_part).astype(jnp.bfloat16)
    mixed = (residual + jnp.dot(activated, down_mat, preferred_element_type=jnp.float32)).astype(
        jnp.bfloat16
    )
    grad_act = jnp.dot(cotangent, down_mat.T, preferred_element_type=jnp.float32)
    sigmoid_gate = jax.nn.sigmoid(gate_part)
    grad_gate_up_act = jnp.concatenate(
        [
            grad_act * up_part * sigmoid_gate * (1.0 + gate_part * (1.0 - sigmoid_gate)),
            grad_act * jax.nn.silu(gate_part),
        ],
        axis=1,
    ).astype(jnp.bfloat16)
    grad_down = jnp.dot(activated.T, cotangent, preferred_element_type=jnp.float32)
    grad_gate_up = jnp.dot(normed_ffn.T, grad_gate_up_act, preferred_element_type=jnp.float32)
    grad_normed_ffn = jnp.dot(grad_gate_up_act, gate_up_mat.T, preferred_element_type=jnp.float32)
    grad_norm_ffn, grad_gain_ffn = norm_backward(grad_normed_ffn, residual, inverse_ffn, gain_ffn)
    grad_residual = cotangent.astype(jnp.float32) + grad_norm_ffn
    grad_residual_b = grad_residual.astype(jnp.bfloat16)
    grad_out = jnp.dot(attended.T, grad_residual_b, preferred_element_type=jnp.float32)
    grad_attended = jnp.dot(grad_residual_b, out_mat.T, preferred_element_type=jnp.float32).astype(
        jnp.bfloat16
    )
    grad_query_rot, grad_window = attend_backward(
        query_rot, window, allowed, attended, grad_attended, totals
    )
    back_near = passed_along(grad_window[:row_count].astype(jnp.bfloat16), "dev", -1).astype(jnp.float32)
    grad_keyval_rot = grad_window[row_count:] + back_near
    key_part = rotate(
        grad_keyval_rot[:, : KVH * HD].reshape(row_count, KVH, HD), cos_table, -sin_table
    ).reshape(row_count, KVH * HD)
    grad_keyval_act = jnp.concatenate([key_part, grad_keyval_rot[:, KVH * HD :]], axis=1).astype(
        jnp.bfloat16
    )
    grad_query_act = (
        rotate(grad_query_rot, cos_table, -sin_table)
        .reshape(row_count, H * HD)
        .astype(jnp.bfloat16)
    )
    grad_query = jnp.dot(normed_attn.T, grad_query_act, preferred_element_type=jnp.float32)
    grad_keyval = jnp.dot(normed_attn.T, grad_keyval_act, preferred_element_type=jnp.float32)
    grad_normed_attn = jnp.dot(
        grad_query_act, query_mat.T, preferred_element_type=jnp.float32
    ) + jnp.dot(grad_keyval_act, keyval_mat.T, preferred_element_type=jnp.float32)
    grad_input, grad_gain_attn = norm_backward(grad_normed_attn, inputs, inverse_attn, gain_attn)
    token_grads = grad_residual + grad_input
    ffn_parts = jnp.concatenate(
        [
            grad_gate_up.reshape(count, -1).astype(jnp.bfloat16),
            grad_down.reshape(count, -1).astype(jnp.bfloat16),
            grad_out.reshape(count, -1).astype(jnp.bfloat16),
        ],
        axis=1,
    )
    ffn_parts = jnp.pad(ffn_parts, ((0, 0), (0, -ffn_parts.shape[1] % 128)))
    ffn_share = scatter_sum(ffn_parts.reshape(count, -1, 128), 4).reshape(-1)
    share_gate_up = ffn_share[: ffn_sizes[0]]
    share_down = ffn_share[ffn_sizes[0] : ffn_sizes[0] + ffn_sizes[1]]
    share_out = ffn_share[ffn_sizes[0] + ffn_sizes[1] : sum(ffn_sizes) + attn_sizes[2]]
    attn_parts = jnp.concatenate(
        [
            grad_query.reshape(count, -1).astype(jnp.bfloat16),
            grad_keyval.reshape(count, -1).astype(jnp.bfloat16),
        ],
        axis=1,
    )
    attn_rows = attn_parts.shape[1]
    attn_parts = jnp.pad(attn_parts, ((0, 0), (0, -attn_rows % 128)))
    attn_share = scatter_sum(attn_parts.reshape(count, -1, 128), 2).reshape(-1)
    share_query = attn_share[: attn_sizes[0]]
    share_keyval = attn_share[attn_sizes[0] : attn_sizes[0] + attn_sizes[1]]
    gain_sums = sum_all(jnp.stack([grad_gain_attn, grad_gain_ffn]))
    gain_attn_sum = gain_sums[0]
    gain_ffn_sum = gain_sums[1]
    return (
        mixed,
        token_grads,
        gain_attn_sum,
        share_query,
        share_keyval,
        share_out,
        gain_ffn_sum,
        share_gate_up,
        share_down,
    )


PAD = 24
FOLD_LANES = 640
CHUNK = 128
bf16 = jnp.bfloat16
f32 = jnp.float32


def dot_nn(a, b):
    return lax.dot_general(a, b, (((1,), (0,)), ((), ())), preferred_element_type=f32)


def dot_nt(a, b):
    return lax.dot_general(a, b, (((1,), (1,)), ((), ())), preferred_element_type=f32)


def spread_wide(source_row):
    rows = lax.broadcasted_iota(jnp.int32, (D, source_row.shape[1]), 0)
    return jnp.where(rows == source_row, 1.0, 0.0).astype(bf16)


def spread_tall(source_col):
    lanes = lax.broadcasted_iota(jnp.int32, (source_col.shape[0], D), 1)
    return jnp.where(lanes == source_col, 1.0, 0.0).astype(bf16)


def turn(a, b, cos_table, sin_table):
    return a * cos_table - b * sin_table, b * cos_table + a * sin_table


def project_kernel(tok, gain, cos, sin, src_a, src_b, wa0, wa1, wb0, wb1, q_out, kv_out):
    x = tok[...].astype(f32)
    inverse = lax.rsqrt(jnp.mean(x * x, axis=0, keepdims=True) + norm_epsilon)
    normed = (x * inverse * gain[...]).astype(bf16).T
    cos_table, sin_table = cos[...], sin[...]
    wa = jnp.concatenate([wa0[...], wa1[...]], axis=0)
    wb = jnp.concatenate([wb0[...], wb1[...]], axis=0)
    wide_a = dot_nn(normed, spread_wide(src_a[...])).astype(bf16)
    wide_b = dot_nn(normed, spread_wide(src_b[...])).astype(bf16)
    qk = dot_nn(wide_a, wa).T
    v = dot_nn(wide_b, wb).T[H * HD :]
    half = HD // 2
    for h in range(H + KVH):
        a = qk[h * HD : h * HD + half]
        b = qk[h * HD + half : (h + 1) * HD]
        ra, rb = turn(a, b, cos_table, sin_table)
        out, row = (q_out, h * HD) if h < H else (kv_out, (h - H) * HD)
        out[row : row + half, :] = ra.astype(bf16)
        out[row + half : row + HD, :] = rb.astype(bf16)
    kv_out[KVH * HD :, :] = v.astype(bf16)


def attend_kernel(q, near, own, pos, prob_out, att_out):
    tokens = q.shape[1]
    group = H // KVH
    scale = 1.0 / math.sqrt(HD)
    span = tokens + CHUNK
    rows = lax.broadcasted_iota(jnp.int32, (span, CHUNK), 0)
    lanes = lax.broadcasted_iota(jnp.int32, (span, CHUNK), 1) + tokens
    for g in range(KVH):
        kw = jnp.concatenate(
            [near[g * HD : (g + 1) * HD, :], own[g * HD : (g + 1) * HD, :]], axis=1
        ).T
        low = (KVH + g) * HD
        vw = jnp.concatenate([near[low : low + HD, :], own[low : low + HD, :]], axis=1)
        for c in range(tokens // CHUNK):
            base = c * CHUNK
            position = pos[:, base : base + CHUNK]
            allowed = (rows <= lanes) & (rows >= lanes - position)
            for i in range(group):
                h = g * group + i
                qh = q[h * HD : (h + 1) * HD, base : base + CHUNK]
                scores = dot_nn(kw[base : base + span], qh) * scale
                scores = jnp.where(allowed, scores, -1e30)
                highest = jnp.max(scores, axis=0, keepdims=True)
                e = jnp.exp(scores - highest)
                total = jnp.sum(e, axis=0, keepdims=True)
                p = (e * (1.0 / total)).astype(bf16)
                prob_out[g, c, :, i * CHUNK : (i + 1) * CHUNK] = p
                att_out[h * HD : (h + 1) * HD, base : base + CHUNK] = dot_nn(
                    vw[:, base : base + span], p
                ).astype(bf16)


def attend_back_kernel(
    q, near, own, prob, att, grad_att, cos, sin, dq_out, dnear_out, down_out, dk, dv
):
    tokens = q.shape[1]
    group = H // KVH
    scale = 1.0 / math.sqrt(HD)
    span = tokens + CHUNK
    half = HD // 2
    for g in range(KVH):
        low = (KVH + g) * HD
        kw = jnp.concatenate(
            [near[g * HD : (g + 1) * HD, :], own[g * HD : (g + 1) * HD, :]], axis=1
        )
        vw = jnp.concatenate([near[low : low + HD, :], own[low : low + HD, :]], axis=1).T
        dk[...] = jnp.zeros_like(dk)
        dv[...] = jnp.zeros_like(dv)
        for c in range(tokens // CHUNK):
            base = c * CHUNK
            cut = slice(base, base + CHUNK)
            heads = [g * group + i for i in range(group)]
            q_all = jnp.concatenate([q[h * HD : (h + 1) * HD, cut] for h in heads], axis=1)
            g_all = jnp.concatenate([grad_att[h * HD : (h + 1) * HD, cut] for h in heads], axis=1)
            a_all = jnp.concatenate([att[h * HD : (h + 1) * HD, cut] for h in heads], axis=1)
            delta = jnp.sum(g_all.astype(f32) * a_all.astype(f32), axis=0, keepdims=True)
            p = prob[g, c]
            grad_prob = dot_nn(vw[base : base + span], g_all)
            ds = (p.astype(f32) * (grad_prob - delta) * scale).astype(bf16)
            dq = dot_nn(kw[:, base : base + span], ds)
            dk[:, base : base + span] += dot_nt(q_all, ds)
            dv[:, base : base + span] += dot_nt(g_all, p)
            for i, h in enumerate(heads):
                part = dq[:, i * CHUNK : (i + 1) * CHUNK]
                ra, rb = turn(part[:half], part[half:], cos[:, cut], -sin[:, cut])
                dq_out[h * HD : h * HD + half, cut] = ra.astype(bf16)
                dq_out[h * HD + half : (h + 1) * HD, cut] = rb.astype(bf16)
        dnear_out[g * HD : (g + 1) * HD, :] = dk[:, :tokens].astype(bf16)
        dnear_out[low : low + HD, :] = dv[:, :tokens].astype(bf16)
        down_out[g * HD : (g + 1) * HD, :] = dk[:, tokens:]
        down_out[low : low + HD, :] = dv[:, tokens:]


def prepare_kernel(
    att,
    tok,
    gain_in,
    gain,
    row_b,
    row_n,
    tall_g,
    tall_u,
    tall_a,
    tall_b,
    wb0,
    wb1,
    res_out,
    wide_n,
    tall_wide_g,
    tall_wide_u,
    tall_wide_a,
    tall_wide_b,
    tall_wide_att,
):
    wb = jnp.concatenate([wb0[...], wb1[...]], axis=0)
    x = tok[...].astype(f32)
    att_wide = dot_nn(att[...].T, spread_wide(row_b[...])).astype(bf16)
    residual = x.T + dot_nn(att_wide, wb)[:, :D]
    res_out[...] = residual
    inverse = lax.rsqrt(jnp.mean(residual * residual, axis=-1, keepdims=True) + norm_epsilon)
    normed = (residual * inverse * gain[...]).astype(bf16)
    wide_n[...] = dot_nn(normed, spread_wide(row_n[...])).astype(bf16)
    normed_t = normed.T
    tall_wide_g[...] = dot_nn(spread_tall(tall_g[...]), normed_t).astype(bf16)
    tall_wide_u[...] = dot_nn(spread_tall(tall_u[...]), normed_t).astype(bf16)
    inverse_in = lax.rsqrt(jnp.mean(x * x, axis=0, keepdims=True) + norm_epsilon)
    normed_in = (x * inverse_in * gain_in[...]).astype(bf16)
    spread_b = spread_tall(tall_b[...])
    tall_wide_a[...] = dot_nn(spread_tall(tall_a[...]), normed_in).astype(bf16)
    tall_wide_b[...] = dot_nn(spread_b, normed_in).astype(bf16)
    tall_wide_att[...] = dot_nn(spread_b, att[...]).astype(bf16)


def feed_kernel(
    slots,
    residual,
    cot,
    wide_n,
    tall_wide_g,
    tall_wide_u,
    wall,
    wd,
    mixed_out,
    dgate,
    dup,
    dg_low,
    du_low,
    dd_low,
    dg_high,
    du_high,
    dd_high,
    act,
    dd,
):
    count = slots.shape[0]
    rows_d = FF // count
    cot_tok = cot[...].T
    block = 256

    def ff_step(j, carry):
        cut = pl.ds(pl.multiple_of(j * block, block), block)
        cut_up = pl.ds(pl.multiple_of(j * block + FF, block), block)
        gate = dot_nn(wide_n[...], wall[:, cut])
        up = dot_nn(wide_n[...], wall[:, cut_up])
        grad_act = dot_nt(cot_tok, wd[cut, :])
        sig = jax.nn.sigmoid(gate)
        silu = gate * sig
        act[:, cut] = (silu * up).astype(bf16)
        dgate[:, cut] = (grad_act * up * sig * (1.0 + gate * (1.0 - sig))).astype(bf16)
        dup[:, cut] = (grad_act * silu).astype(bf16)
        return carry

    lax.fori_loop(0, FF // block, ff_step, 0)
    mixed = residual[...] + dot_nn(act[...], wd[...])
    mixed_out[...] = mixed.T.astype(bf16)
    half = tall_wide_g.shape[0] // 2
    dg_low[...] = dot_nn(tall_wide_g[:half, :], dgate[...]).astype(bf16)
    dg_high[...] = dot_nn(tall_wide_g[half:, :], dgate[...]).astype(bf16)
    du_low[...] = dot_nn(tall_wide_u[:half, :], dup[...]).astype(bf16)
    du_high[...] = dot_nn(tall_wide_u[half:, :], dup[...]).astype(bf16)
    dd[...] = dot_nn(act[...].T, cot_tok).astype(bf16)
    for p in range(count):
        source = pl.multiple_of(slots[p] * rows_d, rows_d)
        out, at = (dd_low, p) if p < count // 2 else (dd_high, p - count // 2)
        out[at * rows_d : (at + 1) * rows_d, :] = dd[pl.ds(source, rows_d), :]


def feed_back_kernel(
    residual_in,
    cot,
    gain,
    src_b,
    src_n,
    dgate,
    dup,
    wb0,
    wb1,
    wall,
    gres_out,
    gatt_out,
    dgain_out,
):
    residual = residual_in[...]
    spread_b = spread_wide(src_b[...])
    spread_n = spread_wide(src_n[...])
    inverse = lax.rsqrt(jnp.mean(residual * residual, axis=-1, keepdims=True) + norm_epsilon)
    dn = dot_nt(dgate[...], wall[:, :FF]) + dot_nt(dup[...], wall[:, FF : 2 * FF])
    grad_normed = dot_nt(dn.astype(bf16), spread_n)
    unit = residual * inverse
    scaled = grad_normed * gain[...]
    dgain_out[...] = jnp.sum(grad_normed * unit, axis=0, keepdims=True)
    grad_res = cot[...].T.astype(f32) + inverse * (
        scaled - unit * jnp.mean(scaled * unit, axis=-1, keepdims=True)
    )
    gres_out[...] = grad_res.T
    wb = jnp.concatenate([wb0[:, :D], wb1[:, :D]], axis=0)
    gatt_wide = dot_nt(wb, grad_res.astype(bf16)).astype(bf16)
    gatt_out[...] = dot_nn(spread_b, gatt_wide).astype(bf16)


def finish_kernel(
    dq,
    own,
    back,
    tok,
    gain,
    cos,
    sin,
    gres,
    wide_a,
    wide_b,
    wide_att,
    dgain_ffn,
    src_a,
    src_b,
    tall_a,
    tall_b,
    wa0,
    wa1,
    wb0,
    wb1,
    dtok_out,
    da_low,
    db_low,
    da_high,
    db_high,
):
    x = tok[...].astype(f32)
    inverse = lax.rsqrt(jnp.mean(x * x, axis=0, keepdims=True) + norm_epsilon)
    unit = x * inverse
    total = own[...] + back[...].astype(f32)
    half = HD // 2
    parts = [dq[...]]
    for g in range(KVH):
        ra, rb = turn(
            total[g * HD : g * HD + half],
            total[g * HD + half : (g + 1) * HD],
            cos[...],
            -sin[...],
        )
        parts += [ra.astype(bf16), rb.astype(bf16)]
    dqk = jnp.concatenate(parts, axis=0)
    dv = total[KVH * HD :].astype(bf16)
    wa = jnp.concatenate([wa0[...], wa1[...]], axis=0)
    wb = jnp.concatenate([wb0[...], wb1[...]], axis=0)
    dvx = jnp.concatenate([jnp.zeros((H * HD, dv.shape[1]), bf16), dv], axis=0)
    dn_a = dot_nn(wa, dqk)
    dn_b = dot_nn(wb, dvx)
    spread_a = spread_wide(src_a[...])
    spread_b = spread_wide(src_b[...])
    grad_normed = dot_nn(spread_a, dn_a.astype(bf16)) + dot_nn(spread_b, dn_b.astype(bf16))
    scaled = grad_normed * gain[...]
    dtok_out[...] = gres[...] + inverse * (
        scaled - unit * jnp.mean(scaled * unit, axis=0, keepdims=True)
    )
    dgain = jnp.sum(grad_normed * unit, axis=1, keepdims=True)
    dgain = jnp.broadcast_to(dgain, (D, CHUNK)).T[:1]
    fill_a = jnp.concatenate([dgain, jnp.zeros((1, KVH * HD), f32)], axis=1)
    gres_b = gres[...].astype(bf16)
    half = wide_a.shape[0] // 2
    for cut, da_out, db_out in ((slice(0, half), da_low, db_low), (slice(half, None), da_high, db_high)):
        da_out[...] = jnp.where(tall_a[cut, :] < 0, fill_a, dot_nt(wide_a[cut, :], dqk)).astype(bf16)
        d_out = dot_nt(wide_att[cut, :], gres_b)
        db_out[:, :D] = jnp.where(tall_b[cut, :] < 0, dgain_ffn[...], d_out).astype(bf16)
        db_out[:, D:] = dot_nt(wide_b[cut, :], dv).astype(bf16)


def call_whole(kernel, outs, operands, scratch=(), scalars=()):
    vmem = pl.BlockSpec(memory_space=pltpu.VMEM)
    smem = pl.BlockSpec(memory_space=pltpu.SMEM)
    return pl.pallas_call(
        kernel,
        out_shape=[jax.ShapeDtypeStruct(s, d) for s, d in outs],
        in_specs=[smem] * len(scalars) + [vmem] * len(operands),
        out_specs=[vmem] * len(outs),
        scratch_shapes=list(scratch),
        compiler_params=pltpu.CompilerParams(vmem_limit_bytes=60 * 1024 * 1024),
    )(*scalars, *operands)


def step_double(held, orders, t):
    got = []
    for h, order in zip(held, orders):
        got.append(swapped(h, order[t]))
    return got


def joined(held, got):
    return [jnp.concatenate([h, g], axis=0) for h, g in zip(held, got)]


def step_halve(pair, orders, t, even=False):
    kept, send = pair
    final = t == len(orders[0]) - 1
    low, high = [], []
    for k, value, order in zip(kept, send, orders):
        g = swapped(value, order[-1 - t])
        if even:
            k = lax.reduce_precision(k.astype(f32), 8, 7)
        half = k.shape[0] if final else k.shape[0] // 2
        low.append(k[:half].astype(f32) + g[:half].astype(f32))
        high.append((k[half:].astype(f32) + g[half:].astype(f32)).astype(bf16))
    return low if final else (low, high)


def sources(order, count, per_slot):
    me = lax.axis_index("dev")
    owner = jnp.arange(count, dtype=jnp.int32)
    if order is not None:
        owner = me ^ jnp.asarray(slot_masks(order), jnp.int32)
    inner = jnp.arange(PAD, dtype=jnp.int32)[None, :]
    value = jnp.where(inner < per_slot, owner[:, None] * per_slot + inner, -1)
    return value.reshape(-1)


def padded_rows(value):
    return jnp.pad(value, ((0, PAD - value.shape[0]), (0, 0)))


def shards(
    tokens, positions, gain_attn, w_query, w_kv, w_out, gain_ffn, w_gate_up, w_down, cotangent
):
    count = lax.axis_size("dev")
    me = lax.axis_index("dev")
    row_count = tokens.shape[0]
    per = D // count
    per_d = FF // count
    first, rest = link_masks(count)
    order_of = [rest[k:] + rest[:k] + [first] for k in range(len(rest))]
    ord_a, ord_b = order_of[0], order_of[2]
    ord_g, ord_u, ord_d = order_of[1], order_of[2], order_of[3]
    src_a, src_b = sources(ord_a, count, per), sources(ord_b, count, per)
    src_n = sources(None, count, per)
    src_g, src_u = sources(ord_g, count, per), sources(ord_u, count, per)
    slots = me ^ jnp.asarray(slot_masks(ord_d), jnp.int32)
    w_qs, w_kvs = w_query.reshape(per, H * HD), w_kv.reshape(per, 2 * KVH * HD)
    kv_cut = KVH * HD
    stream_gu = padded_rows(w_gate_up.reshape(per, 2 * FF))
    folded = w_down.reshape(2, per_d // 2, D)
    folded = jnp.pad(folded, ((0, 0), (0, PAD - per_d // 2), (0, FOLD_LANES - D)))
    stream_ffn = jnp.concatenate([stream_gu, folded[0], folded[1]], axis=1)
    wall = lax.all_gather(stream_ffn, "dev", axis=0, tiled=True)
    stream_a = padded_rows(jnp.concatenate([w_qs, w_kvs[:, :kv_cut]], axis=1))
    stream_b = padded_rows(jnp.concatenate([w_out.reshape(per, D), w_kvs[:, kv_cut:]], axis=1))
    half_dim = HD // 2
    frequency = jnp.exp(jnp.arange(half_dim, dtype=f32) * (-2.0 * math.log(theta_base) / HD))
    angles = frequency[:, None] * positions.astype(f32)[None, :]
    cos, sin = jnp.cos(angles), jnp.sin(angles)
    tok_t, cot_t = tokens.T, cotangent.T
    gain_col = gain_attn.reshape(D, 1)
    orders_ab, orders_gud = [ord_a, ord_b], [ord_g, ord_u, ord_d]
    steps = len(ord_a)
    hold = lax.optimization_barrier
    held = [stream_a, stream_b]
    early = (src_a[None], src_b[None], src_a[:, None], src_b[:, None])
    early = early + (src_n[None], src_g[:, None], src_u[:, None], slots, cos, sin, gain_col)
    for t in range(steps):
        if t == 2:
            held, early = hold((held, early))
        got = step_double(held, orders_ab, t)
        if t < steps - 1:
            held = joined(held, got)
    (wa0, wb0), (wa1, wb1) = held, got
    row_a, row_b, tall_a, tall_b, row_n, tall_g, tall_u, slots, cos, sin, gain_col = early
    q_t, kv_t = call_whole(
        project_kernel,
        [((H * HD, row_count), bf16), ((2 * kv_cut, row_count), bf16)],
        [tok_t, gain_col, cos, sin, row_a, row_b, wa0, wa1, wb0, wb1],
    )
    near = passed_along(kv_t, "dev", 1)
    chunks = row_count // CHUNK
    prob, att_t = call_whole(
        attend_kernel,
        [
            ((KVH, chunks, row_count + CHUNK, H // KVH * CHUNK), bf16),
            ((H * HD, row_count), bf16),
        ],
        [q_t, near, kv_t, positions[None]],
    )
    wide = count * PAD
    folds = []
    for k in range(2):
        at = 2 * FF + k * FOLD_LANES
        folds.append(wall[:, at : at + D].reshape(count, PAD, D)[:, : per_d // 2])
    wd = jnp.concatenate(folds, axis=1).reshape(FF, D)
    tall_shape = ((wide, row_count), bf16)
    residual, wide_n, tall_wide_g, tall_wide_u, wide_a, wide_b, wide_att = call_whole(
        prepare_kernel,
        [((row_count, D), f32), ((row_count, wide), bf16)] + [tall_shape] * 5,
        [att_t, tok_t, gain_col, gain_ffn[None], row_b, row_n, tall_g, tall_u, tall_a, tall_b]
        + [wb0, wb1],
    )
    mixed_t, dgate, dup, *sums = call_whole(
        feed_kernel,
        [
            ((D, row_count), bf16),
            ((row_count, FF), bf16),
            ((row_count, FF), bf16),
        ]
        + [((wide // 2, FF), bf16), ((wide // 2, FF), bf16), ((FF // 2, D), bf16)] * 2,
        [residual, cot_t, wide_n, tall_wide_g, tall_wide_u, wall, wd],
        scratch=[pltpu.VMEM((row_count, FF), bf16), pltpu.VMEM((FF, D), bf16)],
        scalars=[slots],
    )
    sums = (sums[:3], sums[3:])
    gres_t, gatt_t, dgain_ffn = call_whole(
        feed_back_kernel,
        [((D, row_count), f32), ((H * HD, row_count), bf16), ((1, D), f32)],
        [residual, cot_t, gain_ffn[None], row_b, row_n, dgate, dup, wb0, wb1, wall],
    )
    for t in range(3):
        sums = step_halve(sums, orders_gud, t)
    dq_t, dnear, down = call_whole(
        attend_back_kernel,
        [
            ((H * HD, row_count), bf16),
            ((2 * kv_cut, row_count), bf16),
            ((2 * kv_cut, row_count), f32),
        ],
        [q_t, near, kv_t, prob, att_t, gatt_t, cos, sin],
        scratch=[pltpu.VMEM((HD, 2 * row_count), f32)] * 2,
    )
    back = passed_along(dnear, "dev", -1)
    dtok_t, *last = call_whole(
        finish_kernel,
        [
            ((D, row_count), f32),
        ]
        + [((wide // 2, H * HD + kv_cut), bf16), ((wide // 2, D + kv_cut), bf16)] * 2,
        [dq_t, down, back, tok_t, gain_col, cos, sin, gres_t, wide_a, wide_b, wide_att, dgain_ffn]
        + [row_a, row_b, tall_a, tall_b, wa0, wa1, wb0, wb1],
    )
    last = (last[:2], last[2:])
    for t in range(steps):
        last = step_halve(last, orders_ab, t, even=True)
        if t + 3 < steps:
            sums = step_halve(sums, orders_gud, t + 3)
    share_g, share_u, share_d = sums
    share_a, share_b = last
    share_kv = jnp.concatenate([share_a[:per, H * HD :], share_b[:per, D:]], axis=1)
    share_gu = jnp.concatenate([share_g[:per], share_u[:per]], axis=1)
    return (
        mixed_t.T,
        dtok_t.T,
        share_a[per, :D],
        share_a[:per, : H * HD].reshape(-1),
        share_kv.reshape(-1),
        share_b[:per, :D].reshape(-1),
        share_b[per, :D],
        share_gu.reshape(-1),
        share_d.reshape(-1),
    )


def fits_whole_rows(count):
    per = D // count
    return D % count == 0 and FF % count == 0 and (FF // count) % 16 == 0 and 16 <= per < PAD and FF // count <= 2 * PAD


def solution(mesh):
    in_specs = (
        P("dev", None),
        P("dev"),
        P(),
        P("dev"),
        P("dev"),
        P("dev"),
        P(),
        P("dev"),
        P("dev"),
        P("dev", None),
    )
    out_specs = (
        P("dev", None),
        P("dev", None),
        P(),
        P("dev"),
        P("dev"),
        P("dev"),
        P(),
        P("dev"),
        P("dev"),
    )
    whole_rows = fits_whole_rows(mesh.shape["dev"])

    def layer(*args):
        return shards(*args)

    return jax.shard_map(
        layer if whole_rows else shards_general,
        mesh=mesh,
        in_specs=in_specs,
        out_specs=out_specs,
        check_vma=False,
    )
```

```python
import math

import jax
import jax.numpy as jnp
from jax import lax
from jax.experimental import pallas as pl
from jax.experimental.pallas import tpu as pltpu
from jax.sharding import PartitionSpec as P


D = 576
H = 9
KVH = 3
HD = 64
FF = 1536


norm_epsilon = 1e-05
theta_base = 100000.0


def passed_along(value, axis, steps):
    count = lax.axis_size(axis)
    first, last = (max(0, -steps), min(count, count - steps))
    return lax.ppermute(value, axis, [(source, source + steps) for source in range(first, last)])


def link_masks(count):
    bits = [1 << b for b in range(count.bit_length() - 1)]
    if count == 32:
        bits = [1, 2, 4, 8, 24]
    return bits[0], bits[1:]


def swapped(value, mask):
    count = lax.axis_size("dev")
    return lax.ppermute(value, "dev", [(i, i ^ mask) for i in range(count)])


def color_orders(count, colors):
    first, rest = link_masks(count)
    if colors == 1:
        return [rest + [first]]
    step = len(rest) // colors
    return [rest[c * step :] + rest[: c * step] + [first] for c in range(colors)]


def slot_masks(order):
    slots = [0]
    for mask in order:
        slots = slots + [s ^ mask for s in slots]
    return slots


def cut_rows(rows, colors):
    edges = [rows * c // colors for c in range(colors + 1)]
    return list(zip(edges[:-1], edges[1:]))


def gather_all(block, colors):
    count = lax.axis_size("dev")
    me = lax.axis_index("dev")
    orders = color_orders(count, colors)
    held = [block[a:b][None] for a, b in cut_rows(block.shape[0], colors)]
    for t in range(len(orders[0])):
        got = [swapped(h, order[t]) for h, order in zip(held, orders)]
        held = [jnp.concatenate([h, g], axis=0) for h, g in zip(held, got)]
    whole = []
    for h, order in zip(held, orders):
        slots = slot_masks(order)
        where = [0] * count
        for place, mask in enumerate(slots):
            where[mask] = place
        index = jnp.asarray(where, jnp.int32)[me ^ jnp.arange(count, dtype=jnp.int32)]
        whole.append(jnp.take(h, index, axis=0, mode="clip"))
    return jnp.concatenate(whole, axis=1)


def scatter_sum(parts, colors):
    count = lax.axis_size("dev")
    me = lax.axis_index("dev")
    orders = color_orders(count, colors)
    held = []
    for (a, b), order in zip(cut_rows(parts.shape[1], colors), orders):
        slots = jnp.asarray(slot_masks(order), jnp.int32)
        held.append(jnp.take(parts[:, a:b], me ^ slots, axis=0, mode="clip"))
    for t in range(len(orders[0])):
        half = held[0].shape[0] // 2
        masks = [order[-1 - t] for order in orders]
        got = [swapped(h[half:].astype(jnp.bfloat16), m) for h, m in zip(held, masks)]
        held = [h[:half].astype(jnp.float32) + g.astype(jnp.float32) for h, g in zip(held, got)]
    return jnp.concatenate([h[0] for h in held], axis=0)


def sum_all(value):
    first, rest = link_masks(lax.axis_size("dev"))
    for mask in [first] + rest:
        value = value + swapped(value, mask)
    return value


def norm_forward(values, scale_gain):
    inverse = lax.rsqrt(jnp.mean(values * values, axis=-1, keepdims=True) + norm_epsilon)
    return (values * inverse * scale_gain, inverse)


def norm_backward(grad_output, values, inverse, scale_gain):
    unit_rows = values * inverse
    scaled = grad_output * scale_gain
    grad_gain = jnp.sum(grad_output * unit_rows, axis=0)
    grad_input = inverse * (
        scaled - unit_rows * jnp.mean(scaled * unit_rows, axis=-1, keepdims=True)
    )
    return (grad_input, grad_gain)


def rope_angles(position_block):
    half_dim = HD // 2
    frequency = jnp.exp(
        jnp.arange(half_dim, dtype=jnp.float32) * (-2.0 * math.log(theta_base) / HD)
    )
    angles = position_block.astype(jnp.float32)[:, None] * frequency[None, :]
    return (jnp.cos(angles)[:, None, :], jnp.sin(angles)[:, None, :])


def rotate(values, cos_table, sin_table):
    half_dim = values.shape[-1] // 2
    first_half = values[..., :half_dim]
    second_half = values[..., half_dim:]
    return jnp.concatenate(
        [
            first_half * cos_table - second_half * sin_table,
            second_half * cos_table + first_half * sin_table,
        ],
        axis=-1,
    )


def project_heads(normed, query_mat, keyval_mat, cos_table, sin_table):
    row_count = normed.shape[0]
    queries = jnp.dot(normed, query_mat, preferred_element_type=jnp.float32).reshape(
        row_count, H, HD
    )
    keyvals = jnp.dot(normed, keyval_mat, preferred_element_type=jnp.float32)
    keys_rot = rotate(
        keyvals[:, : KVH * HD].reshape(row_count, KVH, HD), cos_table, sin_table
    ).reshape(row_count, KVH * HD)
    query_rot = (
        rotate(queries, cos_table, sin_table).reshape(row_count, H * HD).astype(jnp.bfloat16)
    )
    keyval_rot = jnp.concatenate([keys_rot, keyvals[:, KVH * HD :]], axis=1).astype(jnp.bfloat16)
    return (query_rot, keyval_rot)


def window_mask(position_block, row_count):
    query_at = jnp.arange(row_count, dtype=jnp.int32)[:, None] + row_count
    key_at = jnp.arange(2 * row_count, dtype=jnp.int32)[None, :]
    return (key_at <= query_at) & (key_at >= query_at - position_block[:, None])


def masked_scores(query_group, key_group, allowed):
    scale_factor = 1.0 / math.sqrt(HD)
    scores = (
        jnp.einsum("tqd,wd->qtw", query_group, key_group, preferred_element_type=jnp.float32)
        * scale_factor
    )
    return jnp.where(allowed[None], scores, -1e30)


def attend_forward(query_rot, window, allowed):
    row_count = query_rot.shape[0]
    grouped = H // KVH
    queries = query_rot.reshape(row_count, H, HD)
    outputs = []
    totals = []
    for group_index in range(KVH):
        query_group = queries[:, group_index * grouped : (group_index + 1) * grouped]
        key_group = window[:, group_index * HD : (group_index + 1) * HD]
        value_group = window[:, (KVH + group_index) * HD : (KVH + group_index + 1) * HD]
        scores = masked_scores(query_group, key_group, allowed)
        highest = jnp.max(scores, axis=-1, keepdims=True)
        log_total = highest + jnp.log(jnp.sum(jnp.exp(scores - highest), axis=-1, keepdims=True))
        probability = jnp.exp(scores - log_total).astype(jnp.bfloat16)
        head_out = jnp.einsum(
            "qtw,wd->tqd", probability, value_group, preferred_element_type=jnp.float32
        )
        outputs.append(head_out.astype(jnp.bfloat16))
        totals.append(log_total)
    return (jnp.concatenate(outputs, axis=1).reshape(row_count, H * HD), totals)


def attend_backward(query_rot, window, allowed, attended, grad_attended, totals):
    row_count = query_rot.shape[0]
    grouped = H // KVH
    scale_factor = 1.0 / math.sqrt(HD)
    queries = query_rot.reshape(row_count, H, HD)
    attended_heads = attended.reshape(row_count, H, HD)
    grad_heads = grad_attended.reshape(row_count, H, HD)
    query_grads = []
    key_grads = []
    value_grads = []
    for group_index in range(KVH):
        head_slice = slice(group_index * grouped, (group_index + 1) * grouped)
        query_group = queries[:, head_slice]
        key_group = window[:, group_index * HD : (group_index + 1) * HD]
        value_group = window[:, (KVH + group_index) * HD : (KVH + group_index + 1) * HD]
        scores = masked_scores(query_group, key_group, allowed)
        probability = jnp.exp(scores - totals[group_index])
        grad_group = grad_heads[:, head_slice]
        row_delta = jnp.sum(
            grad_group.astype(jnp.float32) * attended_heads[:, head_slice].astype(jnp.float32),
            axis=-1,
        )
        grad_prob = jnp.einsum(
            "tqd,wd->qtw", grad_group, value_group, preferred_element_type=jnp.float32
        )
        grad_scores = (probability * (grad_prob - row_delta.T[:, :, None]) * scale_factor).astype(
            jnp.bfloat16
        )
        query_grads.append(
            jnp.einsum("qtw,wd->tqd", grad_scores, key_group, preferred_element_type=jnp.float32)
        )
        key_grads.append(
            jnp.einsum("qtw,tqd->wd", grad_scores, query_group, preferred_element_type=jnp.float32)
        )
        value_grads.append(
            jnp.einsum(
                "qtw,tqd->wd",
                probability.astype(jnp.bfloat16),
                grad_group,
                preferred_element_type=jnp.float32,
            )
        )
    return (jnp.concatenate(query_grads, axis=1), jnp.concatenate(key_grads + value_grads, axis=1))


def shards_general(
    tokens, positions, gain_attn, w_query, w_kv, w_out, gain_ffn, w_gate_up, w_down, cotangent
):
    row_count = tokens.shape[0]
    width_kv = 2 * KVH * HD
    count = lax.axis_size("dev")
    attn_sizes = [w_query.shape[0], w_kv.shape[0], w_out.shape[0]]
    ffn_sizes = [w_gate_up.shape[0], w_down.shape[0]]
    attn_all = gather_all(jnp.concatenate([w_query, w_kv, w_out]).reshape(-1, 128), 2)
    attn_all = attn_all.reshape(count, -1)
    query_mat = attn_all[:, : attn_sizes[0]].reshape(D, H * HD)
    keyval_mat = attn_all[:, attn_sizes[0] : attn_sizes[0] + attn_sizes[1]].reshape(D, width_kv)
    out_mat = attn_all[:, attn_sizes[0] + attn_sizes[1] :].reshape(H * HD, D)
    ffn_all = gather_all(jnp.concatenate([w_gate_up, w_down]).reshape(-1, 128), 4)
    ffn_all = ffn_all.reshape(count, -1)
    gate_up_mat = ffn_all[:, : ffn_sizes[0]].reshape(D, 2 * FF)
    down_mat = ffn_all[:, ffn_sizes[0] :].reshape(FF, D)
    inputs = tokens.astype(jnp.float32)
    normed_attn, inverse_attn = norm_forward(inputs, gain_attn)
    normed_attn = normed_attn.astype(jnp.bfloat16)
    cos_table, sin_table = rope_angles(positions)
    query_rot, keyval_rot = project_heads(normed_attn, query_mat, keyval_mat, cos_table, sin_table)
    near_keys = passed_along(keyval_rot, "dev", 1)
    window = jnp.concatenate([near_keys, keyval_rot], axis=0)
    allowed = window_mask(positions, row_count)
    attended, totals = attend_forward(query_rot, window, allowed)
    residual = inputs + jnp.dot(attended, out_mat, preferred_element_type=jnp.float32)
    normed_ffn, inverse_ffn = norm_forward(residual, gain_ffn)
    normed_ffn = normed_ffn.astype(jnp.bfloat16)
    gate_up = jnp.dot(normed_ffn, gate_up_mat, preferred_element_type=jnp.float32)
    gate_part = gate_up[:, :FF]
    up_part = gate_up[:, FF:]
    activated = (jax.nn.silu(gate_part) * up_part).astype(jnp.bfloat16)
    mixed = (residual + jnp.dot(activated, down_mat, preferred_element_type=jnp.float32)).astype(
        jnp.bfloat16
    )
    grad_act = jnp.dot(cotangent, down_mat.T, preferred_element_type=jnp.float32)
    sigmoid_gate = jax.nn.sigmoid(gate_part)
    grad_gate_up_act = jnp.concatenate(
        [
            grad_act * up_part * sigmoid_gate * (1.0 + gate_part * (1.0 - sigmoid_gate)),
            grad_act * jax.nn.silu(gate_part),
        ],
        axis=1,
    ).astype(jnp.bfloat16)
    grad_down = jnp.dot(activated.T, cotangent, preferred_element_type=jnp.float32)
    grad_gate_up = jnp.dot(normed_ffn.T, grad_gate_up_act, preferred_element_type=jnp.float32)
    grad_normed_ffn = jnp.dot(grad_gate_up_act, gate_up_mat.T, preferred_element_type=jnp.float32)
    grad_norm_ffn, grad_gain_ffn = norm_backward(grad_normed_ffn, residual, inverse_ffn, gain_ffn)
    grad_residual = cotangent.astype(jnp.float32) + grad_norm_ffn
    grad_residual_b = grad_residual.astype(jnp.bfloat16)
    grad_out = jnp.dot(attended.T, grad_residual_b, preferred_element_type=jnp.float32)
    grad_attended = jnp.dot(grad_residual_b, out_mat.T, preferred_element_type=jnp.float32).astype(
        jnp.bfloat16
    )
    grad_query_rot, grad_window = attend_backward(
        query_rot, window, allowed, attended, grad_attended, totals
    )
    back_near = passed_along(grad_window[:row_count].astype(jnp.bfloat16), "dev", -1).astype(jnp.float32)
    grad_keyval_rot = grad_window[row_count:] + back_near
    key_part = rotate(
        grad_keyval_rot[:, : KVH * HD].reshape(row_count, KVH, HD), cos_table, -sin_table
    ).reshape(row_count, KVH * HD)
    grad_keyval_act = jnp.concatenate([key_part, grad_keyval_rot[:, KVH * HD :]], axis=1).astype(
        jnp.bfloat16
    )
    grad_query_act = (
        rotate(grad_query_rot, cos_table, -sin_table)
        .reshape(row_count, H * HD)
        .astype(jnp.bfloat16)
    )
    grad_query = jnp.dot(normed_attn.T, grad_query_act, preferred_element_type=jnp.float32)
    grad_keyval = jnp.dot(normed_attn.T, grad_keyval_act, preferred_element_type=jnp.float32)
    grad_normed_attn = jnp.dot(
        grad_query_act, query_mat.T, preferred_element_type=jnp.float32
    ) + jnp.dot(grad_keyval_act, keyval_mat.T, preferred_element_type=jnp.float32)
    grad_input, grad_gain_attn = norm_backward(grad_normed_attn, inputs, inverse_attn, gain_attn)
    token_grads = grad_residual + grad_input
    ffn_parts = jnp.concatenate(
        [
            grad_gate_up.reshape(count, -1).astype(jnp.bfloat16),
            grad_down.reshape(count, -1).astype(jnp.bfloat16),
            grad_out.reshape(count, -1).astype(jnp.bfloat16),
        ],
        axis=1,
    )
    ffn_parts = jnp.pad(ffn_parts, ((0, 0), (0, -ffn_parts.shape[1] % 128)))
    ffn_share = scatter_sum(ffn_parts.reshape(count, -1, 128), 4).reshape(-1)
    share_gate_up = ffn_share[: ffn_sizes[0]]
    share_down = ffn_share[ffn_sizes[0] : ffn_sizes[0] + ffn_sizes[1]]
    share_out = ffn_share[ffn_sizes[0] + ffn_sizes[1] : sum(ffn_sizes) + attn_sizes[2]]
    attn_parts = jnp.concatenate(
        [
            grad_query.reshape(count, -1).astype(jnp.bfloat16),
            grad_keyval.reshape(count, -1).astype(jnp.bfloat16),
        ],
        axis=1,
    )
    attn_rows = attn_parts.shape[1]
    attn_parts = jnp.pad(attn_parts, ((0, 0), (0, -attn_rows % 128)))
    attn_share = scatter_sum(attn_parts.reshape(count, -1, 128), 2).reshape(-1)
    share_query = attn_share[: attn_sizes[0]]
    share_keyval = attn_share[attn_sizes[0] : attn_sizes[0] + attn_sizes[1]]
    gain_sums = sum_all(jnp.stack([grad_gain_attn, grad_gain_ffn]))
    gain_attn_sum = gain_sums[0]
    gain_ffn_sum = gain_sums[1]
    return (
        mixed,
        token_grads,
        gain_attn_sum,
        share_query,
        share_keyval,
        share_out,
        gain_ffn_sum,
        share_gate_up,
        share_down,
    )


PAD = 24
FOLD_LANES = 640
CHUNK = 128
bf16 = jnp.bfloat16
f32 = jnp.float32


def dot_nn(a, b):
    return lax.dot_general(a, b, (((1,), (0,)), ((), ())), preferred_element_type=f32)


def dot_nt(a, b):
    return lax.dot_general(a, b, (((1,), (1,)), ((), ())), preferred_element_type=f32)


def spread_wide(source_row):
    rows = lax.broadcasted_iota(jnp.int32, (D, source_row.shape[1]), 0)
    return jnp.where(rows == source_row, 1.0, 0.0).astype(bf16)


def spread_tall(source_col):
    lanes = lax.broadcasted_iota(jnp.int32, (source_col.shape[0], D), 1)
    return jnp.where(lanes == source_col, 1.0, 0.0).astype(bf16)


def turn(a, b, cos_table, sin_table):
    return a * cos_table - b * sin_table, b * cos_table + a * sin_table


def project_kernel(tok, gain, cos, sin, src_a, src_b, wa0, wa1, wb0, wb1, q_out, kv_out):
    x = tok[...].astype(f32)
    inverse = lax.rsqrt(jnp.mean(x * x, axis=0, keepdims=True) + norm_epsilon)
    normed = (x * inverse * gain[...]).astype(bf16).T
    cos_table, sin_table = cos[...], sin[...]
    wa = jnp.concatenate([wa0[...], wa1[...]], axis=0)
    wb = jnp.concatenate([wb0[...], wb1[...]], axis=0)
    wide_a = dot_nn(normed, spread_wide(src_a[...])).astype(bf16)
    wide_b = dot_nn(normed, spread_wide(src_b[...])).astype(bf16)
    qk = dot_nn(wide_a, wa).T
    v = dot_nn(wide_b, wb).T[H * HD :]
    half = HD // 2
    for h in range(H + KVH):
        a = qk[h * HD : h * HD + half]
        b = qk[h * HD + half : (h + 1) * HD]
        ra, rb = turn(a, b, cos_table, sin_table)
        out, row = (q_out, h * HD) if h < H else (kv_out, (h - H) * HD)
        out[row : row + half, :] = ra.astype(bf16)
        out[row + half : row + HD, :] = rb.astype(bf16)
    kv_out[KVH * HD :, :] = v.astype(bf16)


def attend_kernel(q, near, own, pos, prob_out, att_out):
    tokens = q.shape[1]
    group = H // KVH
    scale = 1.0 / math.sqrt(HD)
    span = tokens + CHUNK
    rows = lax.broadcasted_iota(jnp.int32, (span, CHUNK), 0)
    lanes = lax.broadcasted_iota(jnp.int32, (span, CHUNK), 1) + tokens
    for g in range(KVH):
        kw = jnp.concatenate(
            [near[g * HD : (g + 1) * HD, :], own[g * HD : (g + 1) * HD, :]], axis=1
        ).T
        low = (KVH + g) * HD
        vw = jnp.concatenate([near[low : low + HD, :], own[low : low + HD, :]], axis=1)
        for c in range(tokens // CHUNK):
            base = c * CHUNK
            position = pos[:, base : base + CHUNK]
            allowed = (rows <= lanes) & (rows >= lanes - position)
            for i in range(group):
                h = g * group + i
                qh = q[h * HD : (h + 1) * HD, base : base + CHUNK]
                scores = dot_nn(kw[base : base + span], qh) * scale
                scores = jnp.where(allowed, scores, -1e30)
                highest = jnp.max(scores, axis=0, keepdims=True)
                e = jnp.exp(scores - highest)
                total = jnp.sum(e, axis=0, keepdims=True)
                p = (e * (1.0 / total)).astype(bf16)
                prob_out[g, c, :, i * CHUNK : (i + 1) * CHUNK] = p
                att_out[h * HD : (h + 1) * HD, base : base + CHUNK] = dot_nn(
                    vw[:, base : base + span], p
                ).astype(bf16)


def attend_back_kernel(
    q, near, own, prob, att, grad_att, cos, sin, dq_out, dnear_out, down_out, dk, dv
):
    tokens = q.shape[1]
    group = H // KVH
    scale = 1.0 / math.sqrt(HD)
    span = tokens + CHUNK
    half = HD // 2
    for g in range(KVH):
        low = (KVH + g) * HD
        kw = jnp.concatenate(
            [near[g * HD : (g + 1) * HD, :], own[g * HD : (g + 1) * HD, :]], axis=1
        )
        vw = jnp.concatenate([near[low : low + HD, :], own[low : low + HD, :]], axis=1).T
        dk[...] = jnp.zeros_like(dk)
        dv[...] = jnp.zeros_like(dv)
        for c in range(tokens // CHUNK):
            base = c * CHUNK
            cut = slice(base, base + CHUNK)
            heads = [g * group + i for i in range(group)]
            q_all = jnp.concatenate([q[h * HD : (h + 1) * HD, cut] for h in heads], axis=1)
            g_all = jnp.concatenate([grad_att[h * HD : (h + 1) * HD, cut] for h in heads], axis=1)
            a_all = jnp.concatenate([att[h * HD : (h + 1) * HD, cut] for h in heads], axis=1)
            delta = jnp.sum(g_all.astype(f32) * a_all.astype(f32), axis=0, keepdims=True)
            p = prob[g, c]
            grad_prob = dot_nn(vw[base : base + span], g_all)
            ds = (p.astype(f32) * (grad_prob - delta) * scale).astype(bf16)
            dq = dot_nn(kw[:, base : base + span], ds)
            dk[:, base : base + span] += dot_nt(q_all, ds)
            dv[:, base : base + span] += dot_nt(g_all, p)
            for i, h in enumerate(heads):
                part = dq[:, i * CHUNK : (i + 1) * CHUNK]
                ra, rb = turn(part[:half], part[half:], cos[:, cut], -sin[:, cut])
                dq_out[h * HD : h * HD + half, cut] = ra.astype(bf16)
                dq_out[h * HD + half : (h + 1) * HD, cut] = rb.astype(bf16)
        dnear_out[g * HD : (g + 1) * HD, :] = dk[:, :tokens].astype(bf16)
        dnear_out[low : low + HD, :] = dv[:, :tokens].astype(bf16)
        down_out[g * HD : (g + 1) * HD, :] = dk[:, tokens:]
        down_out[low : low + HD, :] = dv[:, tokens:]


def prepare_kernel(att, tok, gain_in, tall_a, tall_b, wide_a, wide_b, wide_att):
    x = tok[...].astype(f32)
    inverse = lax.rsqrt(jnp.mean(x * x, axis=0, keepdims=True) + norm_epsilon)
    normed = (x * inverse * gain_in[...]).astype(bf16)
    spread_b = spread_tall(tall_b[...])
    wide_a[...] = dot_nn(spread_tall(tall_a[...]), normed).astype(bf16)
    wide_b[...] = dot_nn(spread_b, normed).astype(bf16)
    wide_att[...] = dot_nn(spread_b, att[...]).astype(bf16)


def feed_kernel(
    slots,
    att,
    tok,
    cot,
    gain,
    row_b,
    row_n,
    tall_g,
    tall_u,
    wb0,
    wb1,
    wall,
    mixed_out,
    res_out,
    dgate,
    dup,
    dg_low,
    du_low,
    dd_low,
    dg_high,
    du_high,
    dd_high,
    act,
    wide_n,
    wd,
):
    count = slots.shape[0]
    rows_d = FF // count
    fold = rows_d // 2
    for j in range(count):
        for k in range(2):
            at = 2 * FF + k * FOLD_LANES
            wd[j * rows_d + k * fold : j * rows_d + (k + 1) * fold, :] = wall[
                j * PAD : j * PAD + fold, at : at + D
            ]
    wb = jnp.concatenate([wb0[...], wb1[...]], axis=0)
    cot_tok = cot[...].T
    att_wide = dot_nn(att[...].T, spread_wide(row_b[...])).astype(bf16)
    residual = tok[...].astype(f32).T + dot_nn(att_wide, wb)[:, :D]
    res_out[...] = residual
    inverse = lax.rsqrt(jnp.mean(residual * residual, axis=-1, keepdims=True) + norm_epsilon)
    normed = (residual * inverse * gain[...]).astype(bf16)
    wide_n[...] = dot_nn(normed, spread_wide(row_n[...])).astype(bf16)
    normed_t = normed.T
    block = 256

    def ff_step(j, carry):
        cut = pl.ds(pl.multiple_of(j * block, block), block)
        cut_up = pl.ds(pl.multiple_of(j * block + FF, block), block)
        gate = dot_nn(wide_n[...], wall[:, cut])
        up = dot_nn(wide_n[...], wall[:, cut_up])
        grad_act = dot_nt(cot_tok, wd[cut, :])
        sig = jax.nn.sigmoid(gate)
        silu = gate * sig
        act[:, cut] = (silu * up).astype(bf16)
        dgate[:, cut] = (grad_act * up * sig * (1.0 + gate * (1.0 - sig))).astype(bf16)
        dup[:, cut] = (grad_act * silu).astype(bf16)
        return carry

    lax.fori_loop(0, FF // block, ff_step, 0)
    mixed = residual + dot_nn(act[...], wd[...])
    mixed_out[...] = mixed.T.astype(bf16)
    for tall, grad, low, high in ((tall_g, dgate, dg_low, dg_high), (tall_u, dup, du_low, du_high)):
        wide_t = dot_nn(spread_tall(tall[...]), normed_t).astype(bf16)
        half = wide_t.shape[0] // 2
        low[...] = dot_nn(wide_t[:half], grad[...]).astype(bf16)
        high[...] = dot_nn(wide_t[half:], grad[...]).astype(bf16)
    wd[...] = dot_nn(act[...].T, cot_tok).astype(bf16)
    for p in range(count):
        source = pl.multiple_of(slots[p] * rows_d, rows_d)
        out, at = (dd_low, p) if p < count // 2 else (dd_high, p - count // 2)
        out[at * rows_d : (at + 1) * rows_d, :] = wd[pl.ds(source, rows_d), :]


def feed_back_kernel(
    residual_in,
    cot,
    gain,
    src_b,
    src_n,
    dgate,
    dup,
    wb0,
    wb1,
    wall,
    gres_out,
    gatt_out,
    dgain_out,
):
    residual = residual_in[...]
    spread_b = spread_wide(src_b[...])
    spread_n = spread_wide(src_n[...])
    inverse = lax.rsqrt(jnp.mean(residual * residual, axis=-1, keepdims=True) + norm_epsilon)
    dn = dot_nt(dgate[...], wall[:, :FF]) + dot_nt(dup[...], wall[:, FF : 2 * FF])
    grad_normed = dot_nt(dn.astype(bf16), spread_n)
    unit = residual * inverse
    scaled = grad_normed * gain[...]
    dgain_out[...] = jnp.sum(grad_normed * unit, axis=0, keepdims=True)
    grad_res = cot[...].T.astype(f32) + inverse * (
        scaled - unit * jnp.mean(scaled * unit, axis=-1, keepdims=True)
    )
    gres_out[...] = grad_res.T
    wb = jnp.concatenate([wb0[:, :D], wb1[:, :D]], axis=0)
    gatt_wide = dot_nt(wb, grad_res.astype(bf16)).astype(bf16)
    gatt_out[...] = dot_nn(spread_b, gatt_wide).astype(bf16)


def finish_kernel(
    dq,
    own,
    back,
    tok,
    gain,
    cos,
    sin,
    gres,
    wide_a,
    wide_b,
    wide_att,
    dgain_ffn,
    src_a,
    src_b,
    tall_a,
    tall_b,
    wa0,
    wa1,
    wb0,
    wb1,
    dtok_out,
    da_low,
    db_low,
    da_high,
    db_high,
):
    x = tok[...].astype(f32)
    inverse = lax.rsqrt(jnp.mean(x * x, axis=0, keepdims=True) + norm_epsilon)
    unit = x * inverse
    total = own[...] + back[...].astype(f32)
    half = HD // 2
    parts = [dq[...]]
    for g in range(KVH):
        ra, rb = turn(
            total[g * HD : g * HD + half],
            total[g * HD + half : (g + 1) * HD],
            cos[...],
            -sin[...],
        )
        parts += [ra.astype(bf16), rb.astype(bf16)]
    dqk = jnp.concatenate(parts, axis=0)
    dv = total[KVH * HD :].astype(bf16)
    wa = jnp.concatenate([wa0[...], wa1[...]], axis=0)
    wb = jnp.concatenate([wb0[...], wb1[...]], axis=0)
    dvx = jnp.concatenate([jnp.zeros((H * HD, dv.shape[1]), bf16), dv], axis=0)
    dn_a = dot_nn(wa, dqk)
    dn_b = dot_nn(wb, dvx)
    spread_a = spread_wide(src_a[...])
    spread_b = spread_wide(src_b[...])
    grad_normed = dot_nn(spread_a, dn_a.astype(bf16)) + dot_nn(spread_b, dn_b.astype(bf16))
    scaled = grad_normed * gain[...]
    dtok_out[...] = gres[...] + inverse * (
        scaled - unit * jnp.mean(scaled * unit, axis=0, keepdims=True)
    )
    dgain = jnp.sum(grad_normed * unit, axis=1, keepdims=True)
    dgain = jnp.broadcast_to(dgain, (D, CHUNK)).T[:1]
    fill_a = jnp.concatenate([dgain, jnp.zeros((1, KVH * HD), f32)], axis=1)
    gres_b = gres[...].astype(bf16)
    half = wide_a.shape[0] // 2
    for cut, da_out, db_out in ((slice(0, half), da_low, db_low), (slice(half, None), da_high, db_high)):
        da_out[...] = jnp.where(tall_a[cut, :] < 0, fill_a, dot_nt(wide_a[cut, :], dqk)).astype(bf16)
        d_out = dot_nt(wide_att[cut, :], gres_b)
        db_out[:, :D] = jnp.where(tall_b[cut, :] < 0, dgain_ffn[...], d_out).astype(bf16)
        db_out[:, D:] = dot_nt(wide_b[cut, :], dv).astype(bf16)


def call_whole(kernel, outs, operands, scratch=(), scalars=()):
    vmem = pl.BlockSpec(memory_space=pltpu.VMEM)
    smem = pl.BlockSpec(memory_space=pltpu.SMEM)
    return pl.pallas_call(
        kernel,
        out_shape=[jax.ShapeDtypeStruct(s, d) for s, d in outs],
        in_specs=[smem] * len(scalars) + [vmem] * len(operands),
        out_specs=[vmem] * len(outs),
        scratch_shapes=list(scratch),
        compiler_params=pltpu.CompilerParams(vmem_limit_bytes=60 * 1024 * 1024),
    )(*scalars, *operands)


def step_double(held, orders, t):
    got = []
    for h, order in zip(held, orders):
        got.append(swapped(h, order[t]))
    return got


def joined(held, got):
    return [jnp.concatenate([h, g], axis=0) for h, g in zip(held, got)]


def step_halve(pair, orders, t, even=False):
    kept, send = pair
    final = t == len(orders[0]) - 1
    low, high = [], []
    for k, value, order in zip(kept, send, orders):
        g = swapped(value, order[-1 - t])
        if even:
            k = lax.reduce_precision(k.astype(f32), 8, 7)
        half = k.shape[0] if final else k.shape[0] // 2
        low.append(k[:half].astype(f32) + g[:half].astype(f32))
        high.append((k[half:].astype(f32) + g[half:].astype(f32)).astype(bf16))
    return low if final else (low, high)


def sources(order, count, per_slot):
    me = lax.axis_index("dev")
    owner = jnp.arange(count, dtype=jnp.int32)
    if order is not None:
        owner = me ^ jnp.asarray(slot_masks(order), jnp.int32)
    inner = jnp.arange(PAD, dtype=jnp.int32)[None, :]
    value = jnp.where(inner < per_slot, owner[:, None] * per_slot + inner, -1)
    return value.reshape(-1)


def padded_rows(value):
    return jnp.pad(value, ((0, PAD - value.shape[0]), (0, 0)))


def shards(
    tokens, positions, gain_attn, w_query, w_kv, w_out, gain_ffn, w_gate_up, w_down, cotangent
):
    count = lax.axis_size("dev")
    me = lax.axis_index("dev")
    row_count = tokens.shape[0]
    per = D // count
    per_d = FF // count
    first, rest = link_masks(count)
    order_of = [rest[k:] + rest[:k] + [first] for k in range(len(rest))]
    ord_a, ord_b = order_of[0], order_of[2]
    ord_g, ord_u, ord_d = order_of[1], order_of[2], order_of[3]
    src_a, src_b = sources(ord_a, count, per), sources(ord_b, count, per)
    src_n = sources(None, count, per)
    src_g, src_u = sources(ord_g, count, per), sources(ord_u, count, per)
    slots = me ^ jnp.asarray(slot_masks(ord_d), jnp.int32)
    w_qs, w_kvs = w_query.reshape(per, H * HD), w_kv.reshape(per, 2 * KVH * HD)
    kv_cut = KVH * HD
    stream_gu = padded_rows(w_gate_up.reshape(per, 2 * FF))
    folded = w_down.reshape(2, per_d // 2, D)
    folded = jnp.pad(folded, ((0, 0), (0, PAD - per_d // 2), (0, FOLD_LANES - D)))
    stream_ffn = jnp.concatenate([stream_gu, folded[0], folded[1]], axis=1)
    wall = lax.all_gather(stream_ffn, "dev", axis=0, tiled=True)
    stream_a = padded_rows(jnp.concatenate([w_qs, w_kvs[:, :kv_cut]], axis=1))
    stream_b = padded_rows(jnp.concatenate([w_out.reshape(per, D), w_kvs[:, kv_cut:]], axis=1))
    half_dim = HD // 2
    frequency = jnp.exp(jnp.arange(half_dim, dtype=f32) * (-2.0 * math.log(theta_base) / HD))
    angles = frequency[:, None] * positions.astype(f32)[None, :]
    cos, sin = jnp.cos(angles), jnp.sin(angles)
    tok_t, cot_t = tokens.T, cotangent.T
    gain_col = gain_attn.reshape(D, 1)
    orders_ab, orders_gud = [ord_a, ord_b], [ord_g, ord_u, ord_d]
    steps = len(ord_a)
    hold = lax.optimization_barrier
    held = [stream_a, stream_b]
    early = (src_a[None], src_b[None], src_a[:, None], src_b[:, None])
    early = early + (src_n[None], src_g[:, None], src_u[:, None], slots, cos, sin, gain_col)
    for t in range(steps):
        if t == 2:
            held, early = hold((held, early))
        got = step_double(held, orders_ab, t)
        if t < steps - 1:
            held = joined(held, got)
    (wa0, wb0), (wa1, wb1) = held, got
    row_a, row_b, tall_a, tall_b, row_n, tall_g, tall_u, slots, cos, sin, gain_col = early
    q_t, kv_t = call_whole(
        project_kernel,
        [((H * HD, row_count), bf16), ((2 * kv_cut, row_count), bf16)],
        [tok_t, gain_col, cos, sin, row_a, row_b, wa0, wa1, wb0, wb1],
    )
    near = passed_along(kv_t, "dev", 1)
    chunks = row_count // CHUNK
    prob, att_t = call_whole(
        attend_kernel,
        [
            ((KVH, chunks, row_count + CHUNK, H // KVH * CHUNK), bf16),
            ((H * HD, row_count), bf16),
        ],
        [q_t, near, kv_t, positions[None]],
    )
    wide = count * PAD
    tall_shape = ((wide, row_count), bf16)
    wide_a, wide_b, wide_att = call_whole(
        prepare_kernel, [tall_shape] * 3, [att_t, tok_t, gain_col, tall_a, tall_b]
    )
    att_t, wide_a, wide_b, wide_att = hold((att_t, wide_a, wide_b, wide_att))
    mixed_t, residual, dgate, dup, *sums = call_whole(
        feed_kernel,
        [
            ((D, row_count), bf16),
            ((row_count, D), f32),
            ((row_count, FF), bf16),
            ((row_count, FF), bf16),
        ]
        + [((wide // 2, FF), bf16), ((wide // 2, FF), bf16), ((FF // 2, D), bf16)] * 2,
        [att_t, tok_t, cot_t, gain_ffn[None], row_b, row_n, tall_g, tall_u, wb0, wb1, wall],
        scratch=[
            pltpu.VMEM((row_count, FF), bf16),
            pltpu.VMEM((row_count, wide), bf16),
            pltpu.VMEM((FF, D), bf16),
        ],
        scalars=[slots],
    )
    sums = (sums[:3], sums[3:])
    gres_t, gatt_t, dgain_ffn = call_whole(
        feed_back_kernel,
        [((D, row_count), f32), ((H * HD, row_count), bf16), ((1, D), f32)],
        [residual, cot_t, gain_ffn[None], row_b, row_n, dgate, dup, wb0, wb1, wall],
    )
    for t in range(3):
        sums = step_halve(sums, orders_gud, t)
    dq_t, dnear, down = call_whole(
        attend_back_kernel,
        [
            ((H * HD, row_count), bf16),
            ((2 * kv_cut, row_count), bf16),
            ((2 * kv_cut, row_count), f32),
        ],
        [q_t, near, kv_t, prob, att_t, gatt_t, cos, sin],
        scratch=[pltpu.VMEM((HD, 2 * row_count), f32)] * 2,
    )
    back = passed_along(dnear, "dev", -1)
    dtok_t, *last = call_whole(
        finish_kernel,
        [
            ((D, row_count), f32),
        ]
        + [((wide // 2, H * HD + kv_cut), bf16), ((wide // 2, D + kv_cut), bf16)] * 2,
        [dq_t, down, back, tok_t, gain_col, cos, sin, gres_t, wide_a, wide_b, wide_att, dgain_ffn]
        + [row_a, row_b, tall_a, tall_b, wa0, wa1, wb0, wb1],
    )
    last = (last[:2], last[2:])
    for t in range(steps):
        last = step_halve(last, orders_ab, t, even=True)
        if t + 3 < steps:
            sums = step_halve(sums, orders_gud, t + 3)
    share_g, share_u, share_d = sums
    share_a, share_b = last
    share_kv = jnp.concatenate([share_a[:per, H * HD :], share_b[:per, D:]], axis=1)
    share_gu = jnp.concatenate([share_g[:per], share_u[:per]], axis=1)
    return (
        mixed_t.T,
        dtok_t.T,
        share_a[per, :D],
        share_a[:per, : H * HD].reshape(-1),
        share_kv.reshape(-1),
        share_b[:per, :D].reshape(-1),
        share_b[per, :D],
        share_gu.reshape(-1),
        share_d.reshape(-1),
    )


def fits_whole_rows(count):
    per = D // count
    return D % count == 0 and FF % count == 0 and (FF // count) % 16 == 0 and 16 <= per < PAD and FF // count <= 2 * PAD


def solution(mesh):
    in_specs = (
        P("dev", None),
        P("dev"),
        P(),
        P("dev"),
        P("dev"),
        P("dev"),
        P(),
        P("dev"),
        P("dev"),
        P("dev", None),
    )
    out_specs = (
        P("dev", None),
        P("dev", None),
        P(),
        P("dev"),
        P("dev"),
        P("dev"),
        P(),
        P("dev"),
        P("dev"),
    )
    whole_rows = fits_whole_rows(mesh.shape["dev"])

    def layer(*args):
        return shards(*args)

    return jax.shard_map(
        layer if whole_rows else shards_general,
        mesh=mesh,
        in_specs=in_specs,
        out_specs=out_specs,
        check_vma=False,
    )
```
